32 devices in a mesh: sec: 4 (over y, x), gx: 4 (over z), gy: 2 (over core).
Axes of the slice: x: 2, y: 2, z: 4, core: 2. Of those that a mesh axis runs over, the one named last changes fastest.
Arguments:
- driving: float32 [3, 128, 256], P(None, 'gx', 'gy'), may hold values from -6 to 6
- rate_factor: float32 [3, 128, 256], P(None, 'gx', 'gy'), may hold values from 0.5 to 4
- friction_init: float32 [3, 128, 256], P(None, 'gx', 'gy'), may hold values from 0.2 to 2
- ice_mask: int32 [3, 128, 256], P(None, 'gx', 'gy'), may hold values 0 or 1
- grounded_mask: int32 [3, 128, 256], P(None, 'gx', 'gy'), may hold values 0 or 1
- melt: float32 [3, 128, 256], P(None, 'gx', 'gy'), may hold values from 0.1 to 1
- transmissivity: float32 [3, 128, 256], P(None, 'gx', 'gy'), may hold values from 0.5 to 5
- leakage: float32 [3, 128, 256], P(None, 'gx', 'gy'), may hold values from 0.05 to 0.5
- overburden: float32 [3, 128, 256], P(None, 'gx', 'gy'), may hold values from 0.5 to 2
- friction_scale: float32 [3, 128, 256], P(None, 'gx', 'gy'), may hold values from 0.5 to 4
Outputs:
- column_out: float32 [4, 3, 128, 256], P('sec', None, 'gx', 'gy')
The draws below stay inside these ranges and needn't reach their ends.
All inputs are finite; a program needn't handle non-finite values. No bound on the sum of `ice_mask` or of `grounded_mask` on one device may be relied on, other than what follows from the above.
Results may differ from the reference program's by a relative error of at most 0.00002.
Values sent between devices are 32-bit elements; how exact they have to be, the bound alone decides.
A program may use at most 64 MiB of HBM per device.

```python
import math
import jax
import jax.numpy as jnp
from jax import lax

LAYERS = 40
PICARD = 2
SWEEPS = 4
STRIPS = 3
NX = 128
NY = 256


def plant(entries, key, least, high):
    longest = entries.shape.index(max(entries.shape))
    spots = []
    for shift in (0, 1):
        where = [jax.random.randint(jax.random.fold_in(key, axis), (), 0, length) for axis, length in enumerate(entries.shape)]
        where[longest] = (where[longest] + shift) % entries.shape[longest]
        spots.append(tuple(where))
    return entries.at[spots[0]].set(least).at[spots[1]].set(high)


def shard_levels(rng, dims, shards, least, largest):
    loudness = 1.0
    for dim, shards_of in shards:
        steps = jax.random.uniform(jax.random.fold_in(jax.random.fold_in(rng, 6), dim), (shards_of,), jnp.float32, least / len(shards), largest / len(shards))
        loudness = loudness * jnp.repeat(jnp.exp(steps), dims[dim] // shards_of).reshape((-1,) + (1,) * (len(dims) - 1 - dim))
    return loudness


def noise(stream_key, dims, width, reach, pieces=(), kind=jnp.bfloat16):
    values = jax.random.normal(stream_key, dims, jnp.float32) * width
    if len(pieces) > 0:
        values = shard_levels(stream_key, dims, pieces, -0.22, 0.18) * values
    return jnp.clip(values, min=-reach, max=reach).astype(kind)


def setup_inputs(seed: int = 0) -> dict:
    arg_keys = jax.random.split(jax.random.key(seed), 11)
    return {
        "driving": noise(arg_keys[0], (STRIPS, NX, NY), 1.0, 6.0, ((1, 4), (2, 2)), jnp.float32),
        "rate_factor": jnp.clip(jnp.exp(math.log(4.0) - 2.0794415 * jax.random.uniform(arg_keys[1], (STRIPS, NX, NY), jnp.float32) ** shard_levels(arg_keys[1], (STRIPS, NX, NY), ((1, 4), (2, 2)), -0.2, 0.2)), 0.5, 4.0),
        "friction_init": jnp.clip(jnp.exp(math.log(2.0) - 2.3025851 * jax.random.uniform(arg_keys[2], (STRIPS, NX, NY), jnp.float32) ** shard_levels(arg_keys[2], (STRIPS, NX, NY), ((1, 4), (2, 2)), -0.2, 0.2)), 0.2, 2.0),
        "ice_mask": plant((jax.random.randint(arg_keys[3], (STRIPS, NX, NY), 0, 10) < 9).astype(jnp.int32), jax.random.fold_in(arg_keys[3], 1), 0, 1),
        "grounded_mask": plant((jax.random.randint(arg_keys[4], (STRIPS, NX, NY), 0, 4) < 3).astype(jnp.int32), jax.random.fold_in(arg_keys[4], 1), 0, 1),
        "melt": jnp.clip(jnp.exp(math.log(1.0) - 2.3025851 * jax.random.uniform(arg_keys[5], (STRIPS, NX, NY), jnp.float32) ** shard_levels(arg_keys[5], (STRIPS, NX, NY), ((1, 4), (2, 2)), -0.2, 0.2)), 0.1, 1.0),
        "transmissivity": jnp.clip(jnp.exp(math.log(5.0) - 2.3025851 * jax.random.uniform(arg_keys[6], (STRIPS, NX, NY), jnp.float32) ** shard_levels(arg_keys[6], (STRIPS, NX, NY), ((1, 4), (2, 2)), -0.2, 0.2)), 0.5, 5.0),
        "leakage": jnp.clip(jnp.exp(math.log(0.5) - 2.3025851 * jax.random.uniform(arg_keys[7], (STRIPS, NX, NY), jnp.float32) ** shard_levels(arg_keys[7], (STRIPS, NX, NY), ((1, 4), (2, 2)), -0.2, 0.2)), 0.05, 0.5),
        "overburden": jnp.clip(jnp.exp(math.log(2.0) - 1.3862944 * jax.random.uniform(arg_keys[8], (STRIPS, NX, NY), jnp.float32) ** shard_levels(arg_keys[8], (STRIPS, NX, NY), ((1, 4), (2, 2)), -0.2, 0.2)), 0.5, 2.0),
        "friction_scale": jnp.clip(jnp.exp(math.log(4.0) - 2.0794415 * jax.random.uniform(arg_keys[9], (STRIPS, NX, NY), jnp.float32) ** shard_levels(arg_keys[9], (STRIPS, NX, NY), ((1, 4), (2, 2)), -0.2, 0.2)), 0.5, 4.0),
    }


VERT = 4.0
FLOOR = 0.25
HEATING = 0.5


def shifted(values_in):
    padded = jnp.pad(values_in, ((0, 0), (1, 1), (1, 1)))
    return padded[:, 2:, 1:-1], padded[:, :-2, 1:-1], padded[:, 1:-1, 2:], padded[:, 1:-1, :-2]


def ice_core(velocity, x_plus, x_minus, y_plus, y_minus, driving, rate_here, friction, icemask):
    layers = velocity.shape[0]
    vertical = jnp.concatenate([velocity[1:] - velocity[:-1], jnp.zeros_like(velocity[:1])], axis=0)
    strain = vertical * vertical + 0.25 * (x_plus - x_minus) ** 2 + 0.25 * (y_plus - y_minus) ** 2 + FLOOR
    viscous = rate_here * strain ** (-1.0 / 3.0)
    coupling = VERT * 0.5 * (viscous[:-1] + viscous[1:])
    right_side = driving + viscous * (x_plus + x_minus + y_plus + y_minus)
    ratios = []
    values = []
    for level_k in range(layers):
        pivot_k = 4.0 * viscous[level_k]
        term_k = right_side[level_k]
        if level_k < layers - 1:
            pivot_k = pivot_k + coupling[level_k]
        if level_k > 0:
            pivot_k = pivot_k + coupling[level_k - 1] - coupling[level_k - 1] * ratios[level_k - 1]
            term_k = term_k + coupling[level_k - 1] * values[level_k - 1]
        else:
            pivot_k = pivot_k + friction
        values.append(term_k / pivot_k)
        if level_k < layers - 1:
            ratios.append(coupling[level_k] / pivot_k)
    result = [values[-1]]
    for level_k in range(layers - 2, -1, -1):
        result.insert(0, values[level_k] + ratios[level_k] * result[0])
    return jnp.stack(result) * icemask


def water_sweep(pressure, trans_eff, leakage, source):
    press_views = shifted(pressure)
    trans_views = shifted(trans_eff)
    numerator = source
    denominator = leakage
    for trans_next, press_next in zip(trans_views, press_views):
        face_weight = 0.5 * (trans_eff + trans_next)
        numerator = numerator + face_weight * press_next
        denominator = denominator + face_weight
    return numerator / denominator


def reference(driving, rate_factor, friction_init, ice_mask, grounded_mask, melt, transmissivity, leakage, overburden, friction_scale):
    icemask = ice_mask.astype(jnp.float32)
    grounded = grounded_mask.astype(jnp.float32)
    friction = friction_init * grounded
    pressure = overburden
    velocity = jnp.zeros((STRIPS, LAYERS, NX, NY), jnp.float32)

    def solve_sector(parts):
        current, drive_in, rate_in, fric_in, mask_in = parts
        x_plus, x_minus, y_plus, y_minus = shifted(current)
        return ice_core(current, x_plus, x_minus, y_plus, y_minus, drive_in, rate_in, fric_in, mask_in)

    for picard in range(PICARD):
        velocity = lax.map(solve_sector, (velocity, driving, rate_factor, friction, icemask))
        sliding = velocity[:, 0]
        squared = sliding * sliding
        trans_eff = transmissivity * (1.0 + squared / (1.0 + squared))
        source = melt + HEATING * friction * squared
        for sweep_i in range(SWEEPS):
            pressure = water_sweep(pressure, trans_eff, leakage, source)
        friction = friction_scale * pressure * grounded
    ice_part = jnp.stack([velocity[:, -1], velocity[:, 0], friction], axis=1)
    return jnp.concatenate([ice_part, pressure[None]], axis=0)
```

```python
import functools

import jax
import jax.numpy as jnp
import numpy as np
from jax import lax
from jax.experimental import pallas as pl
from jax.experimental.pallas import tpu as pltpu
from jax.sharding import PartitionSpec as P

LAYERS = 40
SWEEPS = 4
VERT = 4.0
FLOOR = 0.25
HEATING = 0.5

RIM = 8
HALF = RIM // 2
RESCALE = 10
THIRD = -1.0 / (3.0 * float(np.log(2.0)))
MESH = pl.DeviceIdType.MESH


def basal_response():
    matrix = np.zeros((LAYERS, LAYERS))
    for k in range(LAYERS):
        matrix[k, k] = 4.0 + (VERT if k > 0 else 0.0) + (VERT if k < LAYERS - 1 else 0.0)
        if k > 0:
            matrix[k, k - 1] = matrix[k - 1, k] = -VERT
    unit = np.zeros(LAYERS)
    unit[0] = 1.0
    return np.linalg.solve(matrix, unit)


def turn(values, shift, axis):
    return pltpu.roll(values, shift % values.shape[axis], axis)


def neighbours(f):
    return turn(f, -1, 0), turn(f, 1, 0), turn(f, -1, 1), turn(f, 1, 1)


def water_solve(pressure, trans_eff, leakage, source, valid):
    faces = [0.5 * (trans_eff + t) for t in neighbours(trans_eff)]
    total = leakage + ((faces[0] + faces[1]) + (faces[2] + faces[3]))
    inverse = jnp.where(valid, 1.0 / total, 0.0)
    weights = [f * inverse for f in faces]
    base = source * inverse
    for _ in range(SWEEPS):
        parts = [w * p for w, p in zip(weights, neighbours(pressure))]
        pressure = base + ((parts[0] + parts[1]) + (parts[2] + parts[3]))
    return pressure


def kernel(sectors, nx, ny, *refs):
    ins = refs[:10]
    out = refs[10]
    own_f, own_i, floats, ints, near, far, pack_near, pack_far, q_ref, g_ref, r_ref, send_p, results = refs[11:24]
    in_sem, send_sem, recv_sem, credit, out_send, out_recv = refs[24:]
    rows, lanes = ins[0].shape[1:]
    ext = rows + 2 * RIM
    wide_map = ny > 2
    sec = lax.axis_index("sec")
    gx = lax.axis_index("gx")
    gy = lax.axis_index("gy")
    odd = lax.rem(gy, 2)
    even = 1 - odd
    is_odd = odd == 1
    is_even = odd == 0
    partner = gy + even - odd
    far_to = gy + 2 * odd - 2 * even
    far_from = gy + 2 * even - 2 * odd
    strip = lax.rem(sec, sectors)
    is_ice = sec < sectors
    is_water = jnp.logical_not(is_ice)
    sends_last = jnp.logical_and(sec > 0, is_ice)
    below, above = gx > 0, gx < nx - 1

    def in_map(y):
        return jnp.logical_and(y >= 0, y < ny)

    def both(*conditions):
        return functools.reduce(jnp.logical_and, conditions)

    def number(condition):
        return condition.astype(jnp.int32)

    float_ids = (0, 1, 2, 5, 6, 7, 8, 9)
    int_ids = (3, 4)
    for slot, arg in enumerate(float_ids):
        pltpu.make_async_copy(ins[arg].at[strip], own_f.at[slot], in_sem.at[0]).start()
    for slot, arg in enumerate(int_ids):
        pltpu.make_async_copy(ins[arg].at[strip], own_i.at[slot], in_sem.at[1]).start()

    barrier = pltpu.get_barrier_semaphore()

    def signal(condition, sem, target):
        @pl.when(condition)
        def _():
            pl.semaphore_signal(sem, inc=1, device_id=target, device_id_type=MESH)

    signal(above, barrier, {"gx": gx + 1, "gy": partner})
    signal(above, barrier, {"gx": gx + 1})
    signal(is_odd, barrier, {"gy": partner})
    signal(sends_last, barrier, {"sec": sectors, "gy": partner})
    count = number(is_even) + 2 * number(below) + jnp.where(is_ice, 0, sectors - 1)
    if wide_map:
        for y in (gy - 2, gy + 2):
            signal(both(above, in_map(y)), barrier, {"gx": gx + 1, "gy": y})
            count = count + number(both(below, in_map(y)))
        signal(in_map(gy + 2), barrier, {"gy": gy + 2})
        count = count + number(in_map(gy - 2))

    @pl.when(count > 0)
    def _():
        pl.semaphore_wait(barrier, count)

    signal(below, credit.at[0], {"gx": gx - 1, "gy": partner})
    signal(below, credit.at[0], {"gx": gx - 1})
    signal(is_even, credit.at[1], {"gy": partner})
    for s in range(1, sectors):
        signal(is_water, credit.at[3], {"sec": s, "gy": partner})
    if wide_map:
        signal(both(below, in_map(far_from)), credit.at[0], {"gx": gx - 1, "gy": far_from})
        signal(both(is_odd, in_map(gy - 2)), credit.at[2], {"gy": gy - 2})

    for sem, buffer in enumerate((own_f, own_i)):
        pltpu.make_async_copy(buffer, buffer, in_sem.at[sem]).wait()

    def remote(src, dst, m, target):
        return pltpu.make_async_remote_copy(
            src_ref=src, dst_ref=dst, send_sem=send_sem.at[m], recv_sem=recv_sem.at[m],
            device_id=target, device_id_type=MESH,
        )

    def main_copies():
        target = {"gy": partner}
        at = pl.ds(RIM, rows)
        return [remote(own_f, floats.at[:, at], 0, target), remote(own_i, ints.at[:, at], 1, target)]

    def edge_copies(dx):
        target = {"gx": gx + dx, "gy": partner}
        src = pl.ds(rows - RIM if dx > 0 else 0, RIM)
        dst = pl.ds(0 if dx > 0 else RIM + rows, RIM)
        m = 2 + 2 * (dx > 0)
        return [
            remote(own_f.at[:, src], floats.at[:, dst], m, target),
            remote(own_i.at[:, src], ints.at[:, dst], m + 1, target),
        ]

    def corner_copy(dx):
        return remote(
            pack_near.at[int(dx > 0)], near.at[int(dx < 0)], 6 + (dx > 0), {"gx": gx + dx}
        )

    def far_copy(dx):
        src = pl.ds({-1: 0, 0: 0, 1: rows - RIM}[dx], rows if dx == 0 else RIM)
        dst = pl.ds({-1: RIM + rows, 0: RIM, 1: 0}[dx], rows if dx == 0 else RIM)
        return remote(pack_far.at[src], far.at[dst], 9 + dx, {"gx": gx + dx, "gy": far_to})

    def x_copies(dx):
        return [*edge_copies(dx), corner_copy(dx)]

    def pack(top, height, parity):
        group = (lax.broadcasted_iota(jnp.int32, (height, lanes), 1) // RIM + parity) % (lanes // RIM)
        packed = jnp.zeros((height, lanes), jnp.float32)
        for i in range(10):
            f = own_f[i, top : top + height] if i < 8 else own_i[i - 8, top : top + height].astype(jnp.float32)
            packed = jnp.where(group == i, turn(f, RIM * i, 1), packed)
        return packed

    pack_near[0] = pack(0, RIM, even)
    pack_near[1] = pack(rows - RIM, RIM, even)
    if wide_map:
        pack_far[...] = pack(0, rows, odd)

    def start(condition, copies):
        @pl.when(condition)
        def _():
            for c in copies:
                c.start()

    def wait_send(condition, copies):
        @pl.when(condition)
        def _():
            for c in copies:
                c.wait_send()

    def arrive(condition, copies):
        @pl.when(condition)
        def _():
            for c in copies:
                c.wait_recv()

    def await_credit(condition, which, amount):
        @pl.when(condition)
        def _():
            pl.semaphore_wait(credit.at[which], amount)

    start(below, x_copies(-1))
    if wide_map:
        start(both(below, in_map(far_to)), [far_copy(-1)])
    await_credit(is_odd, 1, 1)
    for c in main_copies():
        c.start()
    if wide_map:
        await_credit(both(is_odd, in_map(far_to)), 2, 1)
        start(in_map(far_to), [far_copy(0)])
    await_credit(above, 0, 2 + number(in_map(far_to)) if wide_map else 2)
    start(above, x_copies(1))
    if wide_map:
        start(both(above, in_map(far_to)), [far_copy(1)])

    w = basal_response()
    tall = rows + RIM
    tiles = tall // 8
    wide = 2 * RIM
    slot = lax.broadcasted_iota(jnp.int32, (8, lanes), 1) // wide
    lane_low = jnp.where(partner < ny - 1, lanes + RIM, lanes)
    lane_high = jnp.where(partner > 0, 2 * lanes - RIM, 2 * lanes)

    def in_map_lanes(height):
        lane_i = lax.broadcasted_iota(jnp.int32, (height, 2 * lanes), 1)
        return jnp.logical_or(lane_i < lane_low, lane_i >= lane_high)

    def field_reader(top, height, valid):
        at = slice(top, top + height)
        lane = lax.broadcasted_iota(jnp.int32, (height, lanes), 1)
        is_near = (lane >= lanes // 2) == is_even

        def field(i, fill):
            main = floats[i, at] if i < 8 else ints[i - 8, at].astype(jnp.float32)
            rim = own_f[i] if i < 8 else own_i[i - 8].astype(jnp.float32)
            if height > rows:
                rim = jnp.concatenate([turn(near[0], -RIM * i, 1), rim, turn(near[1], -RIM * i, 1)], axis=0)
            if wide_map:
                rim = jnp.where(is_near, rim, turn(far[at], -RIM * i, 1))
            return jnp.where(valid, jnp.concatenate([main, rim], axis=1), fill)

        return field

    def first_velocity(driving, rate, friction, ice):
        viscous = rate * float(FLOOR ** (-1.0 / 3.0))
        speed = driving / (4.0 * viscous)
        drop = -speed * friction / (viscous + friction * float(w[0]))
        return speed * ice, drop * ice

    def squeeze(f, which):
        tile = jnp.zeros((8, lanes), jnp.float32)
        for n, t in enumerate(which):
            moved = turn(f[8 * t : 8 * t + 8, lanes:], wide * n + RIM, 1)
            tile = jnp.where(slot == n, moved, tile)
        return jnp.concatenate([f[8 * t : 8 * t + 8, :lanes] for t in which] + [tile], axis=0)

    def spread(f, count):
        last = f[8 * count :]
        return [
            jnp.concatenate([f[8 * n : 8 * n + 8], turn(last, -(wide * n + RIM), 1)], axis=1)
            for n in range(count)
        ]

    def eliminate(speed, drop, driving, rate, which, offset, lead):
        sxp, sxm, syp, sym = neighbours(speed)
        dxp, dxm, dyp, dym = neighbours(drop)
        sdx, sdy, ddx, ddy = sxp - sxm, syp - sym, dxp - dxm, dyp - dym
        flat = [
            0.03125 * (sdx * sdx + sdy * sdy) + 0.125 * FLOOR,
            0.0625 * (sdx * ddx + sdy * ddy),
            0.03125 * (ddx * ddx + ddy * ddy),
            0.125 * drop * drop,
            0.25 * ((sxp + sxm) + (syp + sym)),
            0.25 * ((dxp + dxm) + (dyp + dym)),
            driving * (0.5 / rate),
        ]
        flat = [squeeze(turn(f, lead, 0), which) for f in flat]
        for n in range(len(which) + 1):
            at = slice(offset + 8 * n, offset + 8 * n + 8)
            c0, c1, c2, c3, n0, n1, dr = [f[8 * n : 8 * n + 8] for f in flat]
            before = None
            for k in range(LAYERS):
                wk = float(w[k])
                strain = c0 + (c1 * wk + c2 * (wk * wk))
                if k < LAYERS - 1:
                    strain = strain + c3 * float((w[k + 1] - w[k]) ** 2)
                twice = jnp.exp2(jnp.log(strain) * THIRD)
                q_ref[k, at] = twice
                r_ref[k, at] = dr + twice * (n0 + n1 * wk)
                if k > 0:
                    g_ref[k - 1, at] = 0.5 * (before + twice)
                before = twice

        at = slice(offset, offset + 8 * (len(which) + 1))
        up_d, up_e, up_t = None, q_ref[0, at], r_ref[0, at]
        down_d, down_e, down_t = None, q_ref[LAYERS - 1, at], r_ref[LAYERS - 1, at]
        product = None

        def step(d, e, t, g, q, r):
            d = e + (g if d is None else g * d)
            return d, q * d + g * e, r * d + g * t

        for k in range(LAYERS - 1):
            j = LAYERS - 2 - k
            g = g_ref[k, at]
            product = g if product is None else product * g
            up_d, up_e, up_t = step(up_d, up_e, up_t, g, q_ref[k + 1, at], r_ref[k + 1, at])
            down_d, down_e, down_t = step(
                down_d, down_e, down_t, g_ref[j, at], q_ref[j, at], r_ref[j, at]
            )
            if k % RESCALE == RESCALE - 1 and k < LAYERS - 2:
                shrink = 1.0 / up_d
                up_d, up_e, up_t, product = None, up_e * shrink, up_t * shrink, product * shrink
                shrink = 1.0 / down_d
                down_d, down_e, down_t = None, down_e * shrink, down_t * shrink
        shrink = 1.0 / up_e
        return down_d, down_e, down_t, up_t * shrink, product * shrink

    def finish(parts, friction, rate, ice, which):
        down_d, down_e, down_t, top, reach = parts
        base = squeeze(turn(friction * (0.5 / rate), -HALF, 0), which)
        mask = squeeze(turn(ice, -HALF, 0), which)
        basal = down_t / (down_e + base * down_d)
        surface = top - base * basal * reach
        return [spread(f * mask, len(which)) for f in (basal, surface)]

    arrive(gx >= 0, main_copies())
    if wide_map:
        arrive(in_map(far_from), [far_copy(0)])
    early = list(range(1, tiles - 1))
    late = [0, tiles - 1]
    field = field_reader(RIM, rows, in_map_lanes(rows))
    driving, rate = field(0, 0.0), field(1, 1.0)
    speed, drop = first_velocity(driving, rate, field(2, 0.0) * field(9, 0.0), field(8, 0.0))
    early_parts = eliminate(speed, drop, driving, rate, early, 0, HALF)
    for dx, condition in ((-1, above), (1, below)):
        arrive(condition, x_copies(dx))
        if wide_map:
            arrive(both(condition, in_map(far_from)), [far_copy(dx)])

    row_i = lax.broadcasted_iota(jnp.int32, (ext, 2 * lanes), 0)
    row_low = jnp.where(gx > 0, 0, RIM)
    row_high = jnp.where(gx < nx - 1, ext, RIM + rows)
    valid = jnp.logical_and(
        jnp.logical_and(row_i >= row_low, row_i < row_high), in_map_lanes(ext)
    )
    field = field_reader(0, ext, valid)
    driving = field(0, 0.0)
    rate = field(1, 1.0)
    friction = field(2, 0.0)
    melt = field(3, 0.0)
    trans = field(4, 0.0)
    leakage = field(5, 1.0)
    pressure = field(6, 0.0)
    scale = field(7, 0.0)
    ice = field(8, 0.0)
    grounded = field(9, 0.0)
    friction = friction * grounded
    scale = scale * grounded

    speed, drop = first_velocity(driving, rate, friction, ice)
    sliding = speed + drop * float(w[0])
    squared = sliding * sliding
    trans_eff = trans * (1.0 + squared / (1.0 + squared))
    source = melt + HEATING * friction * squared
    pressure = water_solve(pressure, trans_eff, leakage, source, valid)
    friction = scale * pressure

    late_parts = eliminate(speed, drop, driving, rate, late, 8 * (len(early) + 1), -HALF)
    pieces = [None] * tiles
    for parts, which in ((early_parts, early), (late_parts, late)):
        for n, piece in enumerate(zip(*finish(parts, friction, rate, ice, which))):
            pieces[which[n]] = piece
    blank = jnp.zeros((RIM, 2 * lanes), jnp.float32)
    basal = turn(jnp.concatenate([p[0] for p in pieces] + [blank], axis=0), HALF, 0)
    surface = jnp.concatenate([p[1][:, :lanes] for p in pieces], axis=0)
    sliding = jnp.where(valid, basal, 0.0)
    squared = sliding * sliding
    trans_eff = trans * (1.0 + squared / (1.0 + squared))
    source = melt + HEATING * friction * squared
    pressure = water_solve(pressure, trans_eff, leakage, source, valid)
    block = pressure[RIM : RIM + rows, :lanes]
    send_p[...] = block

    def result_copy(src, plane, m, target):
        return pltpu.make_async_remote_copy(
            src_ref=src, dst_ref=out.at[0, plane], send_sem=out_send.at[m], recv_sem=out_recv.at[plane],
            device_id=target, device_id_type=MESH,
        )

    def water_copy():
        return result_copy(send_p, strip, sectors, {"sec": sectors, "gy": partner})

    def own_copy():
        return result_copy(send_p, 0, 0, {"gy": partner})

    def ice_copies():
        return [result_copy(results.at[n], n, n, {"gy": partner}) for n in range(3)]

    await_credit(sends_last, 3, 1)
    start(sends_last, [water_copy()])
    start(is_water, [own_copy()])

    @pl.when(is_ice)
    def _():
        results[0] = turn(surface, -HALF, 0)[:rows]
        results[1] = sliding[RIM : RIM + rows, :lanes]
        results[2] = scale[RIM : RIM + rows, :lanes] * block
        for c in ice_copies():
            c.start()

    for c in main_copies():
        c.wait_send()
    if wide_map:
        wait_send(in_map(far_to), [far_copy(0)])
    for dx, condition in ((-1, below), (1, above)):
        wait_send(condition, x_copies(dx))
        if wide_map:
            wait_send(both(condition, in_map(far_to)), [far_copy(dx)])
    wait_send(sends_last, [water_copy()])
    wait_send(is_water, [own_copy()])
    wait_send(is_ice, ice_copies())
    for plane in range(3):
        result_copy(send_p, plane, 0, {"gy": partner}).wait_recv()


def on_device(nx, ny, *args):
    sectors, rows, lanes = args[0].shape
    ext = rows + 2 * RIM
    f32 = jnp.float32
    vmem = pltpu.VMEM
    dma = pltpu.SemaphoreType.DMA
    return pl.pallas_call(
        functools.partial(kernel, sectors, nx, ny),
        out_shape=pltpu.VMEM((1, sectors, rows, lanes), f32),
        in_specs=[pl.BlockSpec(memory_space=pltpu.HBM)] * len(args),
        out_specs=pl.BlockSpec(memory_space=pltpu.VMEM),
        scratch_shapes=[
            vmem((8, rows, lanes), f32),
            vmem((2, rows, lanes), jnp.int32),
            vmem((8, ext, lanes), f32),
            vmem((2, ext, lanes), jnp.int32),
            vmem((2, RIM, lanes), f32),
            vmem((ext, lanes), f32),
            vmem((2, RIM, lanes), f32),
            vmem((rows, lanes), f32),
            vmem((LAYERS, ext + RIM, lanes), f32),
            vmem((LAYERS, ext + RIM, lanes), f32),
            vmem((LAYERS, ext + RIM, lanes), f32),
            vmem((rows, lanes), f32),
            vmem((3, rows, lanes), f32),
            dma((2,)),
            dma((11,)),
            dma((11,)),
            pltpu.SemaphoreType.REGULAR((4,)),
            dma((4,)),
            dma((3,)),
        ],
        compiler_params=pltpu.CompilerParams(collective_id=0, has_side_effects=True),
    )(*args)


def solution(mesh):
    spec = P(None, "gx", "gy")
    return jax.shard_map(
        functools.partial(on_device, mesh.shape["gx"], mesh.shape["gy"]),
        mesh=mesh,
        in_specs=(spec,) * 10,
        out_specs=P("sec", None, "gx", "gy"),
        check_vma=False,
    )
```

```python
import functools

import jax
import jax.numpy as jnp
import numpy as np
from jax import lax
from jax.experimental import pallas as pl
from jax.experimental.pallas import tpu as pltpu
from jax.sharding import PartitionSpec as P

LAYERS = 40
SWEEPS = 4
VERT = 4.0
FLOOR = 0.25
HEATING = 0.5

RIM = 8
HALF = RIM // 2
RESCALE = 10
THIRD = -1.0 / (3.0 * float(np.log(2.0)))
DIRECTIONS = [(dx, dy) for dx in (-1, 0, 1) for dy in (-1, 0, 1) if (dx, dy) != (0, 0)]
MESH = pl.DeviceIdType.MESH


def basal_response():
    matrix = np.zeros((LAYERS, LAYERS))
    for k in range(LAYERS):
        matrix[k, k] = 4.0 + (VERT if k > 0 else 0.0) + (VERT if k < LAYERS - 1 else 0.0)
        if k > 0:
            matrix[k, k - 1] = matrix[k - 1, k] = -VERT
    unit = np.zeros(LAYERS)
    unit[0] = 1.0
    return np.linalg.solve(matrix, unit)


def turn(values, shift, axis):
    return pltpu.roll(values, shift % values.shape[axis], axis)


def neighbours(f):
    return turn(f, -1, 0), turn(f, 1, 0), turn(f, -1, 1), turn(f, 1, 1)


def water_solve(pressure, trans_eff, leakage, source, valid):
    faces = [0.5 * (trans_eff + t) for t in neighbours(trans_eff)]
    total = leakage + ((faces[0] + faces[1]) + (faces[2] + faces[3]))
    inverse = jnp.where(valid, 1.0 / total, 0.0)
    weights = [f * inverse for f in faces]
    base = source * inverse
    for _ in range(SWEEPS):
        parts = [w * p for w, p in zip(weights, neighbours(pressure))]
        pressure = base + ((parts[0] + parts[1]) + (parts[2] + parts[3]))
    return pressure


def wide_kernel(sectors, nx, ny, *refs):
    ins = refs[:10]
    out = refs[10]
    floats, ints, pack_l, pack_r, rim_l, rim_r, q_ref, g_ref, r_ref, send_p = refs[11:21]
    in_sem, send_sem, recv_sem, last_send, last_recv = refs[21:]
    rows, lanes = ins[0].shape[1:]
    sec = lax.axis_index("sec")
    gx = lax.axis_index("gx")
    gy = lax.axis_index("gy")
    strip = lax.rem(sec, sectors)
    is_ice = sec < sectors
    sends_last = jnp.logical_and(sec > 0, is_ice)

    def exists(dx, dy):
        x, y = gx + dx, gy + dy
        return jnp.logical_and(
            jnp.logical_and(x >= 0, x < nx), jnp.logical_and(y >= 0, y < ny)
        )

    float_ids = (0, 1, 2, 5, 6, 7, 8, 9)
    int_ids = (3, 4)
    loads = []
    for slot, arg in enumerate(float_ids):
        loads.append(pltpu.make_async_copy(ins[arg].at[strip], floats.at[slot, pl.ds(RIM, rows)], in_sem.at[0]))
    for slot, arg in enumerate(int_ids):
        loads.append(pltpu.make_async_copy(ins[arg].at[strip], ints.at[slot, pl.ds(RIM, rows)], in_sem.at[1]))
    barrier = pltpu.get_barrier_semaphore()
    count = jnp.int32(0)
    for dx, dy in sorted(DIRECTIONS, key=lambda d: -abs(d[0])):
        here = exists(dx, dy)
        count = count + here.astype(jnp.int32)

        @pl.when(here)
        def _(dx=dx, dy=dy):
            pl.semaphore_signal(barrier, inc=1, device_id={"gx": gx + dx, "gy": gy + dy}, device_id_type=MESH)

    count = count + sends_last.astype(jnp.int32)
    count = count + jnp.where(is_ice, 0, sectors - 1)

    @pl.when(sends_last)
    def _():
        pl.semaphore_signal(barrier, inc=1, device_id={"sec": sectors}, device_id_type=MESH)

    for s in range(1, sectors):

        @pl.when(jnp.logical_not(is_ice))
        def _(s=s):
            pl.semaphore_signal(barrier, inc=1, device_id={"sec": s}, device_id_type=MESH)

    for load in loads:
        load.start()
    for slot, buffer in enumerate((floats, ints)):
        mine = buffer.at[:, pl.ds(RIM, rows)]
        pltpu.make_async_copy(mine, mine, in_sem.at[slot]).wait()

    lane = lax.broadcasted_iota(jnp.int32, (rows, lanes), 1)
    fields = [floats[i, RIM : RIM + rows] for i in range(8)]
    fields += [ints[i, RIM : RIM + rows].astype(jnp.float32) for i in range(2)]
    left = jnp.zeros((rows, lanes), jnp.float32)
    right = jnp.zeros((rows, lanes), jnp.float32)
    for i, f in enumerate(fields):
        moved = turn(f, RIM * i, 1)
        group = lane // RIM
        left = jnp.where(group == i, moved, left)
        right = jnp.where(group == (i - 1) % (lanes // RIM), moved, right)
    pack_l[...] = left
    pack_r[...] = right

    pl.semaphore_wait(barrier, count)

    def copies(dx, dy, n):
        target = {"gx": gx + dx, "gy": gy + dy}

        def remote(src, dst, m):
            return pltpu.make_async_remote_copy(
                src_ref=src, dst_ref=dst, send_sem=send_sem.at[m], recv_sem=recv_sem.at[m],
                device_id=target, device_id_type=MESH,
            )

        if dy == 0:
            first = rows if dx > 0 else RIM
            landing = 0 if dx > 0 else RIM + rows
            return [
                remote(floats.at[:, pl.ds(first, RIM)], floats.at[:, pl.ds(landing, RIM)], n),
                remote(ints.at[:, pl.ds(first, RIM)], ints.at[:, pl.ds(landing, RIM)], 8 + (dx > 0)),
            ]
        src, dst = (pack_r, rim_l) if dy > 0 else (pack_l, rim_r)
        if dx == 0:
            return [remote(src, dst.at[pl.ds(RIM, rows)], n)]
        first = rows - RIM if dx > 0 else 0
        landing = 0 if dx > 0 else RIM + rows
        return [remote(src.at[pl.ds(first, RIM)], dst.at[pl.ds(landing, RIM)], n)]

    order = sorted(range(8), key=lambda n: abs(DIRECTIONS[n][1]))
    for n in order:
        dx, dy = DIRECTIONS[n]

        @pl.when(exists(dx, dy))
        def _(dx=dx, dy=dy, n=n):
            for c in copies(dx, dy, n):
                c.start()

    def arrive(n):
        dx, dy = DIRECTIONS[n]

        @pl.when(exists(-dx, -dy))
        def _():
            for c in copies(dx, dy, n):
                c.wait_recv()

    w = basal_response()
    ext = rows + 2 * RIM
    tall = rows + RIM
    tiles = tall // 8
    wide = 2 * RIM
    slot = lax.broadcasted_iota(jnp.int32, (8, lanes), 1) // wide
    lane_low = jnp.where(gy < ny - 1, lanes + RIM, lanes)
    lane_high = jnp.where(gy > 0, 2 * lanes - RIM, 2 * lanes)

    def in_map_lanes(height):
        lane_i = lax.broadcasted_iota(jnp.int32, (height, 2 * lanes), 1)
        return jnp.logical_or(lane_i < lane_low, lane_i >= lane_high)

    def field_reader(top, height, valid):
        at = slice(top, top + height)
        packed_l, packed_r = rim_l[at], rim_r[at]
        group = lax.broadcasted_iota(jnp.int32, (height, lanes), 1) // RIM

        def field(i, fill):
            main = floats[i, at] if i < 8 else ints[i - 8, at].astype(jnp.float32)
            rim = turn(jnp.where(group == i, packed_r, packed_l), -RIM * i, 1)
            return jnp.where(valid, jnp.concatenate([main, rim], axis=1), fill)

        return field

    def first_velocity(driving, rate, friction, ice):
        viscous = rate * float(FLOOR ** (-1.0 / 3.0))
        speed = driving / (4.0 * viscous)
        drop = -speed * friction / (viscous + friction * float(w[0]))
        return speed * ice, drop * ice

    def squeeze(f, which):
        tile = jnp.zeros((8, lanes), jnp.float32)
        for n, t in enumerate(which):
            moved = turn(f[8 * t : 8 * t + 8, lanes:], wide * n + RIM, 1)
            tile = jnp.where(slot == n, moved, tile)
        return jnp.concatenate([f[8 * t : 8 * t + 8, :lanes] for t in which] + [tile], axis=0)

    def spread(f, count):
        last = f[8 * count :]
        return [
            jnp.concatenate([f[8 * n : 8 * n + 8], turn(last, -(wide * n + RIM), 1)], axis=1)
            for n in range(count)
        ]

    def eliminate(speed, drop, driving, rate, which, offset, lead):
        sxp, sxm, syp, sym = neighbours(speed)
        dxp, dxm, dyp, dym = neighbours(drop)
        sdx, sdy, ddx, ddy = sxp - sxm, syp - sym, dxp - dxm, dyp - dym
        flat = [
            0.03125 * (sdx * sdx + sdy * sdy) + 0.125 * FLOOR,
            0.0625 * (sdx * ddx + sdy * ddy),
            0.03125 * (ddx * ddx + ddy * ddy),
            0.125 * drop * drop,
            0.25 * ((sxp + sxm) + (syp + sym)),
            0.25 * ((dxp + dxm) + (dyp + dym)),
            driving * (0.5 / rate),
        ]
        flat = [squeeze(turn(f, lead, 0), which) for f in flat]
        for n in range(len(which) + 1):
            at = slice(offset + 8 * n, offset + 8 * n + 8)
            c0, c1, c2, c3, n0, n1, dr = [f[8 * n : 8 * n + 8] for f in flat]
            before = None
            for k in range(LAYERS):
                wk = float(w[k])
                strain = c0 + (c1 * wk + c2 * (wk * wk))
                if k < LAYERS - 1:
                    strain = strain + c3 * float((w[k + 1] - w[k]) ** 2)
                twice = jnp.exp2(jnp.log(strain) * THIRD)
                q_ref[k, at] = twice
                r_ref[k, at] = dr + twice * (n0 + n1 * wk)
                if k > 0:
                    g_ref[k - 1, at] = 0.5 * (before + twice)
                before = twice

        at = slice(offset, offset + 8 * (len(which) + 1))
        up_d, up_e, up_t = None, q_ref[0, at], r_ref[0, at]
        down_d, down_e, down_t = None, q_ref[LAYERS - 1, at], r_ref[LAYERS - 1, at]
        product = None

        def step(d, e, t, g, q, r):
            d = e + (g if d is None else g * d)
            return d, q * d + g * e, r * d + g * t

        for k in range(LAYERS - 1):
            j = LAYERS - 2 - k
            g = g_ref[k, at]
            product = g if product is None else product * g
            up_d, up_e, up_t = step(up_d, up_e, up_t, g, q_ref[k + 1, at], r_ref[k + 1, at])
            down_d, down_e, down_t = step(
                down_d, down_e, down_t, g_ref[j, at], q_ref[j, at], r_ref[j, at]
            )
            if k % RESCALE == RESCALE - 1 and k < LAYERS - 2:
                shrink = 1.0 / up_d
                up_d, up_e, up_t, product = None, up_e * shrink, up_t * shrink, product * shrink
                shrink = 1.0 / down_d
                down_d, down_e, down_t = None, down_e * shrink, down_t * shrink
        shrink = 1.0 / up_e
        return down_d, down_e, down_t, up_t * shrink, product * shrink

    def finish(parts, friction, rate, ice, which):
        down_d, down_e, down_t, top, reach = parts
        base = squeeze(turn(friction * (0.5 / rate), -HALF, 0), which)
        mask = squeeze(turn(ice, -HALF, 0), which)
        basal = down_t / (down_e + base * down_d)
        surface = top - base * basal * reach
        return [spread(f * mask, len(which)) for f in (basal, surface)]

    for n in order:
        if DIRECTIONS[n][0] == 0:
            arrive(n)
    early = list(range(1, tiles - 1))
    late = [0, tiles - 1]
    field = field_reader(RIM, rows, in_map_lanes(rows))
    driving, rate = field(0, 0.0), field(1, 1.0)
    speed, drop = first_velocity(driving, rate, field(2, 0.0) * field(9, 0.0), field(8, 0.0))
    early_parts = eliminate(speed, drop, driving, rate, early, 0, HALF)
    for n in order:
        if DIRECTIONS[n][0] != 0:
            arrive(n)

    row_i = lax.broadcasted_iota(jnp.int32, (ext, 2 * lanes), 0)
    row_low = jnp.where(gx > 0, 0, RIM)
    row_high = jnp.where(gx < nx - 1, ext, RIM + rows)
    valid = jnp.logical_and(
        jnp.logical_and(row_i >= row_low, row_i < row_high), in_map_lanes(ext)
    )
    field = field_reader(0, ext, valid)
    driving = field(0, 0.0)
    rate = field(1, 1.0)
    friction = field(2, 0.0)
    melt = field(3, 0.0)
    trans = field(4, 0.0)
    leakage = field(5, 1.0)
    pressure = field(6, 0.0)
    scale = field(7, 0.0)
    ice = field(8, 0.0)
    grounded = field(9, 0.0)
    friction = friction * grounded
    scale = scale * grounded

    speed, drop = first_velocity(driving, rate, friction, ice)
    sliding = speed + drop * float(w[0])
    squared = sliding * sliding
    trans_eff = trans * (1.0 + squared / (1.0 + squared))
    source = melt + HEATING * friction * squared
    pressure = water_solve(pressure, trans_eff, leakage, source, valid)
    friction = scale * pressure

    late_parts = eliminate(speed, drop, driving, rate, late, 8 * (len(early) + 1), -HALF)
    pieces = [None] * tiles
    for parts, which in ((early_parts, early), (late_parts, late)):
        for n, piece in enumerate(zip(*finish(parts, friction, rate, ice, which))):
            pieces[which[n]] = piece
    blank = jnp.zeros((RIM, 2 * lanes), jnp.float32)
    basal = turn(jnp.concatenate([p[0] for p in pieces] + [blank], axis=0), HALF, 0)
    surface = jnp.concatenate([p[1][:, :lanes] for p in pieces], axis=0)
    sliding = jnp.where(valid, basal, 0.0)
    squared = sliding * sliding
    trans_eff = trans * (1.0 + squared / (1.0 + squared))
    source = melt + HEATING * friction * squared
    pressure = water_solve(pressure, trans_eff, leakage, source, valid)
    block = pressure[RIM : RIM + rows, :lanes]
    send_p[...] = block

    def last():
        return pltpu.make_async_remote_copy(
            src_ref=send_p, dst_ref=out.at[0, strip], send_sem=last_send, recv_sem=last_recv.at[strip],
            device_id={"sec": sectors}, device_id_type=MESH,
        )

    @pl.when(sends_last)
    def _():
        last().start()

    @pl.when(is_ice)
    def _():
        out[0, 0] = turn(surface, -HALF, 0)[:rows]
        out[0, 1] = sliding[RIM : RIM + rows, :lanes]
        out[0, 2] = scale[RIM : RIM + rows, :lanes] * block

    @pl.when(jnp.logical_not(is_ice))
    def _():
        out[0, 0] = block

    for n in order:
        dx, dy = DIRECTIONS[n]

        @pl.when(exists(dx, dy))
        def _(dx=dx, dy=dy, n=n):
            for c in copies(dx, dy, n):
                c.wait_send()

    @pl.when(sends_last)
    def _():
        last().wait_send()

    for s in range(1, sectors):

        @pl.when(jnp.logical_not(is_ice))
        def _(s=s):
            pltpu.make_async_remote_copy(
                src_ref=send_p, dst_ref=out.at[0, s], send_sem=last_send, recv_sem=last_recv.at[s],
                device_id={"sec": 0}, device_id_type=MESH,
            ).wait_recv()


def wide_map(nx, ny, *args):
    sectors, rows, lanes = args[0].shape
    ext = rows + 2 * RIM
    f32 = jnp.float32
    vmem = pltpu.VMEM
    dma = pltpu.SemaphoreType.DMA
    return pl.pallas_call(
        functools.partial(wide_kernel, sectors, nx, ny),
        out_shape=pltpu.VMEM((1, sectors, rows, lanes), f32),
        in_specs=[pl.BlockSpec(memory_space=pltpu.HBM)] * len(args),
        out_specs=pl.BlockSpec(memory_space=pltpu.VMEM),
        scratch_shapes=[
            vmem((8, ext, lanes), f32),
            vmem((2, ext, lanes), jnp.int32),
            vmem((rows, lanes), f32),
            vmem((rows, lanes), f32),
            vmem((ext, lanes), f32),
            vmem((ext, lanes), f32),
            vmem((LAYERS, ext + RIM, lanes), f32),
            vmem((LAYERS, ext + RIM, lanes), f32),
            vmem((LAYERS, ext + RIM, lanes), f32),
            vmem((rows, lanes), f32),
            dma((2,)),
            dma((10,)),
            dma((10,)),
            dma,
            dma((sectors,)),
        ],
        compiler_params=pltpu.CompilerParams(collective_id=0, has_side_effects=True),
    )(*args)


def narrow_kernel(sectors, nx, *refs):
    ins = refs[:10]
    out = refs[10]
    own_f, own_i, part_f, part_i, halo_f, halo_i, q_ref, g_ref, r_ref, send_p, results = refs[11:22]
    in_sem, send_sem, recv_sem, credit, out_send, out_recv = refs[22:]
    rows, lanes = ins[0].shape[1:]
    half = rows // 2
    local = half + RIM
    tiles = local // RIM
    sec = lax.axis_index("sec")
    gx = lax.axis_index("gx")
    gy = lax.axis_index("gy")
    partner = 1 - gy
    is_odd = gy == 1
    is_even = gy == 0
    strip = lax.rem(sec, sectors)
    is_ice = sec < sectors
    is_water = jnp.logical_not(is_ice)
    sends_last = jnp.logical_and(sec > 0, is_ice)
    below, above = gx > 0, gx < nx - 1
    low = jnp.where(sec == 0, 0, 1)
    high = 1 - low
    is_low = gy == low
    is_high = gy == high
    part_low = jnp.where(is_low, 0, rows - local)
    has_halo = jnp.logical_or(jnp.logical_and(is_low, below), jnp.logical_and(is_high, above))

    def both(p, q):
        return jnp.logical_and(p, q)

    def number(condition):
        return condition.astype(jnp.int32)

    def copy_in(n):
        arg = (0, 1, 2, 5, 6, 7, 8, 9, 3, 4)[n]
        dst = own_f.at[n] if n < 8 else own_i.at[n - 8]
        return pltpu.make_async_copy(ins[arg].at[strip], dst, in_sem.at[int(n >= 8)])

    for n in range(10):
        copy_in(n).start()

    barrier = pltpu.get_barrier_semaphore()

    def signal(condition, sem, target):
        @pl.when(condition)
        def _():
            pl.semaphore_signal(sem, inc=1, device_id=target, device_id_type=MESH)

    signal(above, barrier, {"gx": gx + 1, "gy": low})
    signal(both(above, is_high), barrier, {"gx": gx + 1, "gy": high})
    signal(is_odd, barrier, {"gy": partner})
    signal(sends_last, barrier, {"sec": sectors, "gy": partner})
    signal(sends_last, barrier, {"sec": sectors})
    count = number(is_even) + number(below) + number(both(below, is_low)) + jnp.where(is_ice, 0, 2 * (sectors - 1))

    @pl.when(count > 0)
    def _():
        pl.semaphore_wait(barrier, count)

    signal(both(below, is_low), credit.at[0], {"gx": gx - 1, "gy": partner})
    signal(both(below, is_low), credit.at[0], {"gx": gx - 1})
    signal(is_even, credit.at[1], {"gy": partner})
    for s in range(1, sectors):
        signal(is_water, credit.at[2], {"sec": s, "gy": partner})
        signal(is_water, credit.at[2], {"sec": s})

    for sem, buffer in enumerate((own_f, own_i)):
        pltpu.make_async_copy(buffer, buffer, in_sem.at[sem]).wait()

    def remote(src, dst, m, k, target):
        return pltpu.make_async_remote_copy(
            src_ref=src, dst_ref=dst, send_sem=send_sem.at[m], recv_sem=recv_sem.at[k],
            device_id=target, device_id_type=MESH,
        )

    def main_copies():
        at = pl.ds(pl.multiple_of(rows - local - part_low, RIM), local)
        return [
            remote(own_f.at[:, at], part_f, 0, 0, {"gy": partner}),
            remote(own_i.at[:, at], part_i, 1, 1, {"gy": partner}),
        ]

    def edge_copies(dx, region):
        src = pl.ds(half * (dx + 1) - RIM * (dx > 0), RIM)
        target = {"gx": gx + dx, "gy": low if dx > 0 else high}
        return [
            remote(own_f.at[:, src], halo_f.at[region], 3 + dx, 2 + region, target),
            remote(own_i.at[:, src], halo_i.at[region], 4 + dx, 4 + region, target),
        ]

    def start(condition, copies):
        @pl.when(condition)
        def _():
            for c in copies:
                c.start()

    def wait_send(condition, copies):
        @pl.when(condition)
        def _():
            for c in copies:
                c.wait_send()

    def await_credit(condition, which, amount):
        @pl.when(condition)
        def _():
            pl.semaphore_wait(credit.at[which], amount)

    start(below, edge_copies(-1, gy))
    await_credit(is_odd, 1, 1)
    for c in main_copies():
        c.start()
    await_credit(above, 0, 1)
    start(above, edge_copies(1, gy))

    w = basal_response()
    wide = 2 * lanes
    lane = lax.broadcasted_iota(jnp.int32, (RIM, wide), 1)
    upper_sub = lax.broadcasted_iota(jnp.int32, (RIM, wide), 0) >= HALF
    halo_in_late = upper_sub == is_low
    edge = jnp.where(is_even, wide, lanes)
    last_lane = lane == edge - 1
    first_lane = lane == lax.rem(edge, wide)

    def join(parts):
        return jnp.concatenate(parts, axis=0)

    def tall_mask(mask, count):
        return join([mask] * count)

    def field_local(i):
        at = pl.ds(pl.multiple_of(part_low, RIM), local)
        a = own_f[i, at] if i < 8 else own_i[i - 8, at].astype(jnp.float32)
        b = part_f[i] if i < 8 else part_i[i - 8].astype(jnp.float32)
        return jnp.concatenate([a, b], axis=1)

    def field_halo(i, fill):
        a, b = [halo_f[r, i] if i < 8 else halo_i[r, i - 8].astype(jnp.float32) for r in (gy, partner)]
        return jnp.where(has_halo, jnp.concatenate([a, b], axis=1), fill)

    def first_velocity(driving, rate, friction, ice):
        viscous = rate * float(FLOOR ** (-1.0 / 3.0))
        speed = driving / (4.0 * viscous)
        drop = -speed * friction / (viscous + friction * float(w[0]))
        return speed * ice, drop * ice

    def shifts(f):
        count = f.shape[0] // RIM
        yp = jnp.where(tall_mask(last_lane, count), 0.0, turn(f, -1, 1))
        ym = jnp.where(tall_mask(first_lane, count), 0.0, turn(f, 1, 1))
        return turn(f, -1, 0), turn(f, 1, 0), yp, ym

    def sheet(sliding, trans, melt, friction):
        squared = sliding * sliding
        return trans * (1.0 + squared / (1.0 + squared)), melt + HEATING * friction * squared

    def water_solve(pressure, trans_eff, leakage, source, valid):
        faces = [0.5 * (trans_eff + t) for t in shifts(trans_eff)]
        total = leakage + ((faces[0] + faces[1]) + (faces[2] + faces[3]))
        inverse = jnp.where(valid, 1.0 / total, 0.0)
        weights = [f * inverse for f in faces]
        count = pressure.shape[0] // RIM
        weights[2] = jnp.where(tall_mask(last_lane, count), 0.0, weights[2])
        weights[3] = jnp.where(tall_mask(first_lane, count), 0.0, weights[3])
        base = source * inverse
        for _ in range(SWEEPS):
            parts = [w * p for w, p in zip(weights, neighbours(pressure))]
            pressure = base + ((parts[0] + parts[1]) + (parts[2] + parts[3]))
        return pressure

    def between(f):
        pieces = [f[RIM * k : RIM * k + RIM] for k in range(f.shape[0] // RIM)]
        return join([jnp.where(upper_sub, p, q) for p, q in zip(pieces[:-1], pieces[1:])])

    def late_tile(halo, first, last):
        return jnp.where(halo_in_late, halo, jnp.where(is_low, first, last))

    def coefficients(s_shift, d_shift, drop, driving, rate):
        sdx, sdy = s_shift[0] - s_shift[1], s_shift[2] - s_shift[3]
        ddx, ddy = d_shift[0] - d_shift[1], d_shift[2] - d_shift[3]
        return [
            0.03125 * (sdx * sdx + sdy * sdy) + 0.125 * FLOOR,
            0.0625 * (sdx * ddx + sdy * ddy),
            0.03125 * (ddx * ddx + ddy * ddy),
            0.125 * drop * drop,
            0.25 * ((s_shift[0] + s_shift[1]) + (s_shift[2] + s_shift[3])),
            0.25 * ((d_shift[0] + d_shift[1]) + (d_shift[2] + d_shift[3])),
            driving * (0.5 / rate),
        ]

    def viscosity(flat, offset):
        for n in range(flat[0].shape[0] // RIM):
            at = slice(offset + RIM * n, offset + RIM * n + RIM)
            c0, c1, c2, c3, n0, n1, dr = [f[RIM * n : RIM * n + RIM] for f in flat]
            before = None
            for k in range(LAYERS):
                wk = float(w[k])
                strain = c0 + (c1 * wk + c2 * (wk * wk))
                if k < LAYERS - 1:
                    strain = strain + c3 * float((w[k + 1] - w[k]) ** 2)
                twice = jnp.exp2(jnp.log(strain) * THIRD)
                q_ref[k, at] = twice
                r_ref[k, at] = dr + twice * (n0 + n1 * wk)
                if k > 0:
                    g_ref[k - 1, at] = 0.5 * (before + twice)
                before = twice

    def step(d, e, t, g, q, r):
        d = e + (g if d is None else g * d)
        return d, q * d + g * e, r * d + g * t

    def from_surface(at):
        d, e, t = None, q_ref[LAYERS - 1, at], r_ref[LAYERS - 1, at]
        for k in range(LAYERS - 1):
            j = LAYERS - 2 - k
            d, e, t = step(d, e, t, g_ref[j, at], q_ref[j, at], r_ref[j, at])
            if k % RESCALE == RESCALE - 1 and k < LAYERS - 2:
                shrink = 1.0 / d
                d, e, t = None, e * shrink, t * shrink
        return d, e, t

    def from_base(at):
        d, e, t, product = None, q_ref[0, at], r_ref[0, at], None
        for k in range(LAYERS - 1):
            g = g_ref[k, at]
            product = g if product is None else product * g
            d, e, t = step(d, e, t, g, q_ref[k + 1, at], r_ref[k + 1, at])
            if k % RESCALE == RESCALE - 1 and k < LAYERS - 2:
                shrink = 1.0 / d
                d, e, t, product = None, e * shrink, t * shrink, product * shrink
        shrink = 1.0 / e
        return t * shrink, product * shrink

    for n, c in enumerate(main_copies()):
        c.wait_recv()
    driving, rate, friction, melt, trans, leakage, overburden, scale, ice, grounded = [field_local(i) for i in range(10)]
    friction = friction * grounded
    scale = scale * grounded
    speed, drop = first_velocity(driving, rate, friction, ice)
    early_rows = slice(0, local - RIM)
    late_rows = slice(local - RIM, local)
    viscosity(
        coefficients(
            [between(f) for f in shifts(speed)], [between(f) for f in shifts(drop)],
            between(drop), between(driving), between(rate),
        ),
        0,
    )
    early_down = from_surface(early_rows)
    early_up = from_base(early_rows)
    trans_eff, source = sheet(speed + drop * float(w[0]), trans, melt, friction)

    for region in range(2):
        for dx, condition in ((1, both(is_low, below)), (-1, both(is_high, above))):

            @pl.when(condition)
            def _(dx=dx, region=region):
                for c in edge_copies(dx, region):
                    c.wait_recv()

    fills = (0.0, 1.0, 0.0, 0.0, 0.0, 1.0, 0.0, 0.0, 0.0, 0.0)
    halo = [field_halo(i, fill) for i, fill in enumerate(fills)]
    h_driving, h_rate, h_friction, h_melt, h_trans, h_leakage, h_overburden, h_scale, h_ice, h_grounded = halo
    h_friction = h_friction * h_grounded
    h_scale = h_scale * h_grounded
    h_speed, h_drop = first_velocity(h_driving, h_rate, h_friction, h_ice)
    h_trans_eff, h_source = sheet(h_speed + h_drop * float(w[0]), h_trans, h_melt, h_friction)
    valid = join([jnp.broadcast_to(has_halo, (RIM, wide)), jnp.ones((local, wide), jnp.bool_)])
    leakage = join([h_leakage, leakage])
    pressure = water_solve(
        join([h_overburden, overburden]), join([h_trans_eff, trans_eff]), leakage, join([h_source, source]), valid
    )
    scale = join([h_scale, scale])
    friction = scale * pressure

    def around(h, f):
        return join([f[local - RIM :], h, f[:RIM]])

    def pick(f):
        return late_tile(f[RIM : 2 * RIM], f[2 * RIM :], f[:RIM])

    viscosity(
        coefficients(
            [pick(f) for f in shifts(around(h_speed, speed))], [pick(f) for f in shifts(around(h_drop, drop))],
            pick(around(h_drop, drop)), pick(around(h_driving, driving)), pick(around(h_rate, rate)),
        ),
        local - RIM,
    )
    late_down = from_surface(late_rows)
    down_d, down_e, down_t = [join(p) for p in zip(early_down, late_down)]

    def arrange(f):
        return join([between(f[RIM:]), pick(join([f[late_end:], f[: 2 * RIM]]))])

    def restore(f):
        pieces = [f[RIM * k : RIM * k + RIM] for k in range(tiles)]
        pieces = pieces[-1:] + pieces
        return join([pieces[0]] + [jnp.where(upper_sub, q, p) for p, q in zip(pieces[:-1], pieces[1:])])

    late_end = local
    base = arrange(friction * (0.5 / join([h_rate, rate])))
    ice = join([h_ice, ice])
    basal = down_t / (down_e + base * down_d)
    sliding = restore(basal) * ice
    trans_eff, source = sheet(sliding, join([h_trans, trans]), join([h_melt, melt]), friction)
    pressure = water_solve(pressure, trans_eff, leakage, source, valid)

    def mine(f):
        return jnp.where(is_low, f[RIM : RIM + half], f[2 * RIM : 2 * RIM + half])

    block = mine(pressure)
    send_p[0] = block[:, :lanes]
    send_p[1] = block[:, lanes:]
    place = pl.ds(pl.multiple_of(jnp.where(is_low, 0, half), RIM), half)
    side = number(is_high)

    def result_copy(src, plane, m, where, k, target):
        return pltpu.make_async_remote_copy(
            src_ref=src, dst_ref=out.at[0, plane, where], send_sem=out_send.at[m], recv_sem=out_recv.at[plane, k],
            device_id=target, device_id_type=MESH,
        )

    def water_copies():
        return [
            result_copy(send_p.at[1], strip, 3, place, side, {"sec": sectors, "gy": partner}),
            result_copy(send_p.at[0], strip, 4, place, side, {"sec": sectors}),
        ]

    def own_copies():
        return [result_copy(send_p.at[1], 0, 0, place, side, {"gy": partner})]

    def ice_copies():
        return [result_copy(results.at[n], n, n, place, side, {"gy": partner}) for n in range(3)]

    await_credit(sends_last, 2, 2)
    start(sends_last, water_copies())
    start(is_water, own_copies())

    @pl.when(is_water)
    def _():
        out[0, 0, place] = block[:, :lanes]

    late_up = from_base(late_rows)
    top, reach = [join(p) for p in zip(early_up, late_up)]
    surface = mine(restore(top - base * basal * reach) * ice)

    @pl.when(is_ice)
    def _():
        for n, f in enumerate((surface, mine(sliding), mine(scale) * block)):
            out[0, n, place] = f[:, :lanes]
            results[n] = f[:, lanes:]
        for c in ice_copies():
            c.start()

    for c in main_copies():
        c.wait_send()
    for dx, condition in ((-1, below), (1, above)):
        wait_send(condition, edge_copies(dx, gy))
    wait_send(sends_last, water_copies())
    wait_send(is_water, own_copies())
    wait_send(is_ice, ice_copies())

    other = pl.ds(pl.multiple_of(jnp.where(is_low, half, 0), RIM), half)

    def await_result(condition, plane, where, k):
        @pl.when(condition)
        def _():
            result_copy(send_p.at[0], plane, 0, where, k, {"gy": partner}).wait_recv()

    await_result(sec >= 0, 0, other, 1 - side)
    for plane in range(1, 3):
        await_result(is_ice, plane, other, 1 - side)
        for k in range(2):
            await_result(is_water, plane, pl.ds(half * k, half), k)


def narrow_map(nx, *args):
    sectors, rows, lanes = args[0].shape
    half = rows // 2
    local = half + RIM
    f32 = jnp.float32
    vmem = pltpu.VMEM
    dma = pltpu.SemaphoreType.DMA
    return pl.pallas_call(
        functools.partial(narrow_kernel, sectors, nx),
        out_shape=pltpu.VMEM((1, sectors, rows, lanes), f32),
        in_specs=[pl.BlockSpec(memory_space=pltpu.HBM)] * len(args),
        out_specs=pl.BlockSpec(memory_space=pltpu.VMEM),
        scratch_shapes=[
            vmem((8, rows, lanes), f32),
            vmem((2, rows, lanes), jnp.int32),
            vmem((8, local, lanes), f32),
            vmem((2, local, lanes), jnp.int32),
            vmem((2, 8, RIM, lanes), f32),
            vmem((2, 2, RIM, lanes), jnp.int32),
            vmem((LAYERS, local, 2 * lanes), f32),
            vmem((LAYERS, local, 2 * lanes), f32),
            vmem((LAYERS, local, 2 * lanes), f32),
            vmem((2, half, lanes), f32),
            vmem((3, half, lanes), f32),
            dma((2,)),
            dma((6,)),
            dma((6,)),
            pltpu.SemaphoreType.REGULAR((3,)),
            dma((5,)),
            dma((sectors, 2)),
        ],
        compiler_params=pltpu.CompilerParams(collective_id=0, has_side_effects=True),
    )(*args)


def solution(mesh):
    spec = P(None, "gx", "gy")
    nx, ny = mesh.shape["gx"], mesh.shape["gy"]
    on_device = functools.partial(narrow_map, nx) if ny == 2 else functools.partial(wide_map, nx, ny)
    return jax.shard_map(
        on_device,
        mesh=mesh,
        in_specs=(spec,) * 10,
        out_specs=P("sec", None, "gx", "gy"),
        check_vma=False,
    )
```

```python
import functools

import jax
import jax.numpy as jnp
import numpy as np
from jax import lax
from jax.experimental import pallas as pl
from jax.experimental.pallas import tpu as pltpu
from jax.sharding import PartitionSpec as P

LAYERS = 40
SWEEPS = 4
VERT = 4.0
FLOOR = 0.25
HEATING = 0.5

RIM = 8
HALF = RIM // 2
RESCALE = 10
THIRD = -1.0 / (3.0 * float(np.log(2.0)))
DIRECTIONS = [(dx, dy) for dx in (-1, 0, 1) for dy in (-1, 0, 1) if (dx, dy) != (0, 0)]
MESH = pl.DeviceIdType.MESH


def basal_response():
    matrix = np.zeros((LAYERS, LAYERS))
    for k in range(LAYERS):
        matrix[k, k] = 4.0 + (VERT if k > 0 else 0.0) + (VERT if k < LAYERS - 1 else 0.0)
        if k > 0:
            matrix[k, k - 1] = matrix[k - 1, k] = -VERT
    unit = np.zeros(LAYERS)
    unit[0] = 1.0
    return np.linalg.solve(matrix, unit)


def turn(values, shift, axis):
    return pltpu.roll(values, shift % values.shape[axis], axis)


def neighbours(f):
    return turn(f, -1, 0), turn(f, 1, 0), turn(f, -1, 1), turn(f, 1, 1)


def water_solve(pressure, trans_eff, leakage, source, valid):
    faces = [0.5 * (trans_eff + t) for t in neighbours(trans_eff)]
    total = leakage + ((faces[0] + faces[1]) + (faces[2] + faces[3]))
    inverse = jnp.where(valid, 1.0 / total, 0.0)
    weights = [f * inverse for f in faces]
    base = source * inverse
    for _ in range(SWEEPS):
        parts = [w * p for w, p in zip(weights, neighbours(pressure))]
        pressure = base + ((parts[0] + parts[1]) + (parts[2] + parts[3]))
    return pressure


def wide_kernel(sectors, nx, ny, *refs):
    ins = refs[:10]
    out = refs[10]
    floats, ints, pack_l, pack_r, rim_l, rim_r, q_ref, g_ref, r_ref, send_p = refs[11:21]
    in_sem, send_sem, recv_sem, last_send, last_recv = refs[21:]
    rows, lanes = ins[0].shape[1:]
    sec = lax.axis_index("sec")
    gx = lax.axis_index("gx")
    gy = lax.axis_index("gy")
    strip = lax.rem(sec, sectors)
    is_ice = sec < sectors
    sends_last = jnp.logical_and(sec > 0, is_ice)

    def exists(dx, dy):
        x, y = gx + dx, gy + dy
        return jnp.logical_and(
            jnp.logical_and(x >= 0, x < nx), jnp.logical_and(y >= 0, y < ny)
        )

    float_ids = (0, 1, 2, 5, 6, 7, 8, 9)
    int_ids = (3, 4)
    loads = []
    for slot, arg in enumerate(float_ids):
        loads.append(pltpu.make_async_copy(ins[arg].at[strip], floats.at[slot, pl.ds(RIM, rows)], in_sem.at[0]))
    for slot, arg in enumerate(int_ids):
        loads.append(pltpu.make_async_copy(ins[arg].at[strip], ints.at[slot, pl.ds(RIM, rows)], in_sem.at[1]))
    barrier = pltpu.get_barrier_semaphore()
    count = jnp.int32(0)
    for dx, dy in sorted(DIRECTIONS, key=lambda d: -abs(d[0])):
        here = exists(dx, dy)
        count = count + here.astype(jnp.int32)

        @pl.when(here)
        def _(dx=dx, dy=dy):
            pl.semaphore_signal(barrier, inc=1, device_id={"gx": gx + dx, "gy": gy + dy}, device_id_type=MESH)

    count = count + sends_last.astype(jnp.int32)
    count = count + jnp.where(is_ice, 0, sectors - 1)

    @pl.when(sends_last)
    def _():
        pl.semaphore_signal(barrier, inc=1, device_id={"sec": sectors}, device_id_type=MESH)

    for s in range(1, sectors):

        @pl.when(jnp.logical_not(is_ice))
        def _(s=s):
            pl.semaphore_signal(barrier, inc=1, device_id={"sec": s}, device_id_type=MESH)

    for load in loads:
        load.start()
    for slot, buffer in enumerate((floats, ints)):
        mine = buffer.at[:, pl.ds(RIM, rows)]
        pltpu.make_async_copy(mine, mine, in_sem.at[slot]).wait()

    lane = lax.broadcasted_iota(jnp.int32, (rows, lanes), 1)
    fields = [floats[i, RIM : RIM + rows] for i in range(8)]
    fields += [ints[i, RIM : RIM + rows].astype(jnp.float32) for i in range(2)]
    left = jnp.zeros((rows, lanes), jnp.float32)
    right = jnp.zeros((rows, lanes), jnp.float32)
    for i, f in enumerate(fields):
        moved = turn(f, RIM * i, 1)
        group = lane // RIM
        left = jnp.where(group == i, moved, left)
        right = jnp.where(group == (i - 1) % (lanes // RIM), moved, right)
    pack_l[...] = left
    pack_r[...] = right

    pl.semaphore_wait(barrier, count)

    def copies(dx, dy, n):
        target = {"gx": gx + dx, "gy": gy + dy}

        def remote(src, dst, m):
            return pltpu.make_async_remote_copy(
                src_ref=src, dst_ref=dst, send_sem=send_sem.at[m], recv_sem=recv_sem.at[m],
                device_id=target, device_id_type=MESH,
            )

        if dy == 0:
            first = rows if dx > 0 else RIM
            landing = 0 if dx > 0 else RIM + rows
            return [
                remote(floats.at[:, pl.ds(first, RIM)], floats.at[:, pl.ds(landing, RIM)], n),
                remote(ints.at[:, pl.ds(first, RIM)], ints.at[:, pl.ds(landing, RIM)], 8 + (dx > 0)),
            ]
        src, dst = (pack_r, rim_l) if dy > 0 else (pack_l, rim_r)
        if dx == 0:
            return [remote(src, dst.at[pl.ds(RIM, rows)], n)]
        first = rows - RIM if dx > 0 else 0
        landing = 0 if dx > 0 else RIM + rows
        return [remote(src.at[pl.ds(first, RIM)], dst.at[pl.ds(landing, RIM)], n)]

    order = sorted(range(8), key=lambda n: abs(DIRECTIONS[n][1]))
    for n in order:
        dx, dy = DIRECTIONS[n]

        @pl.when(exists(dx, dy))
        def _(dx=dx, dy=dy, n=n):
            for c in copies(dx, dy, n):
                c.start()

    def arrive(n):
        dx, dy = DIRECTIONS[n]

        @pl.when(exists(-dx, -dy))
        def _():
            for c in copies(dx, dy, n):
                c.wait_recv()

    w = basal_response()
    ext = rows + 2 * RIM
    tall = rows + RIM
    tiles = tall // 8
    wide = 2 * RIM
    slot = lax.broadcasted_iota(jnp.int32, (8, lanes), 1) // wide
    lane_low = jnp.where(gy < ny - 1, lanes + RIM, lanes)
    lane_high = jnp.where(gy > 0, 2 * lanes - RIM, 2 * lanes)

    def in_map_lanes(height):
        lane_i = lax.broadcasted_iota(jnp.int32, (height, 2 * lanes), 1)
        return jnp.logical_or(lane_i < lane_low, lane_i >= lane_high)

    def field_reader(top, height, valid):
        at = slice(top, top + height)
        packed_l, packed_r = rim_l[at], rim_r[at]
        group = lax.broadcasted_iota(jnp.int32, (height, lanes), 1) // RIM

        def field(i, fill):
            main = floats[i, at] if i < 8 else ints[i - 8, at].astype(jnp.float32)
            rim = turn(jnp.where(group == i, packed_r, packed_l), -RIM * i, 1)
            return jnp.where(valid, jnp.concatenate([main, rim], axis=1), fill)

        return field

    def first_velocity(driving, rate, friction, ice):
        viscous = rate * float(FLOOR ** (-1.0 / 3.0))
        speed = driving / (4.0 * viscous)
        drop = -speed * friction / (viscous + friction * float(w[0]))
        return speed * ice, drop * ice

    def squeeze(f, which):
        tile = jnp.zeros((8, lanes), jnp.float32)
        for n, t in enumerate(which):
            moved = turn(f[8 * t : 8 * t + 8, lanes:], wide * n + RIM, 1)
            tile = jnp.where(slot == n, moved, tile)
        return jnp.concatenate([f[8 * t : 8 * t + 8, :lanes] for t in which] + [tile], axis=0)

    def spread(f, count):
        last = f[8 * count :]
        return [
            jnp.concatenate([f[8 * n : 8 * n + 8], turn(last, -(wide * n + RIM), 1)], axis=1)
            for n in range(count)
        ]

    def eliminate(speed, drop, driving, rate, which, offset, lead):
        sxp, sxm, syp, sym = neighbours(speed)
        dxp, dxm, dyp, dym = neighbours(drop)
        sdx, sdy, ddx, ddy = sxp - sxm, syp - sym, dxp - dxm, dyp - dym
        flat = [
            0.03125 * (sdx * sdx + sdy * sdy) + 0.125 * FLOOR,
            0.0625 * (sdx * ddx + sdy * ddy),
            0.03125 * (ddx * ddx + ddy * ddy),
            0.125 * drop * drop,
            0.25 * ((sxp + sxm) + (syp + sym)),
            0.25 * ((dxp + dxm) + (dyp + dym)),
            driving * (0.5 / rate),
        ]
        flat = [squeeze(turn(f, lead, 0), which) for f in flat]
        for n in range(len(which) + 1):
            at = slice(offset + 8 * n, offset + 8 * n + 8)
            c0, c1, c2, c3, n0, n1, dr = [f[8 * n : 8 * n + 8] for f in flat]
            before = None
            for k in range(LAYERS):
                wk = float(w[k])
                strain = c0 + (c1 * wk + c2 * (wk * wk))
                if k < LAYERS - 1:
                    strain = strain + c3 * float((w[k + 1] - w[k]) ** 2)
                twice = jnp.exp2(jnp.log(strain) * THIRD)
                q_ref[k, at] = twice
                r_ref[k, at] = dr + twice * (n0 + n1 * wk)
                if k > 0:
                    g_ref[k - 1, at] = 0.5 * (before + twice)
                before = twice

        at = slice(offset, offset + 8 * (len(which) + 1))
        up_d, up_e, up_t = None, q_ref[0, at], r_ref[0, at]
        down_d, down_e, down_t = None, q_ref[LAYERS - 1, at], r_ref[LAYERS - 1, at]
        product = None

        def step(d, e, t, g, q, r):
            d = e + (g if d is None else g * d)
            return d, q * d + g * e, r * d + g * t

        for k in range(LAYERS - 1):
            j = LAYERS - 2 - k
            g = g_ref[k, at]
            product = g if product is None else product * g
            up_d, up_e, up_t = step(up_d, up_e, up_t, g, q_ref[k + 1, at], r_ref[k + 1, at])
            down_d, down_e, down_t = step(
                down_d, down_e, down_t, g_ref[j, at], q_ref[j, at], r_ref[j, at]
            )
            if k % RESCALE == RESCALE - 1 and k < LAYERS - 2:
                shrink = 1.0 / up_d
                up_d, up_e, up_t, product = None, up_e * shrink, up_t * shrink, product * shrink
                shrink = 1.0 / down_d
                down_d, down_e, down_t = None, down_e * shrink, down_t * shrink
        shrink = 1.0 / up_e
        return down_d, down_e, down_t, up_t * shrink, product * shrink

    def finish(parts, friction, rate, ice, which):
        down_d, down_e, down_t, top, reach = parts
        base = squeeze(turn(friction * (0.5 / rate), -HALF, 0), which)
        mask = squeeze(turn(ice, -HALF, 0), which)
        basal = down_t / (down_e + base * down_d)
        surface = top - base * basal * reach
        return [spread(f * mask, len(which)) for f in (basal, surface)]

    for n in order:
        if DIRECTIONS[n][0] == 0:
            arrive(n)
    early = list(range(1, tiles - 1))
    late = [0, tiles - 1]
    field = field_reader(RIM, rows, in_map_lanes(rows))
    driving, rate = field(0, 0.0), field(1, 1.0)
    speed, drop = first_velocity(driving, rate, field(2, 0.0) * field(9, 0.0), field(8, 0.0))
    early_parts = eliminate(speed, drop, driving, rate, early, 0, HALF)
    for n in order:
        if DIRECTIONS[n][0] != 0:
            arrive(n)

    row_i = lax.broadcasted_iota(jnp.int32, (ext, 2 * lanes), 0)
    row_low = jnp.where(gx > 0, 0, RIM)
    row_high = jnp.where(gx < nx - 1, ext, RIM + rows)
    valid = jnp.logical_and(
        jnp.logical_and(row_i >= row_low, row_i < row_high), in_map_lanes(ext)
    )
    field = field_reader(0, ext, valid)
    driving = field(0, 0.0)
    rate = field(1, 1.0)
    friction = field(2, 0.0)
    melt = field(3, 0.0)
    trans = field(4, 0.0)
    leakage = field(5, 1.0)
    pressure = field(6, 0.0)
    scale = field(7, 0.0)
    ice = field(8, 0.0)
    grounded = field(9, 0.0)
    friction = friction * grounded
    scale = scale * grounded

    speed, drop = first_velocity(driving, rate, friction, ice)
    sliding = speed + drop * float(w[0])
    squared = sliding * sliding
    trans_eff = trans * (1.0 + squared / (1.0 + squared))
    source = melt + HEATING * friction * squared
    pressure = water_solve(pressure, trans_eff, leakage, source, valid)
    friction = scale * pressure

    late_parts = eliminate(speed, drop, driving, rate, late, 8 * (len(early) + 1), -HALF)
    pieces = [None] * tiles
    for parts, which in ((early_parts, early), (late_parts, late)):
        for n, piece in enumerate(zip(*finish(parts, friction, rate, ice, which))):
            pieces[which[n]] = piece
    blank = jnp.zeros((RIM, 2 * lanes), jnp.float32)
    basal = turn(jnp.concatenate([p[0] for p in pieces] + [blank], axis=0), HALF, 0)
    surface = jnp.concatenate([p[1][:, :lanes] for p in pieces], axis=0)
    sliding = jnp.where(valid, basal, 0.0)
    squared = sliding * sliding
    trans_eff = trans * (1.0 + squared / (1.0 + squared))
    source = melt + HEATING * friction * squared
    pressure = water_solve(pressure, trans_eff, leakage, source, valid)
    block = pressure[RIM : RIM + rows, :lanes]
    send_p[...] = block

    def last():
        return pltpu.make_async_remote_copy(
            src_ref=send_p, dst_ref=out.at[0, strip], send_sem=last_send, recv_sem=last_recv.at[strip],
            device_id={"sec": sectors}, device_id_type=MESH,
        )

    @pl.when(sends_last)
    def _():
        last().start()

    @pl.when(is_ice)
    def _():
        out[0, 0] = turn(surface, -HALF, 0)[:rows]
        out[0, 1] = sliding[RIM : RIM + rows, :lanes]
        out[0, 2] = scale[RIM : RIM + rows, :lanes] * block

    @pl.when(jnp.logical_not(is_ice))
    def _():
        out[0, 0] = block

    for n in order:
        dx, dy = DIRECTIONS[n]

        @pl.when(exists(dx, dy))
        def _(dx=dx, dy=dy, n=n):
            for c in copies(dx, dy, n):
                c.wait_send()

    @pl.when(sends_last)
    def _():
        last().wait_send()

    for s in range(1, sectors):

        @pl.when(jnp.logical_not(is_ice))
        def _(s=s):
            pltpu.make_async_remote_copy(
                src_ref=send_p, dst_ref=out.at[0, s], send_sem=last_send, recv_sem=last_recv.at[s],
                device_id={"sec": 0}, device_id_type=MESH,
            ).wait_recv()


def wide_map(nx, ny, *args):
    sectors, rows, lanes = args[0].shape
    ext = rows + 2 * RIM
    f32 = jnp.float32
    vmem = pltpu.VMEM
    dma = pltpu.SemaphoreType.DMA
    return pl.pallas_call(
        functools.partial(wide_kernel, sectors, nx, ny),
        out_shape=pltpu.VMEM((1, sectors, rows, lanes), f32),
        in_specs=[pl.BlockSpec(memory_space=pltpu.HBM)] * len(args),
        out_specs=pl.BlockSpec(memory_space=pltpu.VMEM),
        scratch_shapes=[
            vmem((8, ext, lanes), f32),
            vmem((2, ext, lanes), jnp.int32),
            vmem((rows, lanes), f32),
            vmem((rows, lanes), f32),
            vmem((ext, lanes), f32),
            vmem((ext, lanes), f32),
            vmem((LAYERS, ext + RIM, lanes), f32),
            vmem((LAYERS, ext + RIM, lanes), f32),
            vmem((LAYERS, ext + RIM, lanes), f32),
            vmem((rows, lanes), f32),
            dma((2,)),
            dma((10,)),
            dma((10,)),
            dma,
            dma((sectors,)),
        ],
        compiler_params=pltpu.CompilerParams(collective_id=0, has_side_effects=True),
    )(*args)


ORDER = (0, 1, 2, 5, 6, 7, 8, 9, 3, 4)


def narrow_kernel(sectors, nx, *refs):
    ins = refs[:10]
    out = refs[10]
    own_f, own_i, part_f, part_i, halo_f, halo_i, q_ref, g_ref, r_ref, send_p, results = refs[11:22]
    in_sem, send_sem, recv_sem, credit, out_send, out_recv = refs[22:]
    rows, lanes = ins[0].shape[1:]
    sec = lax.axis_index("sec")
    gx = lax.axis_index("gx")
    gy = lax.axis_index("gy")
    partner = 1 - gy
    is_outer = gy == 1
    is_inner = gy == 0
    strip = lax.rem(sec, sectors)
    is_ice = sec < sectors
    is_water = jnp.logical_not(is_ice)
    sends_last = jnp.logical_and(sec > 0, is_ice)
    below, above = gx > 0, gx < nx - 1

    def both(p, q):
        return jnp.logical_and(p, q)

    def number(condition):
        return condition.astype(jnp.int32)

    def copy_in(n):
        arg = ORDER[n]
        dst = own_f.at[n] if n < 8 else own_i.at[n - 8]
        return pltpu.make_async_copy(ins[arg].at[strip], dst, in_sem.at[int(n >= 8)])

    for n in range(10):
        copy_in(n).start()

    barrier = pltpu.get_barrier_semaphore()

    def signal(condition, sem, target):
        @pl.when(condition)
        def _():
            pl.semaphore_signal(sem, inc=1, device_id=target, device_id_type=MESH)

    signal(above, barrier, {"gx": gx + 1, "gy": 1})
    signal(both(above, is_outer), barrier, {"gx": gx + 1, "gy": 0})
    signal(is_outer, barrier, {"gy": 0})
    signal(sends_last, barrier, {"sec": sectors, "gy": partner})
    signal(sends_last, barrier, {"sec": sectors})
    count = number(is_inner) + number(below) + number(both(below, is_outer)) + jnp.where(is_ice, 0, 2 * (sectors - 1))

    @pl.when(count > 0)
    def _():
        pl.semaphore_wait(barrier, count)

    signal(both(below, is_outer), credit.at[0], {"gx": gx - 1, "gy": 0})
    signal(both(below, is_outer), credit.at[0], {"gx": gx - 1, "gy": 1})
    signal(is_inner, credit.at[1], {"gy": 1})
    for s in range(1, sectors):
        signal(is_water, credit.at[2], {"sec": s, "gy": partner})
        signal(is_water, credit.at[2], {"sec": s})

    def remote(src, dst, m, k, target):
        return pltpu.make_async_remote_copy(
            src_ref=src, dst_ref=dst, send_sem=send_sem.at[m], recv_sem=recv_sem.at[k],
            device_id=target, device_id_type=MESH,
        )

    def main_copies():
        return [remote(own_f, part_f, 0, 0, {"gy": partner}), remote(own_i, part_i, 1, 1, {"gy": partner})]

    def edge_copies(dx, region):
        src = pl.ds(rows - RIM if dx > 0 else 0, RIM)
        side = int(dx < 0)
        target = {"gx": gx + dx, "gy": 1}
        return [
            remote(own_f.at[:, src], halo_f.at[side, region], 3 + dx, 2 + 4 * side + region, target),
            remote(own_i.at[:, src], halo_i.at[side, region], 4 + dx, 4 + 4 * side + region, target),
        ]

    def start(condition, copies):
        @pl.when(condition)
        def _():
            for c in copies:
                c.start()

    def wait_send(condition, copies):
        @pl.when(condition)
        def _():
            for c in copies:
                c.wait_send()

    def await_credit(condition, which, amount):
        @pl.when(condition)
        def _():
            pl.semaphore_wait(credit.at[which], amount)

    @pl.when(below)
    def _():
        for n in range(10):
            src = ins[ORDER[n]].at[strip, pl.ds(0, RIM)]
            dst = halo_f.at[1, gy, n] if n < 8 else halo_i.at[1, gy, n - 8]
            m = int(n >= 8)
            remote(src, dst, 2 + m, 6 + 2 * m + gy, {"gx": gx - 1, "gy": 1}).start()

    for sem, buffer in enumerate((own_f, own_i)):
        pltpu.make_async_copy(buffer, buffer, in_sem.at[sem]).wait()
    await_credit(is_outer, 1, 1)
    for c in main_copies():
        c.start()
    await_credit(above, 0, 1)
    start(above, edge_copies(1, gy))

    w = basal_response()
    wide = 2 * lanes
    lane = lax.broadcasted_iota(jnp.int32, (RIM, wide), 1)
    upper_sub = lax.broadcasted_iota(jnp.int32, (RIM, wide), 0) >= HALF
    last_lane = lane == wide - 1
    first_lane = lane == 0

    def join(parts):
        return jnp.concatenate(parts, axis=0)

    def tall_mask(mask, count):
        return join([mask] * count)

    def beside(f, i):
        return f[i] if i < 8 else f[i - 8].astype(jnp.float32)

    def fields(left, right):
        f = [jnp.concatenate([beside(left[i >= 8], i), beside(right[i >= 8], i)], axis=1) for i in range(10)]
        f[2] = f[2] * f[9]
        f[7] = f[7] * f[9]
        return f[:9]

    def halo_fields(side, exists):
        left, right = [(halo_f.at[side, r], halo_i.at[side, r]) for r in range(2)]
        return [
            jnp.where(exists, f, fill)
            for f, fill in zip(fields(left, right), (0.0, 1.0, 0.0, 0.0, 0.0, 1.0, 0.0, 0.0, 0.0))
        ]

    def first_velocity(driving, rate, friction, ice):
        viscous = rate * float(FLOOR ** (-1.0 / 3.0))
        speed = driving / (4.0 * viscous)
        drop = -speed * friction / (viscous + friction * float(w[0]))
        return speed * ice, drop * ice

    def shifts(f):
        count = f.shape[0] // RIM
        yp = jnp.where(tall_mask(last_lane, count), 0.0, turn(f, -1, 1))
        ym = jnp.where(tall_mask(first_lane, count), 0.0, turn(f, 1, 1))
        return turn(f, -1, 0), turn(f, 1, 0), yp, ym

    def sheet(sliding, trans, melt, friction):
        squared = sliding * sliding
        return trans * (1.0 + squared / (1.0 + squared)), melt + HEATING * friction * squared

    def water_solve(pressure, trans_eff, leakage, source, valid):
        faces = [0.5 * (trans_eff + t) for t in shifts(trans_eff)]
        total = leakage + ((faces[0] + faces[1]) + (faces[2] + faces[3]))
        inverse = 1.0 / total if valid is None else jnp.where(valid, 1.0 / total, 0.0)
        weights = [f * inverse for f in faces]
        count = pressure.shape[0] // RIM
        weights[2] = jnp.where(tall_mask(last_lane, count), 0.0, weights[2])
        weights[3] = jnp.where(tall_mask(first_lane, count), 0.0, weights[3])
        base = source * inverse
        for _ in range(SWEEPS):
            parts = [w * p for w, p in zip(weights, neighbours(pressure))]
            pressure = base + ((parts[0] + parts[1]) + (parts[2] + parts[3]))
        return pressure

    def split(f):
        return [f[RIM * k : RIM * k + RIM] for k in range(f.shape[0] // RIM)]

    def between(f, which):
        pieces = split(f)
        return join([jnp.where(upper_sub, pieces[k], pieces[k + 1]) for k in which])

    def restore(pieces):
        middle = [jnp.where(upper_sub, q, p) for p, q in zip(pieces[:-1], pieces[1:])]
        return join([pieces[0], *middle, pieces[-1]])

    def coefficients(speed, drop, driving, rate, which):
        s_shift = [between(f, which) for f in shifts(speed)]
        d_shift = [between(f, which) for f in shifts(drop)]
        drop, driving, rate = [between(f, which) for f in (drop, driving, rate)]
        sdx, sdy = s_shift[0] - s_shift[1], s_shift[2] - s_shift[3]
        ddx, ddy = d_shift[0] - d_shift[1], d_shift[2] - d_shift[3]
        return [
            0.03125 * (sdx * sdx + sdy * sdy) + 0.125 * FLOOR,
            0.0625 * (sdx * ddx + sdy * ddy),
            0.03125 * (ddx * ddx + ddy * ddy),
            0.125 * drop * drop,
            0.25 * ((s_shift[0] + s_shift[1]) + (s_shift[2] + s_shift[3])),
            0.25 * ((d_shift[0] + d_shift[1]) + (d_shift[2] + d_shift[3])),
            driving * (0.5 / rate),
        ]

    def viscosity(flat, offset):
        for n in range(flat[0].shape[0] // RIM):
            at = slice(offset + RIM * n, offset + RIM * n + RIM)
            c0, c1, c2, c3, n0, n1, dr = [f[RIM * n : RIM * n + RIM] for f in flat]
            before = None
            for k in range(LAYERS):
                wk = float(w[k])
                strain = c0 + (c1 * wk + c2 * (wk * wk))
                if k < LAYERS - 1:
                    strain = strain + c3 * float((w[k + 1] - w[k]) ** 2)
                twice = jnp.exp2(jnp.log(strain) * THIRD)
                q_ref[k, at] = twice
                r_ref[k, at] = dr + twice * (n0 + n1 * wk)
                if k > 0:
                    g_ref[k - 1, at] = 0.5 * (before + twice)
                before = twice

    def step(d, e, t, g, q, r):
        d = e + (g if d is None else g * d)
        return d, q * d + g * e, r * d + g * t

    def from_surface(at):
        d, e, t = None, q_ref[LAYERS - 1, at], r_ref[LAYERS - 1, at]
        for k in range(LAYERS - 1):
            j = LAYERS - 2 - k
            d, e, t = step(d, e, t, g_ref[j, at], q_ref[j, at], r_ref[j, at])
            if k % RESCALE == RESCALE - 1 and k < LAYERS - 2:
                shrink = 1.0 / d
                d, e, t = None, e * shrink, t * shrink
        return d, e, t

    def from_base(at):
        d, e, t, product = None, q_ref[0, at], r_ref[0, at], None
        for k in range(LAYERS - 1):
            g = g_ref[k, at]
            product = g if product is None else product * g
            d, e, t = step(d, e, t, g, q_ref[k + 1, at], r_ref[k + 1, at])
            if k % RESCALE == RESCALE - 1 and k < LAYERS - 2:
                shrink = 1.0 / d
                d, e, t, product = None, e * shrink, t * shrink, product * shrink
        shrink = 1.0 / e
        return t * shrink, product * shrink

    def result_copy(src, planes, where, m, k, target):
        return pltpu.make_async_remote_copy(
            src_ref=src, dst_ref=out.at[0, planes, where], send_sem=out_send.at[m], recv_sem=out_recv.at[k],
            device_id=target, device_id_type=MESH,
        )

    inner_chunks = [(0, RIM, rows - 2 * RIM)]
    outer_chunks = [(0, 0, RIM), (RIM, rows - RIM, RIM)]

    def send_results(chunks, k, pressure, surface, sliding, scale):
        count = pressure.shape[0]
        at = pl.ds(0, count)
        send_p[0, at] = pressure[:, :lanes]
        send_p[1, at] = pressure[:, lanes:]
        mine, other = (slice(0, lanes), 1) if k == 0 else (slice(lanes, wide), 0)

        def started(copies):
            for c in copies:
                c.start()

        def pieces(src, planes, m, where_k, target):
            return [
                result_copy(src(pl.ds(a, n)), planes, pl.ds(b, n), m, where_k, target) for a, b, n in chunks
            ]

        @pl.when(sends_last)
        def _():
            pl.semaphore_wait(credit.at[2], 2)
            for r, m in ((other, 1), (1 - other, 2)):
                started(pieces(lambda d, r=r: send_p.at[r, d], strip, m, 2 * strip + k, {"sec": sectors, "gy": r}))

        @pl.when(is_water)
        def _():
            started(pieces(lambda d: send_p.at[other, d], 0, 0, k, {"gy": partner}))
            for a, b, n in chunks:
                out[0, 0, b : b + n] = pressure[a : a + n, mine]

        @pl.when(is_ice)
        def _():
            theirs = slice(lanes, wide) if k == 0 else slice(0, lanes)
            for plane, f in enumerate((surface(), sliding, scale * pressure)):
                results[plane, at] = f[:, theirs]
                for a, b, n in chunks:
                    out[0, plane, b : b + n] = f[a : a + n, mine]
            started(pieces(lambda d: results.at[:, d], slice(None), 0, k, {"gy": partner}))

    for c in main_copies():
        c.wait_recv()
    tiles = rows // RIM

    def down_of(parts, base):
        d, e, t = parts
        return t / (e + base * d)

    @pl.when(is_inner)
    def _():
        driving, rate, friction, melt, trans, leakage, overburden, scale, ice = fields((own_f, own_i), (part_f, part_i))
        which = range(tiles - 1)
        at = slice(0, rows - RIM)
        speed, drop = first_velocity(driving, rate, friction, ice)
        viscosity(coefficients(speed, drop, driving, rate, which), 0)
        trans_eff, source = sheet(speed + drop * float(w[0]), trans, melt, friction)
        pressure = water_solve(overburden, trans_eff, leakage, source, None)
        friction = scale * pressure
        base = between(friction * (0.5 / rate), which)
        basal = down_of(from_surface(at), base)
        sliding = restore(split(basal)) * ice
        trans_eff, source = sheet(sliding, trans, melt, friction)
        pressure = water_solve(pressure, trans_eff, leakage, source, None)
        mine = slice(RIM, rows - RIM)

        def surface():
            top, reach = from_base(at)
            return (restore(split(top - base * basal * reach)) * ice)[mine]

        send_results(inner_chunks, 0, pressure[mine], surface, sliding[mine], scale[mine])

    @pl.when(is_outer)
    def _():
        middle = fields((part_f, part_i), (own_f, own_i))
        driving, rate, friction, melt, trans, leakage, overburden, scale, ice = middle
        m_speed, m_drop = first_velocity(driving, rate, friction, ice)
        which = (0, tiles - 2)
        early, late = slice(0, 2 * RIM), slice(2 * RIM, 4 * RIM)
        viscosity(coefficients(m_speed, m_drop, driving, rate, which), 0)
        early_down = from_surface(early)
        early_up = from_base(early)
        m_sheet = sheet(m_speed + m_drop * float(w[0]), trans, melt, friction)

        for side, exists in ((0, below), (1, above)):

            @pl.when(exists)
            def _(side=side):
                for region in range(2):
                    for c in edge_copies(1 - 2 * side, region):
                        c.wait_recv()

        ends = [halo_fields(0, below), halo_fields(1, above)]
        end_velocity = [first_velocity(f[0], f[1], f[2], f[8]) for f in ends]
        end_sheet = [sheet(s + d * float(w[0]), f[4], f[3], f[2]) for f, (s, d) in zip(ends, end_velocity)]

        def frame(a, f, b):
            return join([a, f, b])

        low, high = ends
        driving, rate, friction, melt, trans, leakage, overburden, scale, ice = [
            frame(*f) for f in zip(low, middle, high)
        ]
        speed = frame(end_velocity[0][0], m_speed, end_velocity[1][0])
        drop = frame(end_velocity[0][1], m_drop, end_velocity[1][1])
        trans_eff, source = [frame(*f) for f in zip(end_sheet[0], m_sheet, end_sheet[1])]
        valid = frame(
            jnp.broadcast_to(below, (RIM, wide)), jnp.ones((rows, wide), jnp.bool_), jnp.broadcast_to(above, (RIM, wide))
        )
        pressure = water_solve(overburden, trans_eff, leakage, source, valid)
        friction = scale * pressure
        viscosity(coefficients(speed, drop, driving, rate, (0, tiles)), 2 * RIM)
        late_down = from_surface(late)
        order = (1, tiles - 1, 0, tiles)
        base = between(friction * (0.5 / rate), order)
        basal = down_of([join(p) for p in zip(early_down, late_down)], base)

        def spread(f):
            pieces = [jnp.zeros((RIM, wide), jnp.float32)] * (tiles + 1)
            for k, piece in zip(order, split(f)):
                pieces[k] = piece
            return restore(pieces) * ice

        sliding = spread(basal)
        trans_eff, source = sheet(sliding, trans, melt, friction)
        pressure = water_solve(pressure, trans_eff, leakage, source, valid)

        def mine(f):
            return join([f[RIM : 2 * RIM], f[rows : rows + RIM]])

        def surface():
            top, reach = [join(p) for p in zip(early_up, from_base(late))]
            return mine(spread(top - base * basal * reach))

        send_results(outer_chunks, 1, mine(pressure), surface, mine(sliding), mine(scale))

    for c in main_copies():
        c.wait_send()
    for dx, condition in ((-1, below), (1, above)):
        wait_send(condition, edge_copies(dx, gy))

    inner_rows, outer_rows = pl.ds(0, rows - 2 * RIM), pl.ds(0, 2 * RIM)
    for k, role, count in ((0, is_inner, inner_rows), (1, is_outer, outer_rows)):
        for m in (1, 2):
            wait_send(both(sends_last, role), [result_copy(send_p.at[0, count], 0, count, m, 0, {"gy": partner})])
        wait_send(both(is_water, role), [result_copy(send_p.at[0, count], 0, count, 0, 0, {"gy": partner})])
        wait_send(both(is_ice, role), [result_copy(results.at[:, count], slice(None), count, 0, 0, {"gy": partner})])

    def await_result(condition, src, planes, where, k):
        @pl.when(condition)
        def _():
            result_copy(src, planes, where, 0, k, {"gy": partner}).wait_recv()

    for k, role, count in ((1, is_inner, outer_rows), (0, is_outer, inner_rows)):
        await_result(both(is_ice, role), results.at[:, count], slice(None), count, k)
        await_result(both(is_water, role), send_p.at[0, count], 0, count, k)
    for s in range(1, sectors):
        for k, count in ((0, inner_rows), (1, outer_rows)):
            await_result(is_water, send_p.at[0, count], s, count, 2 * s + k)


def narrow_map(nx, *args):
    sectors, rows, lanes = args[0].shape
    most = max(rows - 2 * RIM, 2 * RIM)
    f32 = jnp.float32
    vmem = pltpu.VMEM
    dma = pltpu.SemaphoreType.DMA
    return pl.pallas_call(
        functools.partial(narrow_kernel, sectors, nx),
        out_shape=pltpu.VMEM((1, sectors, rows, lanes), f32),
        in_specs=[pl.BlockSpec(memory_space=pltpu.HBM)] * len(args),
        out_specs=pl.BlockSpec(memory_space=pltpu.VMEM),
        scratch_shapes=[
            vmem((8, rows, lanes), f32),
            vmem((2, rows, lanes), jnp.int32),
            vmem((8, rows, lanes), f32),
            vmem((2, rows, lanes), jnp.int32),
            vmem((2, 2, 8, RIM, lanes), f32),
            vmem((2, 2, 2, RIM, lanes), jnp.int32),
            vmem((LAYERS, max(rows, 4 * RIM), 2 * lanes), f32),
            vmem((LAYERS, max(rows, 4 * RIM), 2 * lanes), f32),
            vmem((LAYERS, max(rows, 4 * RIM), 2 * lanes), f32),
            vmem((2, most, lanes), f32),
            vmem((3, most, lanes), f32),
            dma((2,)),
            dma((6,)),
            dma((10,)),
            pltpu.SemaphoreType.REGULAR((3,)),
            dma((3,)),
            dma((2 * sectors,)),
        ],
        compiler_params=pltpu.CompilerParams(collective_id=0, has_side_effects=True),
    )(*args)


def solution(mesh):
    spec = P(None, "gx", "gy")
    nx, ny = mesh.shape["gx"], mesh.shape["gy"]
    on_device = functools.partial(narrow_map, nx) if ny == 2 else functools.partial(wide_map, nx, ny)
    return jax.shard_map(
        on_device,
        mesh=mesh,
        in_specs=(spec,) * 10,
        out_specs=P("sec", None, "gx", "gy"),
        check_vma=False,
    )
```

```python
import functools

import jax
import jax.numpy as jnp
import numpy as np
from jax import lax
from jax.experimental import pallas as pl
from jax.experimental.pallas import tpu as pltpu
from jax.sharding import PartitionSpec as P

LAYERS = 40
SWEEPS = 4
VERT = 4.0
FLOOR = 0.25
HEATING = 0.5

RIM = 8
HALF = RIM // 2
RESCALE = 10
THIRD = -1.0 / (3.0 * float(np.log(2.0)))
DIRECTIONS = [(dx, dy) for dx in (-1, 0, 1) for dy in (-1, 0, 1) if (dx, dy) != (0, 0)]
MESH = pl.DeviceIdType.MESH


def basal_response():
    matrix = np.zeros((LAYERS, LAYERS))
    for k in range(LAYERS):
        matrix[k, k] = 4.0 + (VERT if k > 0 else 0.0) + (VERT if k < LAYERS - 1 else 0.0)
        if k > 0:
            matrix[k, k - 1] = matrix[k - 1, k] = -VERT
    unit = np.zeros(LAYERS)
    unit[0] = 1.0
    return np.linalg.solve(matrix, unit)


def turn(values, shift, axis):
    return pltpu.roll(values, shift % values.shape[axis], axis)


def neighbours(f):
    return turn(f, -1, 0), turn(f, 1, 0), turn(f, -1, 1), turn(f, 1, 1)


def water_solve(pressure, trans_eff, leakage, source, valid):
    faces = [0.5 * (trans_eff + t) for t in neighbours(trans_eff)]
    total = leakage + ((faces[0] + faces[1]) + (faces[2] + faces[3]))
    inverse = jnp.where(valid, 1.0 / total, 0.0)
    weights = [f * inverse for f in faces]
    base = source * inverse
    for _ in range(SWEEPS):
        parts = [w * p for w, p in zip(weights, neighbours(pressure))]
        pressure = base + ((parts[0] + parts[1]) + (parts[2] + parts[3]))
    return pressure


def wide_kernel(sectors, nx, ny, *refs):
    ins = refs[:10]
    out = refs[10]
    floats, ints, pack_l, pack_r, rim_l, rim_r, q_ref, g_ref, r_ref, send_p = refs[11:21]
    in_sem, send_sem, recv_sem, last_send, last_recv = refs[21:]
    rows, lanes = ins[0].shape[1:]
    sec = lax.axis_index("sec")
    gx = lax.axis_index("gx")
    gy = lax.axis_index("gy")
    strip = lax.rem(sec, sectors)
    is_ice = sec < sectors
    sends_last = jnp.logical_and(sec > 0, is_ice)

    def exists(dx, dy):
        x, y = gx + dx, gy + dy
        return jnp.logical_and(
            jnp.logical_and(x >= 0, x < nx), jnp.logical_and(y >= 0, y < ny)
        )

    float_ids = (0, 1, 2, 5, 6, 7, 8, 9)
    int_ids = (3, 4)
    loads = []
    for slot, arg in enumerate(float_ids):
        loads.append(pltpu.make_async_copy(ins[arg].at[strip], floats.at[slot, pl.ds(RIM, rows)], in_sem.at[0]))
    for slot, arg in enumerate(int_ids):
        loads.append(pltpu.make_async_copy(ins[arg].at[strip], ints.at[slot, pl.ds(RIM, rows)], in_sem.at[1]))
    barrier = pltpu.get_barrier_semaphore()
    count = jnp.int32(0)
    for dx, dy in sorted(DIRECTIONS, key=lambda d: -abs(d[0])):
        here = exists(dx, dy)
        count = count + here.astype(jnp.int32)

        @pl.when(here)
        def _(dx=dx, dy=dy):
            pl.semaphore_signal(barrier, inc=1, device_id={"gx": gx + dx, "gy": gy + dy}, device_id_type=MESH)

    count = count + sends_last.astype(jnp.int32)
    count = count + jnp.where(is_ice, 0, sectors - 1)

    @pl.when(sends_last)
    def _():
        pl.semaphore_signal(barrier, inc=1, device_id={"sec": sectors}, device_id_type=MESH)

    for s in range(1, sectors):

        @pl.when(jnp.logical_not(is_ice))
        def _(s=s):
            pl.semaphore_signal(barrier, inc=1, device_id={"sec": s}, device_id_type=MESH)

    for load in loads:
        load.start()
    for slot, buffer in enumerate((floats, ints)):
        mine = buffer.at[:, pl.ds(RIM, rows)]
        pltpu.make_async_copy(mine, mine, in_sem.at[slot]).wait()

    lane = lax.broadcasted_iota(jnp.int32, (rows, lanes), 1)
    fields = [floats[i, RIM : RIM + rows] for i in range(8)]
    fields += [ints[i, RIM : RIM + rows].astype(jnp.float32) for i in range(2)]
    left = jnp.zeros((rows, lanes), jnp.float32)
    right = jnp.zeros((rows, lanes), jnp.float32)
    for i, f in enumerate(fields):
        moved = turn(f, RIM * i, 1)
        group = lane // RIM
        left = jnp.where(group == i, moved, left)
        right = jnp.where(group == (i - 1) % (lanes // RIM), moved, right)
    pack_l[...] = left
    pack_r[...] = right

    pl.semaphore_wait(barrier, count)

    def copies(dx, dy, n):
        target = {"gx": gx + dx, "gy": gy + dy}

        def remote(src, dst, m):
            return pltpu.make_async_remote_copy(
                src_ref=src, dst_ref=dst, send_sem=send_sem.at[m], recv_sem=recv_sem.at[m],
                device_id=target, device_id_type=MESH,
            )

        if dy == 0:
            first = rows if dx > 0 else RIM
            landing = 0 if dx > 0 else RIM + rows
            return [
                remote(floats.at[:, pl.ds(first, RIM)], floats.at[:, pl.ds(landing, RIM)], n),
                remote(ints.at[:, pl.ds(first, RIM)], ints.at[:, pl.ds(landing, RIM)], 8 + (dx > 0)),
            ]
        src, dst = (pack_r, rim_l) if dy > 0 else (pack_l, rim_r)
        if dx == 0:
            return [remote(src, dst.at[pl.ds(RIM, rows)], n)]
        first = rows - RIM if dx > 0 else 0
        landing = 0 if dx > 0 else RIM + rows
        return [remote(src.at[pl.ds(first, RIM)], dst.at[pl.ds(landing, RIM)], n)]

    order = sorted(range(8), key=lambda n: abs(DIRECTIONS[n][1]))
    for n in order:
        dx, dy = DIRECTIONS[n]

        @pl.when(exists(dx, dy))
        def _(dx=dx, dy=dy, n=n):
            for c in copies(dx, dy, n):
                c.start()

    def arrive(n):
        dx, dy = DIRECTIONS[n]

        @pl.when(exists(-dx, -dy))
        def _():
            for c in copies(dx, dy, n):
                c.wait_recv()

    w = basal_response()
    ext = rows + 2 * RIM
    tall = rows + RIM
    tiles = tall // 8
    wide = 2 * RIM
    slot = lax.broadcasted_iota(jnp.int32, (8, lanes), 1) // wide
    lane_low = jnp.where(gy < ny - 1, lanes + RIM, lanes)
    lane_high = jnp.where(gy > 0, 2 * lanes - RIM, 2 * lanes)

    def in_map_lanes(height):
        lane_i = lax.broadcasted_iota(jnp.int32, (height, 2 * lanes), 1)
        return jnp.logical_or(lane_i < lane_low, lane_i >= lane_high)

    def field_reader(top, height, valid):
        at = slice(top, top + height)
        packed_l, packed_r = rim_l[at], rim_r[at]
        group = lax.broadcasted_iota(jnp.int32, (height, lanes), 1) // RIM

        def field(i, fill):
            main = floats[i, at] if i < 8 else ints[i - 8, at].astype(jnp.float32)
            rim = turn(jnp.where(group == i, packed_r, packed_l), -RIM * i, 1)
            return jnp.where(valid, jnp.concatenate([main, rim], axis=1), fill)

        return field

    def first_velocity(driving, rate, friction, ice):
        viscous = rate * float(FLOOR ** (-1.0 / 3.0))
        speed = driving / (4.0 * viscous)
        drop = -speed * friction / (viscous + friction * float(w[0]))
        return speed * ice, drop * ice

    def squeeze(f, which):
        tile = jnp.zeros((8, lanes), jnp.float32)
        for n, t in enumerate(which):
            moved = turn(f[8 * t : 8 * t + 8, lanes:], wide * n + RIM, 1)
            tile = jnp.where(slot == n, moved, tile)
        return jnp.concatenate([f[8 * t : 8 * t + 8, :lanes] for t in which] + [tile], axis=0)

    def spread(f, count):
        last = f[8 * count :]
        return [
            jnp.concatenate([f[8 * n : 8 * n + 8], turn(last, -(wide * n + RIM), 1)], axis=1)
            for n in range(count)
        ]

    def eliminate(speed, drop, driving, rate, which, offset, lead):
        sxp, sxm, syp, sym = neighbours(speed)
        dxp, dxm, dyp, dym = neighbours(drop)
        sdx, sdy, ddx, ddy = sxp - sxm, syp - sym, dxp - dxm, dyp - dym
        flat = [
            0.03125 * (sdx * sdx + sdy * sdy) + 0.125 * FLOOR,
            0.0625 * (sdx * ddx + sdy * ddy),
            0.03125 * (ddx * ddx + ddy * ddy),
            0.125 * drop * drop,
            0.25 * ((sxp + sxm) + (syp + sym)),
            0.25 * ((dxp + dxm) + (dyp + dym)),
            driving * (0.5 / rate),
        ]
        flat = [squeeze(turn(f, lead, 0), which) for f in flat]
        for n in range(len(which) + 1):
            at = slice(offset + 8 * n, offset + 8 * n + 8)
            c0, c1, c2, c3, n0, n1, dr = [f[8 * n : 8 * n + 8] for f in flat]
            before = None
            for k in range(LAYERS):
                wk = float(w[k])
                strain = c0 + (c1 * wk + c2 * (wk * wk))
                if k < LAYERS - 1:
                    strain = strain + c3 * float((w[k + 1] - w[k]) ** 2)
                twice = jnp.exp2(jnp.log(strain) * THIRD)
                q_ref[k, at] = twice
                r_ref[k, at] = dr + twice * (n0 + n1 * wk)
                if k > 0:
                    g_ref[k - 1, at] = 0.5 * (before + twice)
                before = twice

        at = slice(offset, offset + 8 * (len(which) + 1))
        up_d, up_e, up_t = None, q_ref[0, at], r_ref[0, at]
        down_d, down_e, down_t = None, q_ref[LAYERS - 1, at], r_ref[LAYERS - 1, at]
        product = None

        def step(d, e, t, g, q, r):
            d = e + (g if d is None else g * d)
            return d, q * d + g * e, r * d + g * t

        for k in range(LAYERS - 1):
            j = LAYERS - 2 - k
            g = g_ref[k, at]
            product = g if product is None else product * g
            up_d, up_e, up_t = step(up_d, up_e, up_t, g, q_ref[k + 1, at], r_ref[k + 1, at])
            down_d, down_e, down_t = step(
                down_d, down_e, down_t, g_ref[j, at], q_ref[j, at], r_ref[j, at]
            )
            if k % RESCALE == RESCALE - 1 and k < LAYERS - 2:
                shrink = 1.0 / up_d
                up_d, up_e, up_t, product = None, up_e * shrink, up_t * shrink, product * shrink
                shrink = 1.0 / down_d
                down_d, down_e, down_t = None, down_e * shrink, down_t * shrink
        shrink = 1.0 / up_e
        return down_d, down_e, down_t, up_t * shrink, product * shrink

    def finish(parts, friction, rate, ice, which):
        down_d, down_e, down_t, top, reach = parts
        base = squeeze(turn(friction * (0.5 / rate), -HALF, 0), which)
        mask = squeeze(turn(ice, -HALF, 0), which)
        basal = down_t / (down_e + base * down_d)
        surface = top - base * basal * reach
        return [spread(f * mask, len(which)) for f in (basal, surface)]

    for n in order:
        if DIRECTIONS[n][0] == 0:
            arrive(n)
    early = list(range(1, tiles - 1))
    late = [0, tiles - 1]
    field = field_reader(RIM, rows, in_map_lanes(rows))
    driving, rate = field(0, 0.0), field(1, 1.0)
    speed, drop = first_velocity(driving, rate, field(2, 0.0) * field(9, 0.0), field(8, 0.0))
    early_parts = eliminate(speed, drop, driving, rate, early, 0, HALF)
    for n in order:
        if DIRECTIONS[n][0] != 0:
            arrive(n)

    row_i = lax.broadcasted_iota(jnp.int32, (ext, 2 * lanes), 0)
    row_low = jnp.where(gx > 0, 0, RIM)
    row_high = jnp.where(gx < nx - 1, ext, RIM + rows)
    valid = jnp.logical_and(
        jnp.logical_and(row_i >= row_low, row_i < row_high), in_map_lanes(ext)
    )
    field = field_reader(0, ext, valid)
    driving = field(0, 0.0)
    rate = field(1, 1.0)
    friction = field(2, 0.0)
    melt = field(3, 0.0)
    trans = field(4, 0.0)
    leakage = field(5, 1.0)
    pressure = field(6, 0.0)
    scale = field(7, 0.0)
    ice = field(8, 0.0)
    grounded = field(9, 0.0)
    friction = friction * grounded
    scale = scale * grounded

    speed, drop = first_velocity(driving, rate, friction, ice)
    sliding = speed + drop * float(w[0])
    squared = sliding * sliding
    trans_eff = trans * (1.0 + squared / (1.0 + squared))
    source = melt + HEATING * friction * squared
    pressure = water_solve(pressure, trans_eff, leakage, source, valid)
    friction = scale * pressure

    late_parts = eliminate(speed, drop, driving, rate, late, 8 * (len(early) + 1), -HALF)
    pieces = [None] * tiles
    for parts, which in ((early_parts, early), (late_parts, late)):
        for n, piece in enumerate(zip(*finish(parts, friction, rate, ice, which))):
            pieces[which[n]] = piece
    blank = jnp.zeros((RIM, 2 * lanes), jnp.float32)
    basal = turn(jnp.concatenate([p[0] for p in pieces] + [blank], axis=0), HALF, 0)
    surface = jnp.concatenate([p[1][:, :lanes] for p in pieces], axis=0)
    sliding = jnp.where(valid, basal, 0.0)
    squared = sliding * sliding
    trans_eff = trans * (1.0 + squared / (1.0 + squared))
    source = melt + HEATING * friction * squared
    pressure = water_solve(pressure, trans_eff, leakage, source, valid)
    block = pressure[RIM : RIM + rows, :lanes]
    send_p[...] = block

    def last():
        return pltpu.make_async_remote_copy(
            src_ref=send_p, dst_ref=out.at[0, strip], send_sem=last_send, recv_sem=last_recv.at[strip],
            device_id={"sec": sectors}, device_id_type=MESH,
        )

    @pl.when(sends_last)
    def _():
        last().start()

    @pl.when(is_ice)
    def _():
        out[0, 0] = turn(surface, -HALF, 0)[:rows]
        out[0, 1] = sliding[RIM : RIM + rows, :lanes]
        out[0, 2] = scale[RIM : RIM + rows, :lanes] * block

    @pl.when(jnp.logical_not(is_ice))
    def _():
        out[0, 0] = block

    for n in order:
        dx, dy = DIRECTIONS[n]

        @pl.when(exists(dx, dy))
        def _(dx=dx, dy=dy, n=n):
            for c in copies(dx, dy, n):
                c.wait_send()

    @pl.when(sends_last)
    def _():
        last().wait_send()

    for s in range(1, sectors):

        @pl.when(jnp.logical_not(is_ice))
        def _(s=s):
            pltpu.make_async_remote_copy(
                src_ref=send_p, dst_ref=out.at[0, s], send_sem=last_send, recv_sem=last_recv.at[s],
                device_id={"sec": 0}, device_id_type=MESH,
            ).wait_recv()


def wide_map(nx, ny, *args):
    sectors, rows, lanes = args[0].shape
    ext = rows + 2 * RIM
    f32 = jnp.float32
    vmem = pltpu.VMEM
    dma = pltpu.SemaphoreType.DMA
    return pl.pallas_call(
        functools.partial(wide_kernel, sectors, nx, ny),
        out_shape=pltpu.VMEM((1, sectors, rows, lanes), f32),
        in_specs=[pl.BlockSpec(memory_space=pltpu.HBM)] * len(args),
        out_specs=pl.BlockSpec(memory_space=pltpu.VMEM),
        scratch_shapes=[
            vmem((8, ext, lanes), f32),
            vmem((2, ext, lanes), jnp.int32),
            vmem((rows, lanes), f32),
            vmem((rows, lanes), f32),
            vmem((ext, lanes), f32),
            vmem((ext, lanes), f32),
            vmem((LAYERS, ext + RIM, lanes), f32),
            vmem((LAYERS, ext + RIM, lanes), f32),
            vmem((LAYERS, ext + RIM, lanes), f32),
            vmem((rows, lanes), f32),
            dma((2,)),
            dma((10,)),
            dma((10,)),
            dma,
            dma((sectors,)),
        ],
        compiler_params=pltpu.CompilerParams(collective_id=0, has_side_effects=True),
    )(*args)


SHARE = 32.0 ** (-1.0 / 3.0)


def steady_drop(w):
    ratios = np.float32(4.0 * ((w[1:] - w[:-1]) / w[:-1]) ** 2)
    same = np.cumprod(ratios == ratios[0])
    return float(ratios[0]), int(same.sum())


ORDER = (0, 1, 2, 5, 6, 7, 8, 9, 3, 4)


def narrow_kernel(sectors, nx, *refs):
    ins = refs[:10]
    out = refs[10]
    own_f, own_i, part_f, part_i, halo_f, halo_i, q_ref, g_ref, r_ref, up_ref, send_p, results = refs[11:23]
    in_sem, send_sem, recv_sem, credit, out_send, out_recv = refs[23:]
    rows, lanes = ins[0].shape[1:]
    sec = lax.axis_index("sec")
    gx = lax.axis_index("gx")
    gy = lax.axis_index("gy")
    partner = 1 - gy
    is_outer = gy == 1
    is_inner = gy == 0
    strip = lax.rem(sec, sectors)
    is_ice = sec < sectors
    is_water = jnp.logical_not(is_ice)
    sends_last = jnp.logical_and(sec > 0, is_ice)
    below, above = gx > 0, gx < nx - 1
    direct = sec > 0
    first_sector = sec == 0

    def both(p, q):
        return jnp.logical_and(p, q)

    def number(condition):
        return condition.astype(jnp.int32)

    def copy_in(n):
        arg = ORDER[n]
        dst = own_f.at[n] if n < 8 else own_i.at[n - 8]
        return pltpu.make_async_copy(ins[arg].at[strip], dst, in_sem.at[int(n >= 8)])

    def load():
        for n in range(10):
            copy_in(n).start()

    pl.when(is_outer)(load)
    barrier = pltpu.get_barrier_semaphore()

    def signal(condition, sem, target, role=True):
        @pl.when(jnp.logical_and(condition, role))
        def _():
            pl.semaphore_signal(sem, inc=1, device_id=target, device_id_type=MESH)

    signal(above, barrier, {"gx": gx + 1, "gy": 0}, is_outer)
    signal(above, barrier, {"gx": gx + 1, "gy": 1}, is_outer)
    signal(both(below, direct), barrier, {"gx": gx - 1, "gy": 1}, is_outer)
    signal(sec >= 0, barrier, {"gy": partner})
    signal(sends_last, barrier, {"sec": sectors, "gy": partner})
    signal(sends_last, barrier, {"sec": sectors})
    count = 1 + number(below) + number(both(both(above, direct), is_outer)) + jnp.where(is_ice, 0, 2 * (sectors - 1))
    pl.semaphore_wait(barrier, count)
    signal(both(below, first_sector), credit.at[1], {"gx": gx - 1, "gy": 1}, is_outer)
    signal(both(is_outer, direct), credit.at[0], {"gy": 0})
    for s in range(1, sectors):
        signal(is_water, credit.at[2], {"sec": s, "gy": partner})
        signal(is_water, credit.at[2], {"sec": s})

    def remote(src, dst, m, k, target):
        return pltpu.make_async_remote_copy(
            src_ref=src, dst_ref=dst, send_sem=send_sem.at[m], recv_sem=recv_sem.at[k],
            device_id=target, device_id_type=MESH,
        )

    def main_copies():
        return [remote(own_f, part_f, 0, 0, {"gy": partner}), remote(own_i, part_i, 1, 1, {"gy": partner})]

    def edge_copies(dx, region, parts=(0, 1, 2)):
        src = pl.ds(rows - RIM if dx > 0 else 0, RIM)
        side = int(dx < 0)
        target = {"gx": gx + dx, "gy": 1}
        m, k = 5 - 3 * side, 2 + 6 * side + 3 * region
        first, rest = pl.ds(0, 3), pl.ds(3, 5)
        pairs = [
            (own_f.at[first, src], halo_f.at[side, region, first]),
            (own_i.at[:, src], halo_i.at[side, region]),
            (own_f.at[rest, src], halo_f.at[side, region, rest]),
        ]
        return [remote(*pairs[p], m + p, k + p, target) for p in parts]

    def start(condition, copies):
        @pl.when(condition)
        def _():
            for c in copies:
                c.start()

    def wait_send(condition, copies):
        @pl.when(condition)
        def _():
            for c in copies:
                c.wait_send()

    def await_credit(condition, which, amount):
        @pl.when(condition)
        def _():
            pl.semaphore_wait(credit.at[which], amount)

    @pl.when(below)
    def _():
        for n in (0, 1, 2, 8, 9, 3, 4, 5, 6, 7):
            src = ins[ORDER[n]].at[strip, pl.ds(0, RIM)]
            dst = halo_f.at[1, gy, n] if n < 8 else halo_i.at[1, gy, n - 8]
            m = 1 if n >= 8 else 2 * int(n >= 3)
            remote(src, dst, 2 + m, 8 + m + 3 * gy, {"gx": gx - 1, "gy": 1}).start()

    pl.when(is_inner)(load)

    @pl.when(is_inner)
    def _():
        for n in (0, 1, 2, 8, 9, 3, 4, 5, 6, 7):
            dst = part_f.at[n] if n < 8 else part_i.at[n - 8]
            m = int(n >= 8)
            remote(ins[ORDER[n]].at[strip], dst, m, m, {"gy": 1}).start()

    for sem, buffer in enumerate((own_f, own_i)):
        pltpu.make_async_copy(buffer, buffer, in_sem.at[sem]).wait()
    start(is_outer, main_copies())
    await_credit(both(both(above, first_sector), is_outer), 1, 1)
    signal(both(is_outer, first_sector), credit.at[0], {"gy": 0})
    await_credit(is_inner, 0, 1)
    start(above, edge_copies(1, gy))

    w = basal_response()
    steady, settled = steady_drop(w)
    wide = 2 * lanes
    lane = lax.broadcasted_iota(jnp.int32, (RIM, wide), 1)
    upper_sub = lax.broadcasted_iota(jnp.int32, (RIM, wide), 0) >= HALF
    last_lane = lane == wide - 1
    first_lane = lane == 0

    def join(parts):
        return jnp.concatenate(parts, axis=0)

    def tall_mask(mask, count):
        return join([mask] * count)

    def beside(f, i):
        return f[i] if i < 8 else f[i - 8].astype(jnp.float32)

    def fields(left, right, which=range(9)):
        def field(i):
            return jnp.concatenate([beside(left[i >= 8], i), beside(right[i >= 8], i)], axis=1)

        return {i: field(i) * field(9) if i in (2, 7) else field(i) for i in which}

    def halo_fields(side, exists, which):
        left, right = [(halo_f.at[side, r], halo_i.at[side, r]) for r in range(2)]
        return {
            i: jnp.where(exists, f, 1.0 if i in (1, 5) else 0.0) for i, f in fields(left, right, which).items()
        }

    def first_velocity(driving, rate, friction, ice):
        viscous = rate * float(FLOOR ** (-1.0 / 3.0))
        speed = driving / (4.0 * viscous)
        drop = -speed * friction / (viscous + friction * float(w[0]))
        return speed * ice, drop * ice

    def shifts(f):
        count = f.shape[0] // RIM
        yp = jnp.where(tall_mask(last_lane, count), 0.0, turn(f, -1, 1))
        ym = jnp.where(tall_mask(first_lane, count), 0.0, turn(f, 1, 1))
        return turn(f, -1, 0), turn(f, 1, 0), yp, ym

    def sheet(sliding, trans, melt, friction):
        squared = sliding * sliding
        return trans * (1.0 + squared / (1.0 + squared)), melt + HEATING * friction * squared

    def sweeper(trans_eff, leakage, source, valid, keep):
        here = keep(trans_eff)
        faces = [0.5 * (here + keep(t)) for t in shifts(trans_eff)]
        total = leakage + ((faces[0] + faces[1]) + (faces[2] + faces[3]))
        inverse = 1.0 / total if valid is None else jnp.where(valid, 1.0 / total, 0.0)
        weights = [f * inverse for f in faces]
        count = here.shape[0] // RIM
        weights[2] = jnp.where(tall_mask(last_lane, count), 0.0, weights[2])
        weights[3] = jnp.where(tall_mask(first_lane, count), 0.0, weights[3])
        base = source * inverse

        def sweep(pressure):
            parts = [w * keep(p) for w, p in zip(weights, neighbours(pressure))]
            return base + ((parts[0] + parts[1]) + (parts[2] + parts[3]))

        return sweep

    def water_steps(pressure, trans_eff, leakage, source):
        sweep = sweeper(trans_eff, leakage, source, None, lambda f: f)
        steps = [pressure]
        for _ in range(SWEEPS):
            steps.append(sweep(steps[-1]))
        return steps

    def split(f):
        return [f[RIM * k : RIM * k + RIM] for k in range(f.shape[0] // RIM)]

    def between(f, which):
        pieces = split(f)
        return join([jnp.where(upper_sub, pieces[k], pieces[k + 1]) for k in which])

    def restore(pieces):
        middle = [jnp.where(upper_sub, q, p) for p, q in zip(pieces[:-1], pieces[1:])]
        return join([pieces[0], *middle, pieces[-1]])

    def coefficients(speed, drop, driving, rate, which):
        s_shift = [between(f, which) for f in shifts(speed)]
        d_shift = [between(f, which) for f in shifts(drop)]
        drop, driving, rate = [between(f, which) for f in (drop, driving, rate)]
        sdx, sdy = s_shift[0] - s_shift[1], s_shift[2] - s_shift[3]
        ddx, ddy = d_shift[0] - d_shift[1], d_shift[2] - d_shift[3]
        c2, c3 = ddx * ddx + ddy * ddy, drop * drop
        return [
            (sdx * sdx + sdy * sdy) + 4.0 * FLOOR,
            sdx * ddx + sdy * ddy,
            c2,
            c3,
            c2 + steady * c3,
            (s_shift[0] + s_shift[1]) + (s_shift[2] + s_shift[3]),
            (d_shift[0] + d_shift[1]) + (d_shift[2] + d_shift[3]),
            driving * (2.0 * SHARE / rate),
        ]

    def viscosity(flat, offset):
        for n in range(flat[0].shape[0] // RIM):
            at = slice(offset + RIM * n, offset + RIM * n + RIM)
            c0, c1, c2, c3, c23, n0, n1, dr = [f[RIM * n : RIM * n + RIM] for f in flat]
            higher = None
            for k in reversed(range(LAYERS)):
                wk = float(w[k])
                if k < settled:
                    strain = c0 + (c1 * (2.0 * wk) + c23 * (wk * wk))
                else:
                    strain = c0 + (c1 * (2.0 * wk) + c2 * (wk * wk))
                    if k < LAYERS - 1:
                        strain = strain + c3 * float(4.0 * (w[k + 1] - w[k]) ** 2)
                now = jnp.exp2(jnp.log(strain) * THIRD)
                q_ref[k, at] = now
                r_ref[k, at] = dr + now * (n0 + n1 * wk)
                if k < LAYERS - 1:
                    g_ref[k, at] = 0.5 * (now + higher)
                higher = now

    def step(d, e, t, g, q, r):
        d = e + (g if d is None else g * d)
        return d, q * d + g * e, r * d + g * t

    def from_surface(at):
        d, e, t = None, q_ref[LAYERS - 1, at], r_ref[LAYERS - 1, at]
        for k in range(LAYERS - 1):
            j = LAYERS - 2 - k
            d, e, t = step(d, e, t, g_ref[j, at], q_ref[j, at], r_ref[j, at])
            if k % RESCALE == RESCALE - 1 and k < LAYERS - 2:
                shrink = 1.0 / d
                d, e, t = None, e * shrink, t * shrink
        return d, e, t

    def from_base(at):
        d, e, t, product = None, q_ref[0, at], r_ref[0, at], None
        for k in range(LAYERS - 1):
            g = g_ref[k, at]
            product = g if product is None else product * g
            d, e, t = step(d, e, t, g, q_ref[k + 1, at], r_ref[k + 1, at])
            if k % RESCALE == RESCALE - 1 and k < LAYERS - 2:
                shrink = 1.0 / d
                d, e, t, product = None, e * shrink, t * shrink, product * shrink
        shrink = 1.0 / e
        return t * shrink, product * shrink

    def result_copy(src, planes, where, m, k, target):
        return pltpu.make_async_remote_copy(
            src_ref=src, dst_ref=out.at[0, planes, where], send_sem=out_send.at[m], recv_sem=out_recv.at[k],
            device_id=target, device_id_type=MESH,
        )

    inner_chunks = [(0, RIM, rows - 2 * RIM)]
    outer_chunks = [(0, 0, RIM), (RIM, rows - RIM, RIM)]

    def send_results(chunks, k, pressure, surface, sliding, scale):
        count = pressure.shape[0]
        at = pl.ds(0, count)
        send_p[0, at] = pressure[:, :lanes]
        send_p[1, at] = pressure[:, lanes:]
        mine, other = (slice(0, lanes), 1) if k == 0 else (slice(lanes, wide), 0)

        def started(copies):
            for c in copies:
                c.start()

        def pieces(src, planes, m, where_k, target):
            return [
                result_copy(src(pl.ds(a, n)), planes, pl.ds(b, n), m, where_k, target) for a, b, n in chunks
            ]

        @pl.when(sends_last)
        def _():
            pl.semaphore_wait(credit.at[2], 2)
            for r, m in ((other, 1), (1 - other, 2)):
                started(pieces(lambda d, r=r: send_p.at[r, d], strip, m, 2 * strip + k, {"sec": sectors, "gy": r}))

        @pl.when(is_water)
        def _():
            started(pieces(lambda d: send_p.at[other, d], 0, 0, k, {"gy": partner}))
            for a, b, n in chunks:
                out[0, 0, b : b + n] = pressure[a : a + n, mine]

        @pl.when(is_ice)
        def _():
            theirs = slice(lanes, wide) if k == 0 else slice(0, lanes)
            for plane, f in enumerate((surface(), sliding, scale * pressure)):
                results[plane, at] = f[:, theirs]
                for a, b, n in chunks:
                    out[0, plane, b : b + n] = f[a : a + n, mine]
            started(pieces(lambda d: results.at[:, d], slice(None), 0, k, {"gy": partner}))

    for c in main_copies():
        c.wait_recv()
    tiles = rows // RIM

    def down_of(parts, base):
        d, e, t = parts
        return t / (e + base * d)

    @pl.when(is_inner)
    def _():
        driving, rate, friction, melt, trans, leakage, overburden, scale, ice = fields((own_f, own_i), (part_f, part_i)).values()
        which = range(tiles - 1)
        at = slice(0, rows - RIM)
        speed, drop = first_velocity(driving, rate, friction, ice)
        viscosity(coefficients(speed, drop, driving, rate, which), 0)
        trans_eff, source = sheet(speed + drop * float(w[0]), trans, melt, friction)
        pressure = water_steps(overburden, trans_eff, leakage, source)[-1]
        friction = scale * pressure
        base = between(friction * (0.5 * SHARE / rate), which)
        basal = down_of(from_surface(at), base)
        quarter = 0.25 * ice
        sliding = restore(split(basal)) * quarter
        trans_eff, source = sheet(sliding, trans, melt, friction)
        pressure = water_steps(pressure, trans_eff, leakage, source)[-1]
        mine = slice(RIM, rows - RIM)

        def surface():
            top, reach = from_base(at)
            return (restore(split(top - base * basal * reach)) * quarter)[mine]

        send_results(inner_chunks, 0, pressure[mine], surface, sliding[mine], scale[mine])

    @pl.when(is_outer)
    def _():
        middle = fields((part_f, part_i), (own_f, own_i))
        driving, rate, friction, melt, trans, leakage, overburden, scale, ice = middle.values()
        m_speed, m_drop = first_velocity(driving, rate, friction, ice)
        which = (0, tiles - 2)
        early = slice(0, 2 * RIM)
        viscosity(coefficients(m_speed, m_drop, driving, rate, which), 0)
        early_down = from_surface(early)
        top, reach = from_base(early)
        m_first = sheet(m_speed + m_drop * float(w[0]), trans, melt, friction)
        steps_1 = water_steps(overburden, m_first[0], leakage, m_first[1])
        m_friction = scale * steps_1[-1]
        base = between(m_friction * (0.5 * SHARE / rate), which)
        basal = down_of(early_down, base)
        early_basal = split(basal)
        early_surface = split(top - base * basal * reach)
        blank = [jnp.zeros((RIM, wide), jnp.float32)] * (tiles - 3)
        m_second = sheet(
            restore([early_basal[0], *blank, early_basal[1]]) * (0.25 * ice), trans, melt, m_friction
        )
        steps_2 = water_steps(steps_1[-1], m_second[0], leakage, m_second[1])

        halo_sides = ((0, below), (1, above))

        def await_halo(side, exists, parts):
            @pl.when(exists)
            def _():
                for region in range(2):
                    for c in edge_copies(1 - 2 * side, region, parts):
                        c.wait_recv()

        def frame(a, f, b):
            return join([a, f, b])

        def ends(f):
            return join([f[: 2 * RIM], f[rows:]])

        def inside(e, f):
            return join([e[: 2 * RIM], f[RIM : rows - RIM], e[2 * RIM :]])

        def end_frame(i):
            return join([low[i], middle[i][:RIM], middle[i][rows - RIM :], high[i]])

        ends_in, end_velocity, late_down = [], [], []
        for side, exists in halo_sides:
            await_halo(side, exists, (0, 1))
            h = halo_fields(side, exists, (0, 1, 2, 8))
            velocity = first_velocity(h[0], h[1], h[2], h[8])
            inner = slice(0, RIM) if side == 0 else slice(rows - RIM, rows)
            pairs = [(velocity[0], m_speed), (velocity[1], m_drop), (h[0], middle[0]), (h[1], middle[1])]
            viscosity(
                coefficients(*[join([a, f[inner]] if side == 0 else [f[inner], a]) for a, f in pairs], (0,)), (2 + side) * RIM
            )
            tile = slice((2 + side) * RIM, (3 + side) * RIM)
            late_down.append(from_surface(tile))
            ends_in.append(h)
            end_velocity.append(velocity)
            if side == 0:

                @pl.when(jnp.logical_not(below))
                def _():
                    up_ref[0], up_ref[1] = from_base(tile)

        high_up = from_base(slice(3 * RIM, 4 * RIM))
        low, high = ends_in
        low_velocity, high_velocity = end_velocity
        late_down = [join(p) for p in zip(*late_down)]
        for side, exists in halo_sides:
            await_halo(side, exists, (2,))
        low |= halo_fields(0, below, (3, 4, 5, 6, 7))
        high |= halo_fields(1, above, (3, 4, 5, 6, 7))
        end_sheets = [
            sheet(s + d * float(w[0]), f[4], f[3], f[2])
            for f, (s, d) in ((low, low_velocity), (high, high_velocity))
        ]
        rate, melt, trans, leakage, overburden, scale, ice = [end_frame(i) for i in (1, 3, 4, 5, 6, 7, 8)]
        quarter = 0.25 * ice
        valid = join([
            jnp.broadcast_to(below, (RIM, wide)), jnp.ones((2 * RIM, wide), jnp.bool_), jnp.broadcast_to(above, (RIM, wide))
        ])
        trans_eff, source = [frame(*f) for f in zip(end_sheets[0], m_first, end_sheets[1])]
        sweep = sweeper(trans_eff, leakage, ends(source), valid, ends)
        pressure = overburden
        for step_1 in steps_1[:-1]:
            pressure = sweep(inside(pressure, step_1))
        friction = scale * pressure
        base = between(friction * (0.5 * SHARE / rate), (0, 2))
        basal = down_of(late_down, base)

        def arrange(early_pieces, late_pieces):
            first, last = late_pieces
            before, after = early_pieces
            return join([first, jnp.where(upper_sub, before, first), jnp.where(upper_sub, last, after), last]) * quarter

        sliding = arrange(early_basal, split(basal))
        trans_eff, source = sheet(sliding, trans, melt, friction)
        sweep = sweeper(inside(trans_eff, m_second[0]), leakage, source, valid, ends)
        for step_2 in steps_2[:-1]:
            pressure = sweep(inside(pressure, step_2))

        mine = slice(RIM, 3 * RIM)

        def surface():
            @pl.when(below)
            def _():
                up_ref[0], up_ref[1] = from_base(slice(2 * RIM, 3 * RIM))

            top, reach = [join([up_ref[n], f]) for n, f in enumerate(high_up)]
            return arrange(early_surface, split(top - base * basal * reach))[mine]

        send_results(outer_chunks, 1, pressure[mine], surface, sliding[mine], scale[mine])

    for c in main_copies():
        c.wait_send()
    for dx, condition in ((-1, below), (1, above)):
        wait_send(condition, edge_copies(dx, gy))

    inner_rows, outer_rows = pl.ds(0, rows - 2 * RIM), pl.ds(0, 2 * RIM)
    for k, role, count in ((0, is_inner, inner_rows), (1, is_outer, outer_rows)):
        for m in (1, 2):
            wait_send(both(sends_last, role), [result_copy(send_p.at[0, count], 0, count, m, 0, {"gy": partner})])
        wait_send(both(is_water, role), [result_copy(send_p.at[0, count], 0, count, 0, 0, {"gy": partner})])
        wait_send(both(is_ice, role), [result_copy(results.at[:, count], slice(None), count, 0, 0, {"gy": partner})])

    def await_result(condition, src, planes, where, k):
        @pl.when(condition)
        def _():
            result_copy(src, planes, where, 0, k, {"gy": partner}).wait_recv()

    for k, role, count in ((1, is_inner, outer_rows), (0, is_outer, inner_rows)):
        await_result(both(is_ice, role), results.at[:, count], slice(None), count, k)
        await_result(both(is_water, role), send_p.at[0, count], 0, count, k)
    for s in range(1, sectors):
        for k, count in ((0, inner_rows), (1, outer_rows)):
            await_result(is_water, send_p.at[0, count], s, count, 2 * s + k)


def narrow_map(nx, *args):
    sectors, rows, lanes = args[0].shape
    most = max(rows - 2 * RIM, 2 * RIM)
    f32 = jnp.float32
    vmem = pltpu.VMEM
    dma = pltpu.SemaphoreType.DMA
    return pl.pallas_call(
        functools.partial(narrow_kernel, sectors, nx),
        out_shape=pltpu.VMEM((1, sectors, rows, lanes), f32),
        in_specs=[pl.BlockSpec(memory_space=pltpu.HBM)] * len(args),
        out_specs=pl.BlockSpec(memory_space=pltpu.VMEM),
        scratch_shapes=[
            vmem((8, rows, lanes), f32),
            vmem((2, rows, lanes), jnp.int32),
            vmem((8, rows, lanes), f32),
            vmem((2, rows, lanes), jnp.int32),
            vmem((2, 2, 8, RIM, lanes), f32),
            vmem((2, 2, 2, RIM, lanes), jnp.int32),
            vmem((LAYERS, max(rows, 4 * RIM), 2 * lanes), f32),
            vmem((LAYERS, max(rows, 4 * RIM), 2 * lanes), f32),
            vmem((LAYERS, max(rows, 4 * RIM), 2 * lanes), f32),
            vmem((2, RIM, 2 * lanes), f32),
            vmem((2, most, lanes), f32),
            vmem((3, most, lanes), f32),
            dma((2,)),
            dma((8,)),
            dma((14,)),
            pltpu.SemaphoreType.REGULAR((3,)),
            dma((3,)),
            dma((2 * sectors,)),
        ],
        compiler_params=pltpu.CompilerParams(collective_id=0, has_side_effects=True),
    )(*args)


def solution(mesh):
    spec = P(None, "gx", "gy")
    nx, ny = mesh.shape["gx"], mesh.shape["gy"]
    on_device = functools.partial(narrow_map, nx) if ny == 2 else functools.partial(wide_map, nx, ny)
    return jax.shard_map(
        on_device,
        mesh=mesh,
        in_specs=(spec,) * 10,
        out_specs=P("sec", None, "gx", "gy"),
        check_vma=False,
    )
```

```python
import functools

import jax
import jax.numpy as jnp
import numpy as np
from jax import lax
from jax.experimental import pallas as pl
from jax.experimental.pallas import tpu as pltpu
from jax.sharding import PartitionSpec as P

LAYERS = 40
SWEEPS = 4
VERT = 4.0
FLOOR = 0.25
HEATING = 0.5

RIM = 8
HALF = RIM // 2
RESCALE = 10
THIRD = -1.0 / (3.0 * float(np.log(2.0)))
DIRECTIONS = [(dx, dy) for dx in (-1, 0, 1) for dy in (-1, 0, 1) if (dx, dy) != (0, 0)]
MESH = pl.DeviceIdType.MESH


def basal_response():
    matrix = np.zeros((LAYERS, LAYERS))
    for k in range(LAYERS):
        matrix[k, k] = 4.0 + (VERT if k > 0 else 0.0) + (VERT if k < LAYERS - 1 else 0.0)
        if k > 0:
            matrix[k, k - 1] = matrix[k - 1, k] = -VERT
    unit = np.zeros(LAYERS)
    unit[0] = 1.0
    return np.linalg.solve(matrix, unit)


def turn(values, shift, axis):
    return pltpu.roll(values, shift % values.shape[axis], axis)


def neighbours(f):
    return turn(f, -1, 0), turn(f, 1, 0), turn(f, -1, 1), turn(f, 1, 1)


def water_solve(pressure, trans_eff, leakage, source, valid):
    faces = [0.5 * (trans_eff + t) for t in neighbours(trans_eff)]
    total = leakage + ((faces[0] + faces[1]) + (faces[2] + faces[3]))
    inverse = jnp.where(valid, 1.0 / total, 0.0)
    weights = [f * inverse for f in faces]
    base = source * inverse
    for _ in range(SWEEPS):
        parts = [w * p for w, p in zip(weights, neighbours(pressure))]
        pressure = base + ((parts[0] + parts[1]) + (parts[2] + parts[3]))
    return pressure


def wide_kernel(sectors, nx, ny, *refs):
    ins = refs[:10]
    out = refs[10]
    floats, ints, pack_l, pack_r, rim_l, rim_r, q_ref, g_ref, r_ref, send_p = refs[11:21]
    in_sem, send_sem, recv_sem, last_send, last_recv = refs[21:]
    rows, lanes = ins[0].shape[1:]
    sec = lax.axis_index("sec")
    gx = lax.axis_index("gx")
    gy = lax.axis_index("gy")
    strip = lax.rem(sec, sectors)
    is_ice = sec < sectors
    sends_last = jnp.logical_and(sec > 0, is_ice)

    def exists(dx, dy):
        x, y = gx + dx, gy + dy
        return jnp.logical_and(
            jnp.logical_and(x >= 0, x < nx), jnp.logical_and(y >= 0, y < ny)
        )

    float_ids = (0, 1, 2, 5, 6, 7, 8, 9)
    int_ids = (3, 4)
    loads = []
    for slot, arg in enumerate(float_ids):
        loads.append(pltpu.make_async_copy(ins[arg].at[strip], floats.at[slot, pl.ds(RIM, rows)], in_sem.at[0]))
    for slot, arg in enumerate(int_ids):
        loads.append(pltpu.make_async_copy(ins[arg].at[strip], ints.at[slot, pl.ds(RIM, rows)], in_sem.at[1]))
    barrier = pltpu.get_barrier_semaphore()
    count = jnp.int32(0)
    for dx, dy in sorted(DIRECTIONS, key=lambda d: -abs(d[0])):
        here = exists(dx, dy)
        count = count + here.astype(jnp.int32)

        @pl.when(here)
        def _(dx=dx, dy=dy):
            pl.semaphore_signal(barrier, inc=1, device_id={"gx": gx + dx, "gy": gy + dy}, device_id_type=MESH)

    count = count + sends_last.astype(jnp.int32)
    count = count + jnp.where(is_ice, 0, sectors - 1)

    @pl.when(sends_last)
    def _():
        pl.semaphore_signal(barrier, inc=1, device_id={"sec": sectors}, device_id_type=MESH)

    for s in range(1, sectors):

        @pl.when(jnp.logical_not(is_ice))
        def _(s=s):
            pl.semaphore_signal(barrier, inc=1, device_id={"sec": s}, device_id_type=MESH)

    for load in loads:
        load.start()
    for slot, buffer in enumerate((floats, ints)):
        mine = buffer.at[:, pl.ds(RIM, rows)]
        pltpu.make_async_copy(mine, mine, in_sem.at[slot]).wait()

    lane = lax.broadcasted_iota(jnp.int32, (rows, lanes), 1)
    fields = [floats[i, RIM : RIM + rows] for i in range(8)]
    fields += [ints[i, RIM : RIM + rows].astype(jnp.float32) for i in range(2)]
    left = jnp.zeros((rows, lanes), jnp.float32)
    right = jnp.zeros((rows, lanes), jnp.float32)
    for i, f in enumerate(fields):
        moved = turn(f, RIM * i, 1)
        group = lane // RIM
        left = jnp.where(group == i, moved, left)
        right = jnp.where(group == (i - 1) % (lanes // RIM), moved, right)
    pack_l[...] = left
    pack_r[...] = right

    pl.semaphore_wait(barrier, count)

    def copies(dx, dy, n):
        target = {"gx": gx + dx, "gy": gy + dy}

        def remote(src, dst, m):
            return pltpu.make_async_remote_copy(
                src_ref=src, dst_ref=dst, send_sem=send_sem.at[m], recv_sem=recv_sem.at[m],
                device_id=target, device_id_type=MESH,
            )

        if dy == 0:
            first = rows if dx > 0 else RIM
            landing = 0 if dx > 0 else RIM + rows
            return [
                remote(floats.at[:, pl.ds(first, RIM)], floats.at[:, pl.ds(landing, RIM)], n),
                remote(ints.at[:, pl.ds(first, RIM)], ints.at[:, pl.ds(landing, RIM)], 8 + (dx > 0)),
            ]
        src, dst = (pack_r, rim_l) if dy > 0 else (pack_l, rim_r)
        if dx == 0:
            return [remote(src, dst.at[pl.ds(RIM, rows)], n)]
        first = rows - RIM if dx > 0 else 0
        landing = 0 if dx > 0 else RIM + rows
        return [remote(src.at[pl.ds(first, RIM)], dst.at[pl.ds(landing, RIM)], n)]

    order = sorted(range(8), key=lambda n: abs(DIRECTIONS[n][1]))
    for n in order:
        dx, dy = DIRECTIONS[n]

        @pl.when(exists(dx, dy))
        def _(dx=dx, dy=dy, n=n):
            for c in copies(dx, dy, n):
                c.start()

    def arrive(n):
        dx, dy = DIRECTIONS[n]

        @pl.when(exists(-dx, -dy))
        def _():
            for c in copies(dx, dy, n):
                c.wait_recv()

    w = basal_response()
    ext = rows + 2 * RIM
    tall = rows + RIM
    tiles = tall // 8
    wide = 2 * RIM
    slot = lax.broadcasted_iota(jnp.int32, (8, lanes), 1) // wide
    lane_low = jnp.where(gy < ny - 1, lanes + RIM, lanes)
    lane_high = jnp.where(gy > 0, 2 * lanes - RIM, 2 * lanes)

    def in_map_lanes(height):
        lane_i = lax.broadcasted_iota(jnp.int32, (height, 2 * lanes), 1)
        return jnp.logical_or(lane_i < lane_low, lane_i >= lane_high)

    def field_reader(top, height, valid):
        at = slice(top, top + height)
        packed_l, packed_r = rim_l[at], rim_r[at]
        group = lax.broadcasted_iota(jnp.int32, (height, lanes), 1) // RIM

        def field(i, fill):
            main = floats[i, at] if i < 8 else ints[i - 8, at].astype(jnp.float32)
            rim = turn(jnp.where(group == i, packed_r, packed_l), -RIM * i, 1)
            return jnp.where(valid, jnp.concatenate([main, rim], axis=1), fill)

        return field

    def first_velocity(driving, rate, friction, ice):
        viscous = rate * float(FLOOR ** (-1.0 / 3.0))
        speed = driving / (4.0 * viscous)
        drop = -speed * friction / (viscous + friction * float(w[0]))
        return speed * ice, drop * ice

    def squeeze(f, which):
        tile = jnp.zeros((8, lanes), jnp.float32)
        for n, t in enumerate(which):
            moved = turn(f[8 * t : 8 * t + 8, lanes:], wide * n + RIM, 1)
            tile = jnp.where(slot == n, moved, tile)
        return jnp.concatenate([f[8 * t : 8 * t + 8, :lanes] for t in which] + [tile], axis=0)

    def spread(f, count):
        last = f[8 * count :]
        return [
            jnp.concatenate([f[8 * n : 8 * n + 8], turn(last, -(wide * n + RIM), 1)], axis=1)
            for n in range(count)
        ]

    def eliminate(speed, drop, driving, rate, which, offset, lead):
        sxp, sxm, syp, sym = neighbours(speed)
        dxp, dxm, dyp, dym = neighbours(drop)
        sdx, sdy, ddx, ddy = sxp - sxm, syp - sym, dxp - dxm, dyp - dym
        flat = [
            0.03125 * (sdx * sdx + sdy * sdy) + 0.125 * FLOOR,
            0.0625 * (sdx * ddx + sdy * ddy),
            0.03125 * (ddx * ddx + ddy * ddy),
            0.125 * drop * drop,
            0.25 * ((sxp + sxm) + (syp + sym)),
            0.25 * ((dxp + dxm) + (dyp + dym)),
            driving * (0.5 / rate),
        ]
        flat = [squeeze(turn(f, lead, 0), which) for f in flat]
        for n in range(len(which) + 1):
            at = slice(offset + 8 * n, offset + 8 * n + 8)
            c0, c1, c2, c3, n0, n1, dr = [f[8 * n : 8 * n + 8] for f in flat]
            before = None
            for k in range(LAYERS):
                wk = float(w[k])
                strain = c0 + (c1 * wk + c2 * (wk * wk))
                if k < LAYERS - 1:
                    strain = strain + c3 * float((w[k + 1] - w[k]) ** 2)
                twice = jnp.exp2(jnp.log(strain) * THIRD)
                q_ref[k, at] = twice
                r_ref[k, at] = dr + twice * (n0 + n1 * wk)
                if k > 0:
                    g_ref[k - 1, at] = 0.5 * (before + twice)
                before = twice

        at = slice(offset, offset + 8 * (len(which) + 1))
        up_d, up_e, up_t = None, q_ref[0, at], r_ref[0, at]
        down_d, down_e, down_t = None, q_ref[LAYERS - 1, at], r_ref[LAYERS - 1, at]
        product = None

        def step(d, e, t, g, q, r):
            d = e + (g if d is None else g * d)
            return d, q * d + g * e, r * d + g * t

        for k in range(LAYERS - 1):
            j = LAYERS - 2 - k
            g = g_ref[k, at]
            product = g if product is None else product * g
            up_d, up_e, up_t = step(up_d, up_e, up_t, g, q_ref[k + 1, at], r_ref[k + 1, at])
            down_d, down_e, down_t = step(
                down_d, down_e, down_t, g_ref[j, at], q_ref[j, at], r_ref[j, at]
            )
            if k % RESCALE == RESCALE - 1 and k < LAYERS - 2:
                shrink = 1.0 / up_d
                up_d, up_e, up_t, product = None, up_e * shrink, up_t * shrink, product * shrink
                shrink = 1.0 / down_d
                down_d, down_e, down_t = None, down_e * shrink, down_t * shrink
        shrink = 1.0 / up_e
        return down_d, down_e, down_t, up_t * shrink, product * shrink

    def finish(parts, friction, rate, ice, which):
        down_d, down_e, down_t, top, reach = parts
        base = squeeze(turn(friction * (0.5 / rate), -HALF, 0), which)
        mask = squeeze(turn(ice, -HALF, 0), which)
        basal = down_t / (down_e + base * down_d)
        surface = top - base * basal * reach
        return [spread(f * mask, len(which)) for f in (basal, surface)]

    for n in order:
        if DIRECTIONS[n][0] == 0:
            arrive(n)
    early = list(range(1, tiles - 1))
    late = [0, tiles - 1]
    field = field_reader(RIM, rows, in_map_lanes(rows))
    driving, rate = field(0, 0.0), field(1, 1.0)
    speed, drop = first_velocity(driving, rate, field(2, 0.0) * field(9, 0.0), field(8, 0.0))
    early_parts = eliminate(speed, drop, driving, rate, early, 0, HALF)
    for n in order:
        if DIRECTIONS[n][0] != 0:
            arrive(n)

    row_i = lax.broadcasted_iota(jnp.int32, (ext, 2 * lanes), 0)
    row_low = jnp.where(gx > 0, 0, RIM)
    row_high = jnp.where(gx < nx - 1, ext, RIM + rows)
    valid = jnp.logical_and(
        jnp.logical_and(row_i >= row_low, row_i < row_high), in_map_lanes(ext)
    )
    field = field_reader(0, ext, valid)
    driving = field(0, 0.0)
    rate = field(1, 1.0)
    friction = field(2, 0.0)
    melt = field(3, 0.0)
    trans = field(4, 0.0)
    leakage = field(5, 1.0)
    pressure = field(6, 0.0)
    scale = field(7, 0.0)
    ice = field(8, 0.0)
    grounded = field(9, 0.0)
    friction = friction * grounded
    scale = scale * grounded

    speed, drop = first_velocity(driving, rate, friction, ice)
    sliding = speed + drop * float(w[0])
    squared = sliding * sliding
    trans_eff = trans * (1.0 + squared / (1.0 + squared))
    source = melt + HEATING * friction * squared
    pressure = water_solve(pressure, trans_eff, leakage, source, valid)
    friction = scale * pressure

    late_parts = eliminate(speed, drop, driving, rate, late, 8 * (len(early) + 1), -HALF)
    pieces = [None] * tiles
    for parts, which in ((early_parts, early), (late_parts, late)):
        for n, piece in enumerate(zip(*finish(parts, friction, rate, ice, which))):
            pieces[which[n]] = piece
    blank = jnp.zeros((RIM, 2 * lanes), jnp.float32)
    basal = turn(jnp.concatenate([p[0] for p in pieces] + [blank], axis=0), HALF, 0)
    surface = jnp.concatenate([p[1][:, :lanes] for p in pieces], axis=0)
    sliding = jnp.where(valid, basal, 0.0)
    squared = sliding * sliding
    trans_eff = trans * (1.0 + squared / (1.0 + squared))
    source = melt + HEATING * friction * squared
    pressure = water_solve(pressure, trans_eff, leakage, source, valid)
    block = pressure[RIM : RIM + rows, :lanes]
    send_p[...] = block

    def last():
        return pltpu.make_async_remote_copy(
            src_ref=send_p, dst_ref=out.at[0, strip], send_sem=last_send, recv_sem=last_recv.at[strip],
            device_id={"sec": sectors}, device_id_type=MESH,
        )

    @pl.when(sends_last)
    def _():
        last().start()

    @pl.when(is_ice)
    def _():
        out[0, 0] = turn(surface, -HALF, 0)[:rows]
        out[0, 1] = sliding[RIM : RIM + rows, :lanes]
        out[0, 2] = scale[RIM : RIM + rows, :lanes] * block

    @pl.when(jnp.logical_not(is_ice))
    def _():
        out[0, 0] = block

    for n in order:
        dx, dy = DIRECTIONS[n]

        @pl.when(exists(dx, dy))
        def _(dx=dx, dy=dy, n=n):
            for c in copies(dx, dy, n):
                c.wait_send()

    @pl.when(sends_last)
    def _():
        last().wait_send()

    for s in range(1, sectors):

        @pl.when(jnp.logical_not(is_ice))
        def _(s=s):
            pltpu.make_async_remote_copy(
                src_ref=send_p, dst_ref=out.at[0, s], send_sem=last_send, recv_sem=last_recv.at[s],
                device_id={"sec": 0}, device_id_type=MESH,
            ).wait_recv()


def wide_map(nx, ny, *args):
    sectors, rows, lanes = args[0].shape
    ext = rows + 2 * RIM
    f32 = jnp.float32
    vmem = pltpu.VMEM
    dma = pltpu.SemaphoreType.DMA
    return pl.pallas_call(
        functools.partial(wide_kernel, sectors, nx, ny),
        out_shape=pltpu.VMEM((1, sectors, rows, lanes), f32),
        in_specs=[pl.BlockSpec(memory_space=pltpu.HBM)] * len(args),
        out_specs=pl.BlockSpec(memory_space=pltpu.VMEM),
        scratch_shapes=[
            vmem((8, ext, lanes), f32),
            vmem((2, ext, lanes), jnp.int32),
            vmem((rows, lanes), f32),
            vmem((rows, lanes), f32),
            vmem((ext, lanes), f32),
            vmem((ext, lanes), f32),
            vmem((LAYERS, ext + RIM, lanes), f32),
            vmem((LAYERS, ext + RIM, lanes), f32),
            vmem((LAYERS, ext + RIM, lanes), f32),
            vmem((rows, lanes), f32),
            dma((2,)),
            dma((10,)),
            dma((10,)),
            dma,
            dma((sectors,)),
        ],
        compiler_params=pltpu.CompilerParams(collective_id=0, has_side_effects=True),
    )(*args)


SHARE = 32.0 ** (-1.0 / 3.0)


def steady_drop(w):
    ratios = np.float32(4.0 * ((w[1:] - w[:-1]) / w[:-1]) ** 2)
    same = np.cumprod(ratios == ratios[0])
    return float(ratios[0]), int(same.sum())


ORDER = (0, 1, 2, 5, 6, 7, 8, 9, 3, 4)


def narrow_kernel(sectors, nx, *refs):
    ins = refs[:10]
    out = refs[10]
    own_f, own_i, part_f, part_i, halo_f, halo_i, q_ref, g_ref, r_ref, up_ref, send_p, results = refs[11:23]
    in_sem, main_send, edge_send, out_send, main_recv, halo_recv, out_recv, credit = refs[23:]
    rows, lanes = ins[0].shape[1:]
    sec = lax.axis_index("sec")
    gx = lax.axis_index("gx")
    gy = lax.axis_index("gy")
    partner = 1 - gy
    is_outer = gy == 1
    is_inner = gy == 0
    strip = lax.rem(sec, sectors)
    is_ice = sec < sectors
    is_water = jnp.logical_not(is_ice)
    sends_last = jnp.logical_and(sec > 0, is_ice)
    below, above = gx > 0, gx < nx - 1
    direct = sec > 0
    first_sector = sec == 0

    def both(p, q):
        return jnp.logical_and(p, q)

    def number(condition):
        return condition.astype(jnp.int32)

    def await_tiles(sem, count):
        room = q_ref.at[pl.ds(0, count), pl.ds(0, RIM), pl.ds(0, lanes)]
        pltpu.make_async_copy(room, room, sem).wait()

    def copy_in(n):
        dst = own_f.at[n] if n < 8 else own_i.at[n - 8]
        return pltpu.make_async_copy(ins[ORDER[n]].at[strip], dst, in_sem)

    def load():
        for n in range(10):
            copy_in(n).start()

    pl.when(is_outer)(load)
    barrier = pltpu.get_barrier_semaphore()

    def signal(condition, sem, target, role=True):
        @pl.when(jnp.logical_and(condition, role))
        def _():
            pl.semaphore_signal(sem, inc=1, device_id=target, device_id_type=MESH)

    signal(above, barrier, {"gx": gx + 1, "gy": 0}, is_outer)
    signal(above, barrier, {"gx": gx + 1, "gy": 1}, is_outer)
    signal(both(below, direct), barrier, {"gx": gx - 1, "gy": 1}, is_outer)
    signal(sec >= 0, barrier, {"gy": partner})
    signal(sends_last, barrier, {"sec": sectors, "gy": partner})
    signal(sends_last, barrier, {"sec": sectors})
    count = 1 + number(below) + number(both(both(above, direct), is_outer)) + jnp.where(is_ice, 0, 2 * (sectors - 1))
    pl.semaphore_wait(barrier, count)
    signal(both(below, first_sector), credit.at[0], {"gx": gx - 1, "gy": 1}, is_outer)
    signal(both(is_outer, direct), credit.at[0], {"gy": 0})
    for s in range(1, sectors):
        signal(is_water, credit.at[1], {"sec": s, "gy": partner})
        signal(is_water, credit.at[1], {"sec": s})

    def remote(src, dst, sent, landed, target):
        return pltpu.make_async_remote_copy(
            src_ref=src, dst_ref=dst, send_sem=sent, recv_sem=landed, device_id=target, device_id_type=MESH,
        )

    def main_copies():
        target = {"gy": partner}
        return [remote(own_f, part_f, main_send, main_recv, target), remote(own_i, part_i, main_send, main_recv, target)]

    def edge_copies():
        src = pl.ds(rows - RIM, RIM)
        target = {"gx": gx + 1, "gy": 1}
        first, rest = pl.ds(0, 3), pl.ds(3, 5)
        return [
            remote(own_f.at[first, src], halo_f.at[0, gy, first], edge_send, halo_recv.at[0, 0], target),
            remote(own_i.at[:, src], halo_i.at[0, gy], edge_send, halo_recv.at[0, 0], target),
            remote(own_f.at[rest, src], halo_f.at[0, gy, rest], edge_send, halo_recv.at[0, 1], target),
        ]

    def start(condition, copies):
        @pl.when(condition)
        def _():
            for c in copies:
                c.start()

    def await_credit(condition, which, amount):
        @pl.when(condition)
        def _():
            pl.semaphore_wait(credit.at[which], amount)

    @pl.when(below)
    def _():
        for n in (0, 1, 2, 8, 9, 3, 4, 5, 6, 7):
            src = ins[ORDER[n]].at[strip, pl.ds(0, RIM)]
            dst = halo_f.at[1, gy, n] if n < 8 else halo_i.at[1, gy, n - 8]
            part = int(3 <= n < 8)
            remote(src, dst, edge_send, halo_recv.at[1, part], {"gx": gx - 1, "gy": 1}).start()

    pl.when(is_inner)(load)

    @pl.when(is_inner)
    def _():
        for n in (0, 1, 2, 8, 9, 3, 4, 5, 6, 7):
            dst = part_f.at[n] if n < 8 else part_i.at[n - 8]
            remote(ins[ORDER[n]].at[strip], dst, main_send, main_recv, {"gy": 1}).start()

    await_tiles(in_sem, 10 * rows // RIM)
    start(is_outer, main_copies())
    await_credit(both(both(above, first_sector), is_outer), 0, 1)
    signal(both(is_outer, first_sector), credit.at[0], {"gy": 0})
    await_credit(is_inner, 0, 1)
    start(above, edge_copies())

    w = basal_response()
    steady, settled = steady_drop(w)
    wide = 2 * lanes
    lane = lax.broadcasted_iota(jnp.int32, (RIM, wide), 1)
    upper_sub = lax.broadcasted_iota(jnp.int32, (RIM, wide), 0) >= HALF
    last_lane = lane == wide - 1
    first_lane = lane == 0

    def join(parts):
        return jnp.concatenate(parts, axis=0)

    def tall_mask(mask, count):
        return join([mask] * count)

    def beside(f, i):
        return f[i] if i < 8 else f[i - 8].astype(jnp.float32)

    def fields(left, right, which=range(9)):
        def field(i):
            return jnp.concatenate([beside(left[i >= 8], i), beside(right[i >= 8], i)], axis=1)

        return {i: field(i) * field(9) if i in (2, 7) else field(i) for i in which}

    def halo_fields(side, exists, which):
        left, right = [(halo_f.at[side, r], halo_i.at[side, r]) for r in range(2)]
        return {
            i: jnp.where(exists, f, 1.0 if i in (1, 5) else 0.0) for i, f in fields(left, right, which).items()
        }

    def first_velocity(driving, rate, friction, ice):
        viscous = rate * float(FLOOR ** (-1.0 / 3.0))
        speed = driving / (4.0 * viscous)
        drop = -speed * friction / (viscous + friction * float(w[0]))
        return speed * ice, drop * ice

    def shifts(f):
        count = f.shape[0] // RIM
        yp = jnp.where(tall_mask(last_lane, count), 0.0, turn(f, -1, 1))
        ym = jnp.where(tall_mask(first_lane, count), 0.0, turn(f, 1, 1))
        return turn(f, -1, 0), turn(f, 1, 0), yp, ym

    def sheet(sliding, trans, melt, friction):
        squared = sliding * sliding
        return trans * (1.0 + squared / (1.0 + squared)), melt + HEATING * friction * squared

    def sweeper(trans_eff, leakage, source, valid, keep):
        here = keep(trans_eff)
        faces = [0.5 * (here + keep(t)) for t in shifts(trans_eff)]
        total = leakage + ((faces[0] + faces[1]) + (faces[2] + faces[3]))
        inverse = 1.0 / total if valid is None else jnp.where(valid, 1.0 / total, 0.0)
        weights = [f * inverse for f in faces]
        count = here.shape[0] // RIM
        weights[2] = jnp.where(tall_mask(last_lane, count), 0.0, weights[2])
        weights[3] = jnp.where(tall_mask(first_lane, count), 0.0, weights[3])
        base = source * inverse

        def sweep(pressure):
            parts = [w * keep(p) for w, p in zip(weights, neighbours(pressure))]
            return base + ((parts[0] + parts[1]) + (parts[2] + parts[3]))

        return sweep

    def water_steps(pressure, trans_eff, leakage, source):
        sweep = sweeper(trans_eff, leakage, source, None, lambda f: f)
        steps = [pressure]
        for _ in range(SWEEPS):
            steps.append(sweep(steps[-1]))
        return steps

    def split(f):
        return [f[RIM * k : RIM * k + RIM] for k in range(f.shape[0] // RIM)]

    def between(f, which):
        pieces = split(f)
        return join([jnp.where(upper_sub, pieces[k], pieces[k + 1]) for k in which])

    def restore(pieces):
        middle = [jnp.where(upper_sub, q, p) for p, q in zip(pieces[:-1], pieces[1:])]
        return join([pieces[0], *middle, pieces[-1]])

    def coefficients(speed, drop, driving, rate, which):
        s_shift = [between(f, which) for f in shifts(speed)]
        d_shift = [between(f, which) for f in shifts(drop)]
        drop, driving, rate = [between(f, which) for f in (drop, driving, rate)]
        sdx, sdy = s_shift[0] - s_shift[1], s_shift[2] - s_shift[3]
        ddx, ddy = d_shift[0] - d_shift[1], d_shift[2] - d_shift[3]
        c2, c3 = ddx * ddx + ddy * ddy, drop * drop
        return [
            (sdx * sdx + sdy * sdy) + 4.0 * FLOOR,
            sdx * ddx + sdy * ddy,
            c2,
            c3,
            c2 + steady * c3,
            (s_shift[0] + s_shift[1]) + (s_shift[2] + s_shift[3]),
            (d_shift[0] + d_shift[1]) + (d_shift[2] + d_shift[3]),
            driving * (2.0 * SHARE / rate),
        ]

    def viscosity(flat, offset):
        for n in range(flat[0].shape[0] // RIM):
            at = slice(offset + RIM * n, offset + RIM * n + RIM)
            c0, c1, c2, c3, c23, n0, n1, dr = [f[RIM * n : RIM * n + RIM] for f in flat]
            higher = None
            for k in reversed(range(LAYERS)):
                wk = float(w[k])
                if k < settled:
                    strain = c0 + (c1 * (2.0 * wk) + c23 * (wk * wk))
                else:
                    strain = c0 + (c1 * (2.0 * wk) + c2 * (wk * wk))
                    if k < LAYERS - 1:
                        strain = strain + c3 * float(4.0 * (w[k + 1] - w[k]) ** 2)
                now = jnp.exp2(jnp.log(strain) * THIRD)
                q_ref[k, at] = now
                r_ref[k, at] = dr + now * (n0 + n1 * wk)
                if k < LAYERS - 1:
                    g_ref[k, at] = 0.5 * (now + higher)
                higher = now

    def step(d, e, t, g, q, r):
        d = e + (g if d is None else g * d)
        return d, q * d + g * e, r * d + g * t

    def from_surface(at):
        d, e, t = None, q_ref[LAYERS - 1, at], r_ref[LAYERS - 1, at]
        for k in range(LAYERS - 1):
            j = LAYERS - 2 - k
            d, e, t = step(d, e, t, g_ref[j, at], q_ref[j, at], r_ref[j, at])
            if k % RESCALE == RESCALE - 1 and k < LAYERS - 2:
                shrink = 1.0 / d
                d, e, t = None, e * shrink, t * shrink
        return d, e, t

    def from_base(at):
        d, e, t, product = None, q_ref[0, at], r_ref[0, at], None
        for k in range(LAYERS - 1):
            g = g_ref[k, at]
            product = g if product is None else product * g
            d, e, t = step(d, e, t, g, q_ref[k + 1, at], r_ref[k + 1, at])
            if k % RESCALE == RESCALE - 1 and k < LAYERS - 2:
                shrink = 1.0 / d
                d, e, t, product = None, e * shrink, t * shrink, product * shrink
        shrink = 1.0 / e
        return t * shrink, product * shrink

    def result_copy(src, planes, where, target):
        return remote(src, out.at[0, planes, where], out_send, out_recv, target)

    inner_chunks = [(0, RIM, rows - 2 * RIM)]
    outer_chunks = [(0, 0, RIM), (RIM, rows - RIM, RIM)]

    def send_results(chunks, k, pressure, surface, sliding, scale):
        count = pressure.shape[0]
        at = pl.ds(0, count)
        send_p[0, at] = pressure[:, :lanes]
        send_p[1, at] = pressure[:, lanes:]
        mine, other = (slice(0, lanes), 1) if k == 0 else (slice(lanes, wide), 0)

        def started(copies):
            for c in copies:
                c.start()

        def pieces(src, planes, target):
            return [result_copy(src(pl.ds(a, n)), planes, pl.ds(b, n), target) for a, b, n in chunks]

        @pl.when(sends_last)
        def _():
            pl.semaphore_wait(credit.at[1], 2)
            for r in (other, 1 - other):
                started(pieces(lambda d, r=r: send_p.at[r, d], strip, {"sec": sectors, "gy": r}))

        @pl.when(is_water)
        def _():
            started(pieces(lambda d: send_p.at[other, d], 0, {"gy": partner}))
            for a, b, n in chunks:
                out[0, 0, b : b + n] = pressure[a : a + n, mine]

        @pl.when(is_ice)
        def _():
            theirs = slice(lanes, wide) if k == 0 else slice(0, lanes)
            for plane, f in enumerate((surface(), sliding, scale * pressure)):
                results[plane, at] = f[:, theirs]
                for a, b, n in chunks:
                    out[0, plane, b : b + n] = f[a : a + n, mine]
            started(pieces(lambda d: results.at[:, d], slice(None), {"gy": partner}))

    tiles = rows // RIM
    await_tiles(main_recv, 10 * tiles)

    def down_of(parts, base):
        d, e, t = parts
        return t / (e + base * d)

    @pl.when(is_inner)
    def _():
        driving, rate, friction, melt, trans, leakage, overburden, scale, ice = fields((own_f, own_i), (part_f, part_i)).values()
        which = range(tiles - 1)
        at = slice(0, rows - RIM)
        speed, drop = first_velocity(driving, rate, friction, ice)
        viscosity(coefficients(speed, drop, driving, rate, which), 0)
        trans_eff, source = sheet(speed + drop * float(w[0]), trans, melt, friction)
        pressure = water_steps(overburden, trans_eff, leakage, source)[-1]
        friction = scale * pressure
        base = between(friction * (0.5 * SHARE / rate), which)
        basal = down_of(from_surface(at), base)
        quarter = 0.25 * ice
        sliding = restore(split(basal)) * quarter
        trans_eff, source = sheet(sliding, trans, melt, friction)
        pressure = water_steps(pressure, trans_eff, leakage, source)[-1]
        mine = slice(RIM, rows - RIM)

        def surface():
            top, reach = from_base(at)
            return (restore(split(top - base * basal * reach)) * quarter)[mine]

        send_results(inner_chunks, 0, pressure[mine], surface, sliding[mine], scale[mine])

    @pl.when(is_outer)
    def _():
        middle = fields((part_f, part_i), (own_f, own_i))
        driving, rate, friction, melt, trans, leakage, overburden, scale, ice = middle.values()
        m_speed, m_drop = first_velocity(driving, rate, friction, ice)
        which = (0, tiles - 2)
        early = slice(0, 2 * RIM)
        viscosity(coefficients(m_speed, m_drop, driving, rate, which), 0)
        early_down = from_surface(early)
        top, reach = from_base(early)
        m_first = sheet(m_speed + m_drop * float(w[0]), trans, melt, friction)
        steps_1 = water_steps(overburden, m_first[0], leakage, m_first[1])
        m_friction = scale * steps_1[-1]
        base = between(m_friction * (0.5 * SHARE / rate), which)
        basal = down_of(early_down, base)
        early_basal = split(basal)
        early_surface = split(top - base * basal * reach)
        blank = [jnp.zeros((RIM, wide), jnp.float32)] * (tiles - 3)
        m_second = sheet(
            restore([early_basal[0], *blank, early_basal[1]]) * (0.25 * ice), trans, melt, m_friction
        )
        steps_2 = water_steps(steps_1[-1], m_second[0], leakage, m_second[1])

        halo_sides = ((0, below), (1, above))

        def await_halo(side, exists, part):
            pl.when(exists)(functools.partial(await_tiles, halo_recv.at[side, part], 10))

        def frame(a, f, b):
            return join([a, f, b])

        def ends(f):
            return join([f[: 2 * RIM], f[rows:]])

        def inside(e, f):
            return join([e[: 2 * RIM], f[RIM : rows - RIM], e[2 * RIM :]])

        def end_frame(i):
            return join([low[i], middle[i][:RIM], middle[i][rows - RIM :], high[i]])

        ends_in, end_velocity, late_down = [], [], []
        for side, exists in halo_sides:
            await_halo(side, exists, 0)
            h = halo_fields(side, exists, (0, 1, 2, 8))
            velocity = first_velocity(h[0], h[1], h[2], h[8])
            inner = slice(0, RIM) if side == 0 else slice(rows - RIM, rows)
            pairs = [(velocity[0], m_speed), (velocity[1], m_drop), (h[0], middle[0]), (h[1], middle[1])]
            viscosity(
                coefficients(*[join([a, f[inner]] if side == 0 else [f[inner], a]) for a, f in pairs], (0,)), (2 + side) * RIM
            )
            tile = slice((2 + side) * RIM, (3 + side) * RIM)
            late_down.append(from_surface(tile))
            ends_in.append(h)
            end_velocity.append(velocity)
            if side == 0:

                @pl.when(jnp.logical_not(below))
                def _():
                    up_ref[0], up_ref[1] = from_base(tile)

        high_up = from_base(slice(3 * RIM, 4 * RIM))
        low, high = ends_in
        low_velocity, high_velocity = end_velocity
        late_down = [join(p) for p in zip(*late_down)]
        for side, exists in halo_sides:
            await_halo(side, exists, 1)
        low |= halo_fields(0, below, (3, 4, 5, 6, 7))
        high |= halo_fields(1, above, (3, 4, 5, 6, 7))
        end_sheets = [
            sheet(s + d * float(w[0]), f[4], f[3], f[2])
            for f, (s, d) in ((low, low_velocity), (high, high_velocity))
        ]
        rate, melt, trans, leakage, overburden, scale, ice = [end_frame(i) for i in (1, 3, 4, 5, 6, 7, 8)]
        quarter = 0.25 * ice
        valid = join([
            jnp.broadcast_to(below, (RIM, wide)), jnp.ones((2 * RIM, wide), jnp.bool_), jnp.broadcast_to(above, (RIM, wide))
        ])
        trans_eff, source = [frame(*f) for f in zip(end_sheets[0], m_first, end_sheets[1])]
        sweep = sweeper(trans_eff, leakage, ends(source), valid, ends)
        pressure = overburden
        for step_1 in steps_1[:-1]:
            pressure = sweep(inside(pressure, step_1))
        friction = scale * pressure
        base = between(friction * (0.5 * SHARE / rate), (0, 2))
        basal = down_of(late_down, base)

        def arrange(early_pieces, late_pieces):
            first, last = late_pieces
            before, after = early_pieces
            return join([first, jnp.where(upper_sub, before, first), jnp.where(upper_sub, last, after), last]) * quarter

        sliding = arrange(early_basal, split(basal))
        trans_eff, source = sheet(sliding, trans, melt, friction)
        sweep = sweeper(inside(trans_eff, m_second[0]), leakage, source, valid, ends)
        for step_2 in steps_2[:-1]:
            pressure = sweep(inside(pressure, step_2))

        mine = slice(RIM, 3 * RIM)

        def surface():
            @pl.when(below)
            def _():
                up_ref[0], up_ref[1] = from_base(slice(2 * RIM, 3 * RIM))

            top, reach = [join([up_ref[n], f]) for n, f in enumerate(high_up)]
            return arrange(early_surface, split(top - base * basal * reach))[mine]

        send_results(outer_chunks, 1, pressure[mine], surface, sliding[mine], scale[mine])

    await_tiles(main_send, 10 * tiles)
    pl.when(both(below, above))(functools.partial(await_tiles, edge_send, 20))
    pl.when(below != above)(functools.partial(await_tiles, edge_send, 10))
    counts = (tiles - 2, 2)
    for role, mine, theirs in ((is_inner, *counts), (is_outer, *counts[::-1])):
        pl.when(both(sends_last, role))(functools.partial(await_tiles, out_send, 5 * mine))
        pl.when(both(first_sector, role))(functools.partial(await_tiles, out_send, 3 * mine))
        pl.when(both(is_water, role))(functools.partial(await_tiles, out_send, mine))
        pl.when(both(is_ice, role))(functools.partial(await_tiles, out_recv, 3 * theirs))
        pl.when(both(is_water, role))(functools.partial(await_tiles, out_recv, theirs + (sectors - 1) * tiles))


def narrow_map(nx, *args):
    sectors, rows, lanes = args[0].shape
    most = max(rows - 2 * RIM, 2 * RIM)
    f32 = jnp.float32
    vmem = pltpu.VMEM
    dma = pltpu.SemaphoreType.DMA
    return pl.pallas_call(
        functools.partial(narrow_kernel, sectors, nx),
        out_shape=pltpu.VMEM((1, sectors, rows, lanes), f32),
        in_specs=[pl.BlockSpec(memory_space=pltpu.HBM)] * len(args),
        out_specs=pl.BlockSpec(memory_space=pltpu.VMEM),
        scratch_shapes=[
            vmem((8, rows, lanes), f32),
            vmem((2, rows, lanes), jnp.int32),
            vmem((8, rows, lanes), f32),
            vmem((2, rows, lanes), jnp.int32),
            vmem((2, 2, 8, RIM, lanes), f32),
            vmem((2, 2, 2, RIM, lanes), jnp.int32),
            vmem((LAYERS, max(rows, 4 * RIM), 2 * lanes), f32),
            vmem((LAYERS, max(rows, 4 * RIM), 2 * lanes), f32),
            vmem((LAYERS, max(rows, 4 * RIM), 2 * lanes), f32),
            vmem((2, RIM, 2 * lanes), f32),
            vmem((2, most, lanes), f32),
            vmem((3, most, lanes), f32),
            dma,
            dma,
            dma,
            dma,
            dma,
            dma((2, 2)),
            dma,
            pltpu.SemaphoreType.REGULAR((2,)),
        ],
        compiler_params=pltpu.CompilerParams(collective_id=0, has_side_effects=True),
    )(*args)


def solution(mesh):
    spec = P(None, "gx", "gy")
    nx, ny = mesh.shape["gx"], mesh.shape["gy"]
    on_device = functools.partial(narrow_map, nx) if ny == 2 else functools.partial(wide_map, nx, ny)
    return jax.shard_map(
        on_device,
        mesh=mesh,
        in_specs=(spec,) * 10,
        out_specs=P("sec", None, "gx", "gy"),
        check_vma=False,
    )
```

```python
import functools

import jax
import jax.numpy as jnp
import numpy as np
from jax import lax
from jax.experimental import pallas as pl
from jax.experimental.pallas import tpu as pltpu
from jax.sharding import PartitionSpec as P

LAYERS = 40
SWEEPS = 4
VERT = 4.0
FLOOR = 0.25
HEATING = 0.5

RIM = 8
HALF = RIM // 2
RESCALE = 10
THIRD = -1.0 / (3.0 * float(np.log(2.0)))
DIRECTIONS = [(dx, dy) for dx in (-1, 0, 1) for dy in (-1, 0, 1) if (dx, dy) != (0, 0)]
MESH = pl.DeviceIdType.MESH


def basal_response():
    matrix = np.zeros((LAYERS, LAYERS))
    for k in range(LAYERS):
        matrix[k, k] = 4.0 + (VERT if k > 0 else 0.0) + (VERT if k < LAYERS - 1 else 0.0)
        if k > 0:
            matrix[k, k - 1] = matrix[k - 1, k] = -VERT
    unit = np.zeros(LAYERS)
    unit[0] = 1.0
    return np.linalg.solve(matrix, unit)


def turn(values, shift, axis):
    return pltpu.roll(values, shift % values.shape[axis], axis)


def neighbours(f):
    return turn(f, -1, 0), turn(f, 1, 0), turn(f, -1, 1), turn(f, 1, 1)


def water_solve(pressure, trans_eff, leakage, source, valid):
    faces = [0.5 * (trans_eff + t) for t in neighbours(trans_eff)]
    total = leakage + ((faces[0] + faces[1]) + (faces[2] + faces[3]))
    inverse = jnp.where(valid, 1.0 / total, 0.0)
    weights = [f * inverse for f in faces]
    base = source * inverse
    for _ in range(SWEEPS):
        parts = [w * p for w, p in zip(weights, neighbours(pressure))]
        pressure = base + ((parts[0] + parts[1]) + (parts[2] + parts[3]))
    return pressure


def wide_kernel(sectors, nx, ny, *refs):
    ins = refs[:10]
    out = refs[10]
    floats, ints, pack_l, pack_r, rim_l, rim_r, q_ref, g_ref, r_ref, send_p = refs[11:21]
    in_sem, send_sem, recv_sem, last_send, last_recv = refs[21:]
    rows, lanes = ins[0].shape[1:]
    sec = lax.axis_index("sec")
    gx = lax.axis_index("gx")
    gy = lax.axis_index("gy")
    strip = lax.rem(sec, sectors)
    is_ice = sec < sectors
    sends_last = jnp.logical_and(sec > 0, is_ice)

    def exists(dx, dy):
        x, y = gx + dx, gy + dy
        return jnp.logical_and(
            jnp.logical_and(x >= 0, x < nx), jnp.logical_and(y >= 0, y < ny)
        )

    float_ids = (0, 1, 2, 5, 6, 7, 8, 9)
    int_ids = (3, 4)
    loads = []
    for slot, arg in enumerate(float_ids):
        loads.append(pltpu.make_async_copy(ins[arg].at[strip], floats.at[slot, pl.ds(RIM, rows)], in_sem.at[0]))
    for slot, arg in enumerate(int_ids):
        loads.append(pltpu.make_async_copy(ins[arg].at[strip], ints.at[slot, pl.ds(RIM, rows)], in_sem.at[1]))
    barrier = pltpu.get_barrier_semaphore()
    count = jnp.int32(0)
    for dx, dy in sorted(DIRECTIONS, key=lambda d: -abs(d[0])):
        here = exists(dx, dy)
        count = count + here.astype(jnp.int32)

        @pl.when(here)
        def _(dx=dx, dy=dy):
            pl.semaphore_signal(barrier, inc=1, device_id={"gx": gx + dx, "gy": gy + dy}, device_id_type=MESH)

    count = count + sends_last.astype(jnp.int32)
    count = count + jnp.where(is_ice, 0, sectors - 1)

    @pl.when(sends_last)
    def _():
        pl.semaphore_signal(barrier, inc=1, device_id={"sec": sectors}, device_id_type=MESH)

    for s in range(1, sectors):

        @pl.when(jnp.logical_not(is_ice))
        def _(s=s):
            pl.semaphore_signal(barrier, inc=1, device_id={"sec": s}, device_id_type=MESH)

    for load in loads:
        load.start()
    for slot, buffer in enumerate((floats, ints)):
        mine = buffer.at[:, pl.ds(RIM, rows)]
        pltpu.make_async_copy(mine, mine, in_sem.at[slot]).wait()

    lane = lax.broadcasted_iota(jnp.int32, (rows, lanes), 1)
    fields = [floats[i, RIM : RIM + rows] for i in range(8)]
    fields += [ints[i, RIM : RIM + rows].astype(jnp.float32) for i in range(2)]
    left = jnp.zeros((rows, lanes), jnp.float32)
    right = jnp.zeros((rows, lanes), jnp.float32)
    for i, f in enumerate(fields):
        moved = turn(f, RIM * i, 1)
        group = lane // RIM
        left = jnp.where(group == i, moved, left)
        right = jnp.where(group == (i - 1) % (lanes // RIM), moved, right)
    pack_l[...] = left
    pack_r[...] = right

    pl.semaphore_wait(barrier, count)

    def copies(dx, dy, n):
        target = {"gx": gx + dx, "gy": gy + dy}

        def remote(src, dst, m):
            return pltpu.make_async_remote_copy(
                src_ref=src, dst_ref=dst, send_sem=send_sem.at[m], recv_sem=recv_sem.at[m],
                device_id=target, device_id_type=MESH,
            )

        if dy == 0:
            first = rows if dx > 0 else RIM
            landing = 0 if dx > 0 else RIM + rows
            return [
                remote(floats.at[:, pl.ds(first, RIM)], floats.at[:, pl.ds(landing, RIM)], n),
                remote(ints.at[:, pl.ds(first, RIM)], ints.at[:, pl.ds(landing, RIM)], 8 + (dx > 0)),
            ]
        src, dst = (pack_r, rim_l) if dy > 0 else (pack_l, rim_r)
        if dx == 0:
            return [remote(src, dst.at[pl.ds(RIM, rows)], n)]
        first = rows - RIM if dx > 0 else 0
        landing = 0 if dx > 0 else RIM + rows
        return [remote(src.at[pl.ds(first, RIM)], dst.at[pl.ds(landing, RIM)], n)]

    order = sorted(range(8), key=lambda n: abs(DIRECTIONS[n][1]))
    for n in order:
        dx, dy = DIRECTIONS[n]

        @pl.when(exists(dx, dy))
        def _(dx=dx, dy=dy, n=n):
            for c in copies(dx, dy, n):
                c.start()

    def arrive(n):
        dx, dy = DIRECTIONS[n]

        @pl.when(exists(-dx, -dy))
        def _():
            for c in copies(dx, dy, n):
                c.wait_recv()

    w = basal_response()
    ext = rows + 2 * RIM
    tall = rows + RIM
    tiles = tall // 8
    wide = 2 * RIM
    slot = lax.broadcasted_iota(jnp.int32, (8, lanes), 1) // wide
    lane_low = jnp.where(gy < ny - 1, lanes + RIM, lanes)
    lane_high = jnp.where(gy > 0, 2 * lanes - RIM, 2 * lanes)

    def in_map_lanes(height):
        lane_i = lax.broadcasted_iota(jnp.int32, (height, 2 * lanes), 1)
        return jnp.logical_or(lane_i < lane_low, lane_i >= lane_high)

    def field_reader(top, height, valid):
        at = slice(top, top + height)
        packed_l, packed_r = rim_l[at], rim_r[at]
        group = lax.broadcasted_iota(jnp.int32, (height, lanes), 1) // RIM

        def field(i, fill):
            main = floats[i, at] if i < 8 else ints[i - 8, at].astype(jnp.float32)
            rim = turn(jnp.where(group == i, packed_r, packed_l), -RIM * i, 1)
            return jnp.where(valid, jnp.concatenate([main, rim], axis=1), fill)

        return field

    def first_velocity(driving, rate, friction, ice):
        viscous = rate * float(FLOOR ** (-1.0 / 3.0))
        speed = driving / (4.0 * viscous)
        drop = -speed * friction / (viscous + friction * float(w[0]))
        return speed * ice, drop * ice

    def squeeze(f, which):
        tile = jnp.zeros((8, lanes), jnp.float32)
        for n, t in enumerate(which):
            moved = turn(f[8 * t : 8 * t + 8, lanes:], wide * n + RIM, 1)
            tile = jnp.where(slot == n, moved, tile)
        return jnp.concatenate([f[8 * t : 8 * t + 8, :lanes] for t in which] + [tile], axis=0)

    def spread(f, count):
        last = f[8 * count :]
        return [
            jnp.concatenate([f[8 * n : 8 * n + 8], turn(last, -(wide * n + RIM), 1)], axis=1)
            for n in range(count)
        ]

    def eliminate(speed, drop, driving, rate, which, offset, lead):
        sxp, sxm, syp, sym = neighbours(speed)
        dxp, dxm, dyp, dym = neighbours(drop)
        sdx, sdy, ddx, ddy = sxp - sxm, syp - sym, dxp - dxm, dyp - dym
        flat = [
            0.03125 * (sdx * sdx + sdy * sdy) + 0.125 * FLOOR,
            0.0625 * (sdx * ddx + sdy * ddy),
            0.03125 * (ddx * ddx + ddy * ddy),
            0.125 * drop * drop,
            0.25 * ((sxp + sxm) + (syp + sym)),
            0.25 * ((dxp + dxm) + (dyp + dym)),
            driving * (0.5 / rate),
        ]
        flat = [squeeze(turn(f, lead, 0), which) for f in flat]
        for n in range(len(which) + 1):
            at = slice(offset + 8 * n, offset + 8 * n + 8)
            c0, c1, c2, c3, n0, n1, dr = [f[8 * n : 8 * n + 8] for f in flat]
            before = None
            for k in range(LAYERS):
                wk = float(w[k])
                strain = c0 + (c1 * wk + c2 * (wk * wk))
                if k < LAYERS - 1:
                    strain = strain + c3 * float((w[k + 1] - w[k]) ** 2)
                twice = jnp.exp2(jnp.log(strain) * THIRD)
                q_ref[k, at] = twice
                r_ref[k, at] = dr + twice * (n0 + n1 * wk)
                if k > 0:
                    g_ref[k - 1, at] = 0.5 * (before + twice)
                before = twice

        at = slice(offset, offset + 8 * (len(which) + 1))
        up_d, up_e, up_t = None, q_ref[0, at], r_ref[0, at]
        down_d, down_e, down_t = None, q_ref[LAYERS - 1, at], r_ref[LAYERS - 1, at]
        product = None

        def step(d, e, t, g, q, r):
            d = e + (g if d is None else g * d)
            return d, q * d + g * e, r * d + g * t

        for k in range(LAYERS - 1):
            j = LAYERS - 2 - k
            g = g_ref[k, at]
            product = g if product is None else product * g
            up_d, up_e, up_t = step(up_d, up_e, up_t, g, q_ref[k + 1, at], r_ref[k + 1, at])
            down_d, down_e, down_t = step(
                down_d, down_e, down_t, g_ref[j, at], q_ref[j, at], r_ref[j, at]
            )
            if k % RESCALE == RESCALE - 1 and k < LAYERS - 2:
                shrink = 1.0 / up_d
                up_d, up_e, up_t, product = None, up_e * shrink, up_t * shrink, product * shrink
                shrink = 1.0 / down_d
                down_d, down_e, down_t = None, down_e * shrink, down_t * shrink
        shrink = 1.0 / up_e
        return down_d, down_e, down_t, up_t * shrink, product * shrink

    def finish(parts, friction, rate, ice, which):
        down_d, down_e, down_t, top, reach = parts
        base = squeeze(turn(friction * (0.5 / rate), -HALF, 0), which)
        mask = squeeze(turn(ice, -HALF, 0), which)
        basal = down_t / (down_e + base * down_d)
        surface = top - base * basal * reach
        return [spread(f * mask, len(which)) for f in (basal, surface)]

    for n in order:
        if DIRECTIONS[n][0] == 0:
            arrive(n)
    early = list(range(1, tiles - 1))
    late = [0, tiles - 1]
    field = field_reader(RIM, rows, in_map_lanes(rows))
    driving, rate = field(0, 0.0), field(1, 1.0)
    speed, drop = first_velocity(driving, rate, field(2, 0.0) * field(9, 0.0), field(8, 0.0))
    early_parts = eliminate(speed, drop, driving, rate, early, 0, HALF)
    for n in order:
        if DIRECTIONS[n][0] != 0:
            arrive(n)

    row_i = lax.broadcasted_iota(jnp.int32, (ext, 2 * lanes), 0)
    row_low = jnp.where(gx > 0, 0, RIM)
    row_high = jnp.where(gx < nx - 1, ext, RIM + rows)
    valid = jnp.logical_and(
        jnp.logical_and(row_i >= row_low, row_i < row_high), in_map_lanes(ext)
    )
    field = field_reader(0, ext, valid)
    driving = field(0, 0.0)
    rate = field(1, 1.0)
    friction = field(2, 0.0)
    melt = field(3, 0.0)
    trans = field(4, 0.0)
    leakage = field(5, 1.0)
    pressure = field(6, 0.0)
    scale = field(7, 0.0)
    ice = field(8, 0.0)
    grounded = field(9, 0.0)
    friction = friction * grounded
    scale = scale * grounded

    speed, drop = first_velocity(driving, rate, friction, ice)
    sliding = speed + drop * float(w[0])
    squared = sliding * sliding
    trans_eff = trans * (1.0 + squared / (1.0 + squared))
    source = melt + HEATING * friction * squared
    pressure = water_solve(pressure, trans_eff, leakage, source, valid)
    friction = scale * pressure

    late_parts = eliminate(speed, drop, driving, rate, late, 8 * (len(early) + 1), -HALF)
    pieces = [None] * tiles
    for parts, which in ((early_parts, early), (late_parts, late)):
        for n, piece in enumerate(zip(*finish(parts, friction, rate, ice, which))):
            pieces[which[n]] = piece
    blank = jnp.zeros((RIM, 2 * lanes), jnp.float32)
    basal = turn(jnp.concatenate([p[0] for p in pieces] + [blank], axis=0), HALF, 0)
    surface = jnp.concatenate([p[1][:, :lanes] for p in pieces], axis=0)
    sliding = jnp.where(valid, basal, 0.0)
    squared = sliding * sliding
    trans_eff = trans * (1.0 + squared / (1.0 + squared))
    source = melt + HEATING * friction * squared
    pressure = water_solve(pressure, trans_eff, leakage, source, valid)
    block = pressure[RIM : RIM + rows, :lanes]
    send_p[...] = block

    def last():
        return pltpu.make_async_remote_copy(
            src_ref=send_p, dst_ref=out.at[0, strip], send_sem=last_send, recv_sem=last_recv.at[strip],
            device_id={"sec": sectors}, device_id_type=MESH,
        )

    @pl.when(sends_last)
    def _():
        last().start()

    @pl.when(is_ice)
    def _():
        out[0, 0] = turn(surface, -HALF, 0)[:rows]
        out[0, 1] = sliding[RIM : RIM + rows, :lanes]
        out[0, 2] = scale[RIM : RIM + rows, :lanes] * block

    @pl.when(jnp.logical_not(is_ice))
    def _():
        out[0, 0] = block

    for n in order:
        dx, dy = DIRECTIONS[n]

        @pl.when(exists(dx, dy))
        def _(dx=dx, dy=dy, n=n):
            for c in copies(dx, dy, n):
                c.wait_send()

    @pl.when(sends_last)
    def _():
        last().wait_send()

    for s in range(1, sectors):

        @pl.when(jnp.logical_not(is_ice))
        def _(s=s):
            pltpu.make_async_remote_copy(
                src_ref=send_p, dst_ref=out.at[0, s], send_sem=last_send, recv_sem=last_recv.at[s],
                device_id={"sec": 0}, device_id_type=MESH,
            ).wait_recv()


def wide_map(nx, ny, *args):
    sectors, rows, lanes = args[0].shape
    ext = rows + 2 * RIM
    f32 = jnp.float32
    vmem = pltpu.VMEM
    dma = pltpu.SemaphoreType.DMA
    return pl.pallas_call(
        functools.partial(wide_kernel, sectors, nx, ny),
        out_shape=pltpu.VMEM((1, sectors, rows, lanes), f32),
        in_specs=[pl.BlockSpec(memory_space=pltpu.HBM)] * len(args),
        out_specs=pl.BlockSpec(memory_space=pltpu.VMEM),
        scratch_shapes=[
            vmem((8, ext, lanes), f32),
            vmem((2, ext, lanes), jnp.int32),
            vmem((rows, lanes), f32),
            vmem((rows, lanes), f32),
            vmem((ext, lanes), f32),
            vmem((ext, lanes), f32),
            vmem((LAYERS, ext + RIM, lanes), f32),
            vmem((LAYERS, ext + RIM, lanes), f32),
            vmem((LAYERS, ext + RIM, lanes), f32),
            vmem((rows, lanes), f32),
            dma((2,)),
            dma((10,)),
            dma((10,)),
            dma,
            dma((sectors,)),
        ],
        compiler_params=pltpu.CompilerParams(collective_id=0, has_side_effects=True),
    )(*args)


SHARE = 32.0 ** (-1.0 / 3.0)


def steady_drop(w):
    ratios = np.float32(4.0 * ((w[1:] - w[:-1]) / w[:-1]) ** 2)
    same = np.cumprod(ratios == ratios[0])
    return float(ratios[0]), int(same.sum())


ORDER = (0, 1, 2, 5, 6, 7, 8, 9, 3, 4)


def narrow_kernel(sectors, nx, *refs):
    ins = refs[:10]
    out = refs[10]
    own_f, own_i, part_f, part_i, halo_f, halo_i, q_ref, g_ref, r_ref, up_ref, send_p, results = refs[11:23]
    in_sem, main_send, edge_send, out_send, main_recv, halo_recv, out_recv, credit = refs[23:]
    rows, lanes = ins[0].shape[1:]
    sec = lax.axis_index("sec")
    gx = lax.axis_index("gx")
    gy = lax.axis_index("gy")
    partner = 1 - gy
    is_outer = gy == 1
    is_inner = gy == 0
    strip = lax.rem(sec, sectors)
    is_ice = sec < sectors
    is_water = jnp.logical_not(is_ice)
    sends_last = jnp.logical_and(sec > 0, is_ice)
    below, above = gx > 0, gx < nx - 1
    direct = sec > 0
    first_sector = sec == 0

    def both(p, q):
        return jnp.logical_and(p, q)

    def number(condition):
        return condition.astype(jnp.int32)

    def await_tiles(sem, count):
        room = q_ref.at[pl.ds(0, count), pl.ds(0, RIM), pl.ds(0, lanes)]
        pltpu.make_async_copy(room, room, sem).wait()

    def copy_in(n):
        dst = own_f.at[n] if n < 8 else own_i.at[n - 8]
        return pltpu.make_async_copy(ins[ORDER[n]].at[strip], dst, in_sem)

    def load():
        for n in range(10):
            copy_in(n).start()

    pl.when(is_outer)(load)
    barrier = pltpu.get_barrier_semaphore()

    def signal(condition, sem, target, role=True):
        @pl.when(jnp.logical_and(condition, role))
        def _():
            pl.semaphore_signal(sem, inc=1, device_id=target, device_id_type=MESH)

    signal(above, barrier, {"gx": gx + 1, "gy": 0}, is_outer)
    signal(above, barrier, {"gx": gx + 1, "gy": 1}, is_outer)
    signal(both(below, direct), barrier, {"gx": gx - 1, "gy": 1}, is_outer)
    signal(sec >= 0, barrier, {"gy": partner})
    signal(sends_last, barrier, {"sec": sectors, "gy": partner})
    signal(sends_last, barrier, {"sec": sectors})
    count = 1 + number(below) + number(both(both(above, direct), is_outer)) + jnp.where(is_ice, 0, 2 * (sectors - 1))
    pl.semaphore_wait(barrier, count)
    signal(both(below, first_sector), credit.at[0], {"gx": gx - 1, "gy": 1}, is_outer)
    signal(both(is_outer, direct), credit.at[0], {"gy": 0})

    def remote(src, dst, sent, landed, target):
        return pltpu.make_async_remote_copy(
            src_ref=src, dst_ref=dst, send_sem=sent, recv_sem=landed, device_id=target, device_id_type=MESH,
        )

    def main_copies():
        target = {"gy": partner}
        return [remote(own_f, part_f, main_send, main_recv, target), remote(own_i, part_i, main_send, main_recv, target)]

    def edge_copies():
        src = pl.ds(rows - RIM, RIM)
        target = {"gx": gx + 1, "gy": 1}
        first, rest = pl.ds(0, 3), pl.ds(3, 5)
        return [
            remote(own_f.at[first, src], halo_f.at[0, gy, first], edge_send, halo_recv.at[0, 0], target),
            remote(own_i.at[:, src], halo_i.at[0, gy], edge_send, halo_recv.at[0, 0], target),
            remote(own_f.at[rest, src], halo_f.at[0, gy, rest], edge_send, halo_recv.at[0, 1], target),
        ]

    def start(condition, copies):
        @pl.when(condition)
        def _():
            for c in copies:
                c.start()

    def await_credit(condition, which, amount):
        @pl.when(condition)
        def _():
            pl.semaphore_wait(credit.at[which], amount)

    @pl.when(below)
    def _():
        for n in (0, 1, 2, 8, 9, 3, 4, 5, 6, 7):
            src = ins[ORDER[n]].at[strip, pl.ds(0, RIM)]
            dst = halo_f.at[1, gy, n] if n < 8 else halo_i.at[1, gy, n - 8]
            part = int(3 <= n < 8)
            remote(src, dst, edge_send, halo_recv.at[1, part], {"gx": gx - 1, "gy": 1}).start()

    pl.when(is_inner)(load)

    @pl.when(is_inner)
    def _():
        for n in (0, 1, 2, 8, 9, 3, 4, 5, 6, 7):
            dst = part_f.at[n] if n < 8 else part_i.at[n - 8]
            remote(ins[ORDER[n]].at[strip], dst, main_send, main_recv, {"gy": 1}).start()

    for s in range(1, sectors):
        signal(is_water, credit.at[1], {"sec": s, "gy": partner})
        signal(is_water, credit.at[1], {"sec": s})
    await_tiles(in_sem, 10 * rows // RIM)
    start(is_outer, main_copies())
    await_credit(both(both(above, first_sector), is_outer), 0, 1)
    signal(both(is_outer, first_sector), credit.at[0], {"gy": 0})
    await_credit(is_inner, 0, 1)
    start(above, edge_copies())

    w = basal_response()
    steady, settled = steady_drop(w)
    wide = 2 * lanes
    lane = lax.broadcasted_iota(jnp.int32, (RIM, wide), 1)
    upper_sub = lax.broadcasted_iota(jnp.int32, (RIM, wide), 0) >= HALF
    last_lane = lane == wide - 1
    first_lane = lane == 0

    def join(parts):
        return jnp.concatenate(parts, axis=0)

    def tall_mask(mask, count):
        return join([mask] * count)

    def beside(f, i):
        return f[i] if i < 8 else f[i - 8].astype(jnp.float32)

    def fields(left, right, which=range(9)):
        def field(i):
            return jnp.concatenate([beside(left[i >= 8], i), beside(right[i >= 8], i)], axis=1)

        return {i: field(i) * field(9) if i in (2, 7) else field(i) for i in which}

    def halo_fields(side, exists, which):
        left, right = [(halo_f.at[side, r], halo_i.at[side, r]) for r in range(2)]
        return {
            i: jnp.where(exists, f, 1.0 if i in (1, 5) else 0.0) for i, f in fields(left, right, which).items()
        }

    def first_velocity(driving, rate, friction, ice):
        viscous = rate * float(FLOOR ** (-1.0 / 3.0))
        speed = driving / (4.0 * viscous)
        drop = -speed * friction / (viscous + friction * float(w[0]))
        return speed * ice, drop * ice

    def shifts(f):
        count = f.shape[0] // RIM
        yp = jnp.where(tall_mask(last_lane, count), 0.0, turn(f, -1, 1))
        ym = jnp.where(tall_mask(first_lane, count), 0.0, turn(f, 1, 1))
        return turn(f, -1, 0), turn(f, 1, 0), yp, ym

    def sheet(sliding, trans, melt, friction):
        squared = sliding * sliding
        return trans * (1.0 + squared / (1.0 + squared)), melt + HEATING * friction * squared

    def sweeper(trans_eff, leakage, source, valid, keep):
        here = keep(trans_eff)
        faces = [0.5 * (here + keep(t)) for t in shifts(trans_eff)]
        total = leakage + ((faces[0] + faces[1]) + (faces[2] + faces[3]))
        inverse = 1.0 / total if valid is None else jnp.where(valid, 1.0 / total, 0.0)
        weights = [f * inverse for f in faces]
        count = here.shape[0] // RIM
        weights[2] = jnp.where(tall_mask(last_lane, count), 0.0, weights[2])
        weights[3] = jnp.where(tall_mask(first_lane, count), 0.0, weights[3])
        base = source * inverse

        def sweep(pressure):
            parts = [w * keep(p) for w, p in zip(weights, neighbours(pressure))]
            return base + ((parts[0] + parts[1]) + (parts[2] + parts[3]))

        return sweep

    def water_steps(pressure, trans_eff, leakage, source):
        sweep = sweeper(trans_eff, leakage, source, None, lambda f: f)
        steps = [pressure]
        for _ in range(SWEEPS):
            steps.append(sweep(steps[-1]))
        return steps

    def split(f):
        return [f[RIM * k : RIM * k + RIM] for k in range(f.shape[0] // RIM)]

    def between(f, which):
        pieces = split(f)
        return join([jnp.where(upper_sub, pieces[k], pieces[k + 1]) for k in which])

    def restore(pieces):
        middle = [jnp.where(upper_sub, q, p) for p, q in zip(pieces[:-1], pieces[1:])]
        return join([pieces[0], *middle, pieces[-1]])

    def coefficients(speed, drop, driving, rate, which):
        s_shift = [between(f, which) for f in shifts(speed)]
        d_shift = [between(f, which) for f in shifts(drop)]
        drop, driving, rate = [between(f, which) for f in (drop, driving, rate)]
        sdx, sdy = s_shift[0] - s_shift[1], s_shift[2] - s_shift[3]
        ddx, ddy = d_shift[0] - d_shift[1], d_shift[2] - d_shift[3]
        c2, c3 = ddx * ddx + ddy * ddy, drop * drop
        return [
            (sdx * sdx + sdy * sdy) + 4.0 * FLOOR,
            sdx * ddx + sdy * ddy,
            c2,
            c3,
            c2 + steady * c3,
            (s_shift[0] + s_shift[1]) + (s_shift[2] + s_shift[3]),
            (d_shift[0] + d_shift[1]) + (d_shift[2] + d_shift[3]),
            driving * (2.0 * SHARE / rate),
        ]

    def viscosity(flat, offset):
        for n in range(flat[0].shape[0] // RIM):
            at = slice(offset + RIM * n, offset + RIM * n + RIM)
            c0, c1, c2, c3, c23, n0, n1, dr = [f[RIM * n : RIM * n + RIM] for f in flat]
            higher = None
            for k in reversed(range(LAYERS)):
                wk = float(w[k])
                if k < settled:
                    strain = c0 + (c1 * (2.0 * wk) + c23 * (wk * wk))
                else:
                    strain = c0 + (c1 * (2.0 * wk) + c2 * (wk * wk))
                    if k < LAYERS - 1:
                        strain = strain + c3 * float(4.0 * (w[k + 1] - w[k]) ** 2)
                now = jnp.exp2(jnp.log(strain) * THIRD)
                q_ref[k, at] = now
                r_ref[k, at] = dr + now * (n0 + n1 * wk)
                if k < LAYERS - 1:
                    g_ref[k, at] = 0.5 * (now + higher)
                higher = now

    def step(d, e, t, g, q, r):
        d = e + (g if d is None else g * d)
        return d, q * d + g * e, r * d + g * t

    def from_surface(at):
        d, e, t = None, q_ref[LAYERS - 1, at], r_ref[LAYERS - 1, at]
        for k in range(LAYERS - 1):
            j = LAYERS - 2 - k
            d, e, t = step(d, e, t, g_ref[j, at], q_ref[j, at], r_ref[j, at])
            if k % RESCALE == RESCALE - 1 and k < LAYERS - 2:
                shrink = 1.0 / d
                d, e, t = None, e * shrink, t * shrink
        return d, e, t

    def from_base(at):
        d, e, t, product = None, q_ref[0, at], r_ref[0, at], None
        for k in range(LAYERS - 1):
            g = g_ref[k, at]
            product = g if product is None else product * g
            d, e, t = step(d, e, t, g, q_ref[k + 1, at], r_ref[k + 1, at])
            if k % RESCALE == RESCALE - 1 and k < LAYERS - 2:
                shrink = 1.0 / d
                d, e, t, product = None, e * shrink, t * shrink, product * shrink
        shrink = 1.0 / e
        return t * shrink, product * shrink

    def result_copy(src, planes, where, target):
        return remote(src, out.at[0, planes, where], out_send, out_recv, target)

    inner_chunks = [(0, RIM, rows - 2 * RIM)]
    outer_chunks = [(0, 0, RIM), (RIM, rows - RIM, RIM)]

    def send_results(chunks, k, pressure, surface, sliding, scale):
        count = pressure.shape[0]
        at = pl.ds(0, count)
        send_p[0, at] = pressure[:, :lanes]
        send_p[1, at] = pressure[:, lanes:]
        mine, other = (slice(0, lanes), 1) if k == 0 else (slice(lanes, wide), 0)

        def started(copies):
            for c in copies:
                c.start()

        def pieces(src, planes, target):
            return [result_copy(src(pl.ds(a, n)), planes, pl.ds(b, n), target) for a, b, n in chunks]

        @pl.when(sends_last)
        def _():
            pl.semaphore_wait(credit.at[1], 2)
            for r in (other, 1 - other):
                started(pieces(lambda d, r=r: send_p.at[r, d], strip, {"sec": sectors, "gy": r}))

        @pl.when(is_water)
        def _():
            started(pieces(lambda d: send_p.at[other, d], 0, {"gy": partner}))
            for a, b, n in chunks:
                out[0, 0, b : b + n] = pressure[a : a + n, mine]

        @pl.when(is_ice)
        def _():
            theirs = slice(lanes, wide) if k == 0 else slice(0, lanes)
            for plane, f in enumerate((surface(), sliding, scale * pressure)):
                results[plane, at] = f[:, theirs]
                for a, b, n in chunks:
                    out[0, plane, b : b + n] = f[a : a + n, mine]
            started(pieces(lambda d: results.at[:, d], slice(None), {"gy": partner}))

    tiles = rows // RIM
    await_tiles(main_recv, 10 * tiles)

    def down_of(parts, base):
        d, e, t = parts
        return t / (e + base * d)

    @pl.when(is_inner)
    def _():
        driving, rate, friction, melt, trans, leakage, overburden, scale, ice = fields((own_f, own_i), (part_f, part_i)).values()
        which = range(tiles - 1)
        at = slice(0, rows - RIM)
        speed, drop = first_velocity(driving, rate, friction, ice)
        viscosity(coefficients(speed, drop, driving, rate, which), 0)
        trans_eff, source = sheet(speed + drop * float(w[0]), trans, melt, friction)
        pressure = water_steps(overburden, trans_eff, leakage, source)[-1]
        friction = scale * pressure
        base = between(friction * (0.5 * SHARE / rate), which)
        basal = down_of(from_surface(at), base)
        quarter = 0.25 * ice
        sliding = restore(split(basal)) * quarter
        trans_eff, source = sheet(sliding, trans, melt, friction)
        pressure = water_steps(pressure, trans_eff, leakage, source)[-1]
        mine = slice(RIM, rows - RIM)

        def surface():
            top, reach = from_base(at)
            return (restore(split(top - base * basal * reach)) * quarter)[mine]

        send_results(inner_chunks, 0, pressure[mine], surface, sliding[mine], scale[mine])

    @pl.when(is_outer)
    def _():
        middle = fields((part_f, part_i), (own_f, own_i))
        driving, rate, friction, melt, trans, leakage, overburden, scale, ice = middle.values()
        m_speed, m_drop = first_velocity(driving, rate, friction, ice)
        which = (0, tiles - 2)
        early = slice(0, 2 * RIM)
        viscosity(coefficients(m_speed, m_drop, driving, rate, which), 0)
        early_down = from_surface(early)
        top, reach = from_base(early)
        m_first = sheet(m_speed + m_drop * float(w[0]), trans, melt, friction)
        steps_1 = water_steps(overburden, m_first[0], leakage, m_first[1])
        m_friction = scale * steps_1[-1]
        base = between(m_friction * (0.5 * SHARE / rate), which)
        basal = down_of(early_down, base)
        early_basal = split(basal)
        early_surface = split(top - base * basal * reach)
        blank = [jnp.zeros((RIM, wide), jnp.float32)] * (tiles - 3)
        m_second = sheet(
            restore([early_basal[0], *blank, early_basal[1]]) * (0.25 * ice), trans, melt, m_friction
        )
        steps_2 = water_steps(steps_1[-1], m_second[0], leakage, m_second[1])

        halo_sides = ((0, below), (1, above))

        def await_halo(side, exists, part):
            pl.when(exists)(functools.partial(await_tiles, halo_recv.at[side, part], 10))

        def frame(a, f, b):
            return join([a, f, b])

        def ends(f):
            return join([f[: 2 * RIM], f[rows:]])

        def inside(e, f):
            return join([e[: 2 * RIM], f[RIM : rows - RIM], e[2 * RIM :]])

        def end_frame(i):
            return join([low[i], middle[i][:RIM], middle[i][rows - RIM :], high[i]])

        ends_in, end_velocity, late_down = [], [], []
        for side, exists in halo_sides:
            await_halo(side, exists, 0)
            h = halo_fields(side, exists, (0, 1, 2, 8))
            velocity = first_velocity(h[0], h[1], h[2], h[8])
            inner = slice(0, RIM) if side == 0 else slice(rows - RIM, rows)
            pairs = [(velocity[0], m_speed), (velocity[1], m_drop), (h[0], middle[0]), (h[1], middle[1])]
            viscosity(
                coefficients(*[join([a, f[inner]] if side == 0 else [f[inner], a]) for a, f in pairs], (0,)), (2 + side) * RIM
            )
            tile = slice((2 + side) * RIM, (3 + side) * RIM)
            if side == 0:
                late_down.append(from_surface(tile))
            ends_in.append(h)
            end_velocity.append(velocity)
            if side == 0:

                @pl.when(jnp.logical_not(below))
                def _():
                    up_ref[0], up_ref[1] = from_base(tile)

        low, high = ends_in
        low_velocity, high_velocity = end_velocity
        for side, exists in halo_sides:
            await_halo(side, exists, 1)
        late_down.append(from_surface(slice(3 * RIM, 4 * RIM)))
        late_down = [join(p) for p in zip(*late_down)]
        high_up = from_base(slice(3 * RIM, 4 * RIM))
        low |= halo_fields(0, below, (3, 4, 5, 6, 7))
        high |= halo_fields(1, above, (3, 4, 5, 6, 7))
        end_sheets = [
            sheet(s + d * float(w[0]), f[4], f[3], f[2])
            for f, (s, d) in ((low, low_velocity), (high, high_velocity))
        ]
        rate, melt, trans, leakage, overburden, scale, ice = [end_frame(i) for i in (1, 3, 4, 5, 6, 7, 8)]
        quarter = 0.25 * ice
        valid = join([
            jnp.broadcast_to(below, (RIM, wide)), jnp.ones((2 * RIM, wide), jnp.bool_), jnp.broadcast_to(above, (RIM, wide))
        ])
        trans_eff, source = [frame(*f) for f in zip(end_sheets[0], m_first, end_sheets[1])]
        sweep = sweeper(trans_eff, leakage, ends(source), valid, ends)
        pressure = overburden
        for step_1 in steps_1[:-1]:
            pressure = sweep(inside(pressure, step_1))
        friction = scale * pressure
        base = between(friction * (0.5 * SHARE / rate), (0, 2))
        basal = down_of(late_down, base)

        def arrange(early_pieces, late_pieces):
            first, last = late_pieces
            before, after = early_pieces
            return join([first, jnp.where(upper_sub, before, first), jnp.where(upper_sub, last, after), last]) * quarter

        sliding = arrange(early_basal, split(basal))
        trans_eff, source = sheet(sliding, trans, melt, friction)
        sweep = sweeper(inside(trans_eff, m_second[0]), leakage, source, valid, ends)
        for step_2 in steps_2[:-1]:
            pressure = sweep(inside(pressure, step_2))

        mine = slice(RIM, 3 * RIM)

        def surface():
            @pl.when(below)
            def _():
                up_ref[0], up_ref[1] = from_base(slice(2 * RIM, 3 * RIM))

            top, reach = [join([up_ref[n], f]) for n, f in enumerate(high_up)]
            return arrange(early_surface, split(top - base * basal * reach))[mine]

        send_results(outer_chunks, 1, pressure[mine], surface, sliding[mine], scale[mine])

    await_tiles(main_send, 10 * tiles)
    pl.when(both(below, above))(functools.partial(await_tiles, edge_send, 20))
    pl.when(below != above)(functools.partial(await_tiles, edge_send, 10))
    counts = (tiles - 2, 2)
    for role, mine, theirs in ((is_inner, *counts), (is_outer, *counts[::-1])):
        pl.when(both(sends_last, role))(functools.partial(await_tiles, out_send, 5 * mine))
        pl.when(both(first_sector, role))(functools.partial(await_tiles, out_send, 3 * mine))
        pl.when(both(is_water, role))(functools.partial(await_tiles, out_send, mine))
        pl.when(both(is_ice, role))(functools.partial(await_tiles, out_recv, 3 * theirs))
        pl.when(both(is_water, role))(functools.partial(await_tiles, out_recv, theirs + (sectors - 1) * tiles))


def narrow_map(nx, *args):
    sectors, rows, lanes = args[0].shape
    most = max(rows - 2 * RIM, 2 * RIM)
    f32 = jnp.float32
    vmem = pltpu.VMEM
    dma = pltpu.SemaphoreType.DMA
    return pl.pallas_call(
        functools.partial(narrow_kernel, sectors, nx),
        out_shape=pltpu.VMEM((1, sectors, rows, lanes), f32),
        in_specs=[pl.BlockSpec(memory_space=pltpu.HBM)] * len(args),
        out_specs=pl.BlockSpec(memory_space=pltpu.VMEM),
        scratch_shapes=[
            vmem((8, rows, lanes), f32),
            vmem((2, rows, lanes), jnp.int32),
            vmem((8, rows, lanes), f32),
            vmem((2, rows, lanes), jnp.int32),
            vmem((2, 2, 8, RIM, lanes), f32),
            vmem((2, 2, 2, RIM, lanes), jnp.int32),
            vmem((LAYERS, max(rows, 4 * RIM), 2 * lanes), f32),
            vmem((LAYERS, max(rows, 4 * RIM), 2 * lanes), f32),
            vmem((LAYERS, max(rows, 4 * RIM), 2 * lanes), f32),
            vmem((2, RIM, 2 * lanes), f32),
            vmem((2, most, lanes), f32),
            vmem((3, most, lanes), f32),
            dma,
            dma,
            dma,
            dma,
            dma,
            dma((2, 2)),
            dma,
            pltpu.SemaphoreType.REGULAR((2,)),
        ],
        compiler_params=pltpu.CompilerParams(collective_id=0, has_side_effects=True),
    )(*args)


def solution(mesh):
    spec = P(None, "gx", "gy")
    nx, ny = mesh.shape["gx"], mesh.shape["gy"]
    on_device = functools.partial(narrow_map, nx) if ny == 2 else functools.partial(wide_map, nx, ny)
    return jax.shard_map(
        on_device,
        mesh=mesh,
        in_specs=(spec,) * 10,
        out_specs=P("sec", None, "gx", "gy"),
        check_vma=False,
    )
```

```python
import functools

import jax
import jax.numpy as jnp
import numpy as np
from jax import lax
from jax.experimental import pallas as pl
from jax.experimental.pallas import tpu as pltpu
from jax.sharding import PartitionSpec as P

LAYERS = 40
SWEEPS = 4
VERT = 4.0
FLOOR = 0.25
HEATING = 0.5

RIM = 8
HALF = RIM // 2
RESCALE = 10
THIRD = -1.0 / (3.0 * float(np.log(2.0)))
DIRECTIONS = [(dx, dy) for dx in (-1, 0, 1) for dy in (-1, 0, 1) if (dx, dy) != (0, 0)]
MESH = pl.DeviceIdType.MESH


def basal_response():
    matrix = np.zeros((LAYERS, LAYERS))
    for k in range(LAYERS):
        matrix[k, k] = 4.0 + (VERT if k > 0 else 0.0) + (VERT if k < LAYERS - 1 else 0.0)
        if k > 0:
            matrix[k, k - 1] = matrix[k - 1, k] = -VERT
    unit = np.zeros(LAYERS)
    unit[0] = 1.0
    return np.linalg.solve(matrix, unit)


def turn(values, shift, axis):
    return pltpu.roll(values, shift % values.shape[axis], axis)


def neighbours(f):
    return turn(f, -1, 0), turn(f, 1, 0), turn(f, -1, 1), turn(f, 1, 1)


def water_solve(pressure, trans_eff, leakage, source, valid):
    faces = [0.5 * (trans_eff + t) for t in neighbours(trans_eff)]
    total = leakage + ((faces[0] + faces[1]) + (faces[2] + faces[3]))
    inverse = jnp.where(valid, 1.0 / total, 0.0)
    weights = [f * inverse for f in faces]
    base = source * inverse
    for _ in range(SWEEPS):
        parts = [w * p for w, p in zip(weights, neighbours(pressure))]
        pressure = base + ((parts[0] + parts[1]) + (parts[2] + parts[3]))
    return pressure


def wide_kernel(sectors, nx, ny, *refs):
    ins = refs[:10]
    out = refs[10]
    floats, ints, pack_l, pack_r, rim_l, rim_r, q_ref, g_ref, r_ref, send_p = refs[11:21]
    in_sem, send_sem, recv_sem, last_send, last_recv = refs[21:]
    rows, lanes = ins[0].shape[1:]
    sec = lax.axis_index("sec")
    gx = lax.axis_index("gx")
    gy = lax.axis_index("gy")
    strip = lax.rem(sec, sectors)
    is_ice = sec < sectors
    sends_last = jnp.logical_and(sec > 0, is_ice)

    def exists(dx, dy):
        x, y = gx + dx, gy + dy
        return jnp.logical_and(
            jnp.logical_and(x >= 0, x < nx), jnp.logical_and(y >= 0, y < ny)
        )

    float_ids = (0, 1, 2, 5, 6, 7, 8, 9)
    int_ids = (3, 4)
    loads = []
    for slot, arg in enumerate(float_ids):
        loads.append(pltpu.make_async_copy(ins[arg].at[strip], floats.at[slot, pl.ds(RIM, rows)], in_sem.at[0]))
    for slot, arg in enumerate(int_ids):
        loads.append(pltpu.make_async_copy(ins[arg].at[strip], ints.at[slot, pl.ds(RIM, rows)], in_sem.at[1]))
    barrier = pltpu.get_barrier_semaphore()
    count = jnp.int32(0)
    for dx, dy in sorted(DIRECTIONS, key=lambda d: -abs(d[0])):
        here = exists(dx, dy)
        count = count + here.astype(jnp.int32)

        @pl.when(here)
        def _(dx=dx, dy=dy):
            pl.semaphore_signal(barrier, inc=1, device_id={"gx": gx + dx, "gy": gy + dy}, device_id_type=MESH)

    count = count + sends_last.astype(jnp.int32)
    count = count + jnp.where(is_ice, 0, sectors - 1)

    @pl.when(sends_last)
    def _():
        pl.semaphore_signal(barrier, inc=1, device_id={"sec": sectors}, device_id_type=MESH)

    for s in range(1, sectors):

        @pl.when(jnp.logical_not(is_ice))
        def _(s=s):
            pl.semaphore_signal(barrier, inc=1, device_id={"sec": s}, device_id_type=MESH)

    for load in loads:
        load.start()
    for slot, buffer in enumerate((floats, ints)):
        mine = buffer.at[:, pl.ds(RIM, rows)]
        pltpu.make_async_copy(mine, mine, in_sem.at[slot]).wait()

    lane = lax.broadcasted_iota(jnp.int32, (rows, lanes), 1)
    fields = [floats[i, RIM : RIM + rows] for i in range(8)]
    fields += [ints[i, RIM : RIM + rows].astype(jnp.float32) for i in range(2)]
    left = jnp.zeros((rows, lanes), jnp.float32)
    right = jnp.zeros((rows, lanes), jnp.float32)
    for i, f in enumerate(fields):
        moved = turn(f, RIM * i, 1)
        group = lane // RIM
        left = jnp.where(group == i, moved, left)
        right = jnp.where(group == (i - 1) % (lanes // RIM), moved, right)
    pack_l[...] = left
    pack_r[...] = right

    pl.semaphore_wait(barrier, count)

    def copies(dx, dy, n):
        target = {"gx": gx + dx, "gy": gy + dy}

        def remote(src, dst, m):
            return pltpu.make_async_remote_copy(
                src_ref=src, dst_ref=dst, send_sem=send_sem.at[m], recv_sem=recv_sem.at[m],
                device_id=target, device_id_type=MESH,
            )

        if dy == 0:
            first = rows if dx > 0 else RIM
            landing = 0 if dx > 0 else RIM + rows
            return [
                remote(floats.at[:, pl.ds(first, RIM)], floats.at[:, pl.ds(landing, RIM)], n),
                remote(ints.at[:, pl.ds(first, RIM)], ints.at[:, pl.ds(landing, RIM)], 8 + (dx > 0)),
            ]
        src, dst = (pack_r, rim_l) if dy > 0 else (pack_l, rim_r)
        if dx == 0:
            return [remote(src, dst.at[pl.ds(RIM, rows)], n)]
        first = rows - RIM if dx > 0 else 0
        landing = 0 if dx > 0 else RIM + rows
        return [remote(src.at[pl.ds(first, RIM)], dst.at[pl.ds(landing, RIM)], n)]

    order = sorted(range(8), key=lambda n: abs(DIRECTIONS[n][1]))
    for n in order:
        dx, dy = DIRECTIONS[n]

        @pl.when(exists(dx, dy))
        def _(dx=dx, dy=dy, n=n):
            for c in copies(dx, dy, n):
                c.start()

    def arrive(n):
        dx, dy = DIRECTIONS[n]

        @pl.when(exists(-dx, -dy))
        def _():
            for c in copies(dx, dy, n):
                c.wait_recv()

    w = basal_response()
    ext = rows + 2 * RIM
    tall = rows + RIM
    tiles = tall // 8
    wide = 2 * RIM
    slot = lax.broadcasted_iota(jnp.int32, (8, lanes), 1) // wide
    lane_low = jnp.where(gy < ny - 1, lanes + RIM, lanes)
    lane_high = jnp.where(gy > 0, 2 * lanes - RIM, 2 * lanes)

    def in_map_lanes(height):
        lane_i = lax.broadcasted_iota(jnp.int32, (height, 2 * lanes), 1)
        return jnp.logical_or(lane_i < lane_low, lane_i >= lane_high)

    def field_reader(top, height, valid):
        at = slice(top, top + height)
        packed_l, packed_r = rim_l[at], rim_r[at]
        group = lax.broadcasted_iota(jnp.int32, (height, lanes), 1) // RIM

        def field(i, fill):
            main = floats[i, at] if i < 8 else ints[i - 8, at].astype(jnp.float32)
            rim = turn(jnp.where(group == i, packed_r, packed_l), -RIM * i, 1)
            return jnp.where(valid, jnp.concatenate([main, rim], axis=1), fill)

        return field

    def first_velocity(driving, rate, friction, ice):
        viscous = rate * float(FLOOR ** (-1.0 / 3.0))
        speed = driving / (4.0 * viscous)
        drop = -speed * friction / (viscous + friction * float(w[0]))
        return speed * ice, drop * ice

    def squeeze(f, which):
        tile = jnp.zeros((8, lanes), jnp.float32)
        for n, t in enumerate(which):
            moved = turn(f[8 * t : 8 * t + 8, lanes:], wide * n + RIM, 1)
            tile = jnp.where(slot == n, moved, tile)
        return jnp.concatenate([f[8 * t : 8 * t + 8, :lanes] for t in which] + [tile], axis=0)

    def spread(f, count):
        last = f[8 * count :]
        return [
            jnp.concatenate([f[8 * n : 8 * n + 8], turn(last, -(wide * n + RIM), 1)], axis=1)
            for n in range(count)
        ]

    def eliminate(speed, drop, driving, rate, which, offset, lead):
        sxp, sxm, syp, sym = neighbours(speed)
        dxp, dxm, dyp, dym = neighbours(drop)
        sdx, sdy, ddx, ddy = sxp - sxm, syp - sym, dxp - dxm, dyp - dym
        flat = [
            0.03125 * (sdx * sdx + sdy * sdy) + 0.125 * FLOOR,
            0.0625 * (sdx * ddx + sdy * ddy),
            0.03125 * (ddx * ddx + ddy * ddy),
            0.125 * drop * drop,
            0.25 * ((sxp + sxm) + (syp + sym)),
            0.25 * ((dxp + dxm) + (dyp + dym)),
            driving * (0.5 / rate),
        ]
        flat = [squeeze(turn(f, lead, 0), which) for f in flat]
        for n in range(len(which) + 1):
            at = slice(offset + 8 * n, offset + 8 * n + 8)
            c0, c1, c2, c3, n0, n1, dr = [f[8 * n : 8 * n + 8] for f in flat]
            before = None
            for k in range(LAYERS):
                wk = float(w[k])
                strain = c0 + (c1 * wk + c2 * (wk * wk))
                if k < LAYERS - 1:
                    strain = strain + c3 * float((w[k + 1] - w[k]) ** 2)
                twice = jnp.exp2(jnp.log(strain) * THIRD)
                q_ref[k, at] = twice
                r_ref[k, at] = dr + twice * (n0 + n1 * wk)
                if k > 0:
                    g_ref[k - 1, at] = 0.5 * (before + twice)
                before = twice

        at = slice(offset, offset + 8 * (len(which) + 1))
        up_d, up_e, up_t = None, q_ref[0, at], r_ref[0, at]
        down_d, down_e, down_t = None, q_ref[LAYERS - 1, at], r_ref[LAYERS - 1, at]
        product = None

        def step(d, e, t, g, q, r):
            d = e + (g if d is None else g * d)
            return d, q * d + g * e, r * d + g * t

        for k in range(LAYERS - 1):
            j = LAYERS - 2 - k
            g = g_ref[k, at]
            product = g if product is None else product * g
            up_d, up_e, up_t = step(up_d, up_e, up_t, g, q_ref[k + 1, at], r_ref[k + 1, at])
            down_d, down_e, down_t = step(
                down_d, down_e, down_t, g_ref[j, at], q_ref[j, at], r_ref[j, at]
            )
            if k % RESCALE == RESCALE - 1 and k < LAYERS - 2:
                shrink = 1.0 / up_d
                up_d, up_e, up_t, product = None, up_e * shrink, up_t * shrink, product * shrink
                shrink = 1.0 / down_d
                down_d, down_e, down_t = None, down_e * shrink, down_t * shrink
        shrink = 1.0 / up_e
        return down_d, down_e, down_t, up_t * shrink, product * shrink

    def finish(parts, friction, rate, ice, which):
        down_d, down_e, down_t, top, reach = parts
        base = squeeze(turn(friction * (0.5 / rate), -HALF, 0), which)
        mask = squeeze(turn(ice, -HALF, 0), which)
        basal = down_t / (down_e + base * down_d)
        surface = top - base * basal * reach
        return [spread(f * mask, len(which)) for f in (basal, surface)]

    for n in order:
        if DIRECTIONS[n][0] == 0:
            arrive(n)
    early = list(range(1, tiles - 1))
    late = [0, tiles - 1]
    field = field_reader(RIM, rows, in_map_lanes(rows))
    driving, rate = field(0, 0.0), field(1, 1.0)
    speed, drop = first_velocity(driving, rate, field(2, 0.0) * field(9, 0.0), field(8, 0.0))
    early_parts = eliminate(speed, drop, driving, rate, early, 0, HALF)
    for n in order:
        if DIRECTIONS[n][0] != 0:
            arrive(n)

    row_i = lax.broadcasted_iota(jnp.int32, (ext, 2 * lanes), 0)
    row_low = jnp.where(gx > 0, 0, RIM)
    row_high = jnp.where(gx < nx - 1, ext, RIM + rows)
    valid = jnp.logical_and(
        jnp.logical_and(row_i >= row_low, row_i < row_high), in_map_lanes(ext)
    )
    field = field_reader(0, ext, valid)
    driving = field(0, 0.0)
    rate = field(1, 1.0)
    friction = field(2, 0.0)
    melt = field(3, 0.0)
    trans = field(4, 0.0)
    leakage = field(5, 1.0)
    pressure = field(6, 0.0)
    scale = field(7, 0.0)
    ice = field(8, 0.0)
    grounded = field(9, 0.0)
    friction = friction * grounded
    scale = scale * grounded

    speed, drop = first_velocity(driving, rate, friction, ice)
    sliding = speed + drop * float(w[0])
    squared = sliding * sliding
    trans_eff = trans * (1.0 + squared / (1.0 + squared))
    source = melt + HEATING * friction * squared
    pressure = water_solve(pressure, trans_eff, leakage, source, valid)
    friction = scale * pressure

    late_parts = eliminate(speed, drop, driving, rate, late, 8 * (len(early) + 1), -HALF)
    pieces = [None] * tiles
    for parts, which in ((early_parts, early), (late_parts, late)):
        for n, piece in enumerate(zip(*finish(parts, friction, rate, ice, which))):
            pieces[which[n]] = piece
    blank = jnp.zeros((RIM, 2 * lanes), jnp.float32)
    basal = turn(jnp.concatenate([p[0] for p in pieces] + [blank], axis=0), HALF, 0)
    surface = jnp.concatenate([p[1][:, :lanes] for p in pieces], axis=0)
    sliding = jnp.where(valid, basal, 0.0)
    squared = sliding * sliding
    trans_eff = trans * (1.0 + squared / (1.0 + squared))
    source = melt + HEATING * friction * squared
    pressure = water_solve(pressure, trans_eff, leakage, source, valid)
    block = pressure[RIM : RIM + rows, :lanes]
    send_p[...] = block

    def last():
        return pltpu.make_async_remote_copy(
            src_ref=send_p, dst_ref=out.at[0, strip], send_sem=last_send, recv_sem=last_recv.at[strip],
            device_id={"sec": sectors}, device_id_type=MESH,
        )

    @pl.when(sends_last)
    def _():
        last().start()

    @pl.when(is_ice)
    def _():
        out[0, 0] = turn(surface, -HALF, 0)[:rows]
        out[0, 1] = sliding[RIM : RIM + rows, :lanes]
        out[0, 2] = scale[RIM : RIM + rows, :lanes] * block

    @pl.when(jnp.logical_not(is_ice))
    def _():
        out[0, 0] = block

    for n in order:
        dx, dy = DIRECTIONS[n]

        @pl.when(exists(dx, dy))
        def _(dx=dx, dy=dy, n=n):
            for c in copies(dx, dy, n):
                c.wait_send()

    @pl.when(sends_last)
    def _():
        last().wait_send()

    for s in range(1, sectors):

        @pl.when(jnp.logical_not(is_ice))
        def _(s=s):
            pltpu.make_async_remote_copy(
                src_ref=send_p, dst_ref=out.at[0, s], send_sem=last_send, recv_sem=last_recv.at[s],
                device_id={"sec": 0}, device_id_type=MESH,
            ).wait_recv()


def wide_map(nx, ny, *args):
    sectors, rows, lanes = args[0].shape
    ext = rows + 2 * RIM
    f32 = jnp.float32
    vmem = pltpu.VMEM
    dma = pltpu.SemaphoreType.DMA
    return pl.pallas_call(
        functools.partial(wide_kernel, sectors, nx, ny),
        out_shape=pltpu.VMEM((1, sectors, rows, lanes), f32),
        in_specs=[pl.BlockSpec(memory_space=pltpu.HBM)] * len(args),
        out_specs=pl.BlockSpec(memory_space=pltpu.VMEM),
        scratch_shapes=[
            vmem((8, ext, lanes), f32),
            vmem((2, ext, lanes), jnp.int32),
            vmem((rows, lanes), f32),
            vmem((rows, lanes), f32),
            vmem((ext, lanes), f32),
            vmem((ext, lanes), f32),
            vmem((LAYERS, ext + RIM, lanes), f32),
            vmem((LAYERS, ext + RIM, lanes), f32),
            vmem((LAYERS, ext + RIM, lanes), f32),
            vmem((rows, lanes), f32),
            dma((2,)),
            dma((10,)),
            dma((10,)),
            dma,
            dma((sectors,)),
        ],
        compiler_params=pltpu.CompilerParams(collective_id=0, has_side_effects=True),
    )(*args)


SHARE = 32.0 ** (-1.0 / 3.0)


def steady_drop(w):
    ratios = np.float32(4.0 * ((w[1:] - w[:-1]) / w[:-1]) ** 2)
    same = np.cumprod(ratios == ratios[0])
    return float(ratios[0]), int(same.sum())


ORDER = (0, 1, 2, 5, 6, 7, 8, 9, 3, 4)


def narrow_kernel(sectors, nx, *refs):
    ins = refs[:10]
    out = refs[10]
    own_f, own_i, part_f, part_i, halo_f, halo_i, q_ref, g_ref, r_ref, up_ref, send_p, results = refs[11:23]
    in_sem, main_send, edge_send, out_send, main_recv, halo_recv, out_recv, credit = refs[23:]
    rows, lanes = ins[0].shape[1:]
    sec = lax.axis_index("sec")
    gx = lax.axis_index("gx")
    gy = lax.axis_index("gy")
    partner = 1 - gy
    is_outer = gy == 1
    is_inner = gy == 0
    strip = lax.rem(sec, sectors)
    is_ice = sec < sectors
    is_water = jnp.logical_not(is_ice)
    sends_last = jnp.logical_and(sec > 0, is_ice)
    below, above = gx > 0, gx < nx - 1
    first_sector = sec == 0

    def both(p, q):
        return jnp.logical_and(p, q)

    def number(condition):
        return condition.astype(jnp.int32)

    def await_tiles(sem, count):
        room = q_ref.at[pl.ds(0, count), pl.ds(0, RIM), pl.ds(0, lanes)]
        pltpu.make_async_copy(room, room, sem).wait()

    def copy_in(n):
        dst = own_f.at[n] if n < 8 else own_i.at[n - 8]
        return pltpu.make_async_copy(ins[ORDER[n]].at[strip], dst, in_sem)

    def load():
        for n in range(10):
            copy_in(n).start()

    pl.when(is_outer)(load)
    barrier = pltpu.get_barrier_semaphore()

    def signal(condition, sem, target, role=True):
        @pl.when(jnp.logical_and(condition, role))
        def _():
            pl.semaphore_signal(sem, inc=1, device_id=target, device_id_type=MESH)

    signal(above, barrier, {"gx": gx + 1, "gy": 0}, is_outer)
    signal(above, barrier, {"gx": gx + 1, "gy": 1}, is_outer)
    signal(is_outer, barrier, {"gy": 0})
    signal(sends_last, barrier, {"sec": sectors, "gy": partner})
    signal(sends_last, barrier, {"sec": sectors})
    count = number(is_inner) + number(below) + jnp.where(is_ice, 0, 2 * (sectors - 1))

    @pl.when(count > 0)
    def _():
        pl.semaphore_wait(barrier, count)

    signal(below, credit.at[0], {"gx": gx - 1, "gy": 1}, is_outer)
    signal(is_inner, credit.at[2], {"gy": 1})

    def remote(src, dst, sent, landed, target):
        return pltpu.make_async_remote_copy(
            src_ref=src, dst_ref=dst, send_sem=sent, recv_sem=landed, device_id=target, device_id_type=MESH,
        )

    def main_copies():
        target = {"gy": partner}
        return [remote(own_f, part_f, main_send, main_recv, target), remote(own_i, part_i, main_send, main_recv, target)]

    def edge_copies():
        src = pl.ds(rows - RIM, RIM)
        target = {"gx": gx + 1, "gy": 1}
        first, rest = pl.ds(0, 3), pl.ds(3, 5)
        return [
            remote(own_f.at[first, src], halo_f.at[0, gy, first], edge_send, halo_recv.at[0, 0], target),
            remote(own_i.at[:, src], halo_i.at[0, gy], edge_send, halo_recv.at[0, 0], target),
            remote(own_f.at[rest, src], halo_f.at[0, gy, rest], edge_send, halo_recv.at[0, 1], target),
        ]

    def start(condition, copies):
        @pl.when(condition)
        def _():
            for c in copies:
                c.start()

    def await_credit(condition, which, amount):
        @pl.when(condition)
        def _():
            pl.semaphore_wait(credit.at[which], amount)

    @pl.when(below)
    def _():
        for n in (0, 1, 2, 8, 9, 3, 4, 5, 6, 7):
            src = ins[ORDER[n]].at[strip, pl.ds(0, RIM)]
            dst = halo_f.at[1, gy, n] if n < 8 else halo_i.at[1, gy, n - 8]
            part = int(3 <= n < 8)
            remote(src, dst, edge_send, halo_recv.at[1, part], {"gx": gx - 1, "gy": 1}).start()

    pl.when(is_inner)(load)

    @pl.when(is_inner)
    def _():
        for n in (0, 1, 2, 8, 9, 3, 4, 5, 6, 7):
            dst = part_f.at[n] if n < 8 else part_i.at[n - 8]
            remote(ins[ORDER[n]].at[strip], dst, main_send, main_recv, {"gy": 1}).start()

    for s in range(1, sectors):
        signal(is_water, credit.at[1], {"sec": s, "gy": partner})
        signal(is_water, credit.at[1], {"sec": s})
    await_tiles(in_sem, 10 * rows // RIM)
    await_credit(is_outer, 2, 1)
    start(is_outer, main_copies())

    def send_upwards():
        await_credit(both(above, is_outer), 0, 1)
        signal(is_outer, credit.at[0], {"gy": 0})
        await_credit(is_inner, 0, 1)
        start(above, edge_copies())

    starts_first = both(first_sector, gx == 0)
    pl.when(jnp.logical_not(starts_first))(send_upwards)


    w = basal_response()
    steady, settled = steady_drop(w)
    wide = 2 * lanes
    lane = lax.broadcasted_iota(jnp.int32, (RIM, wide), 1)
    upper_sub = lax.broadcasted_iota(jnp.int32, (RIM, wide), 0) >= HALF
    last_lane = lane == wide - 1
    first_lane = lane == 0

    def join(parts):
        return jnp.concatenate(parts, axis=0)

    def tall_mask(mask, count):
        return join([mask] * count)

    def beside(f, i):
        return f[i] if i < 8 else f[i - 8].astype(jnp.float32)

    def fields(left, right, which=range(9)):
        def field(i):
            return jnp.concatenate([beside(left[i >= 8], i), beside(right[i >= 8], i)], axis=1)

        return {i: field(i) * field(9) if i in (2, 7) else field(i) for i in which}

    def halo_fields(side, exists, which):
        left, right = [(halo_f.at[side, r], halo_i.at[side, r]) for r in range(2)]
        return {
            i: jnp.where(exists, f, 1.0 if i in (1, 5) else 0.0) for i, f in fields(left, right, which).items()
        }

    def first_velocity(driving, rate, friction, ice):
        viscous = rate * float(FLOOR ** (-1.0 / 3.0))
        speed = driving / (4.0 * viscous)
        drop = -speed * friction / (viscous + friction * float(w[0]))
        return speed * ice, drop * ice

    def shifts(f):
        count = f.shape[0] // RIM
        yp = jnp.where(tall_mask(last_lane, count), 0.0, turn(f, -1, 1))
        ym = jnp.where(tall_mask(first_lane, count), 0.0, turn(f, 1, 1))
        return turn(f, -1, 0), turn(f, 1, 0), yp, ym

    def sheet(sliding, trans, melt, friction):
        squared = sliding * sliding
        return trans * (1.0 + squared / (1.0 + squared)), melt + HEATING * friction * squared

    def sweeper(trans_eff, leakage, source, valid, keep):
        here = keep(trans_eff)
        faces = [0.5 * (here + keep(t)) for t in shifts(trans_eff)]
        total = leakage + ((faces[0] + faces[1]) + (faces[2] + faces[3]))
        inverse = 1.0 / total if valid is None else jnp.where(valid, 1.0 / total, 0.0)
        weights = [f * inverse for f in faces]
        count = here.shape[0] // RIM
        weights[2] = jnp.where(tall_mask(last_lane, count), 0.0, weights[2])
        weights[3] = jnp.where(tall_mask(first_lane, count), 0.0, weights[3])
        base = source * inverse

        def sweep(pressure):
            parts = [w * keep(p) for w, p in zip(weights, neighbours(pressure))]
            return base + ((parts[0] + parts[1]) + (parts[2] + parts[3]))

        return sweep

    def water_steps(pressure, trans_eff, leakage, source):
        sweep = sweeper(trans_eff, leakage, source, None, lambda f: f)
        steps = [pressure]
        for _ in range(SWEEPS):
            steps.append(sweep(steps[-1]))
        return steps

    def split(f):
        return [f[RIM * k : RIM * k + RIM] for k in range(f.shape[0] // RIM)]

    def between(f, which):
        pieces = split(f)
        return join([jnp.where(upper_sub, pieces[k], pieces[k + 1]) for k in which])

    def restore(pieces):
        middle = [jnp.where(upper_sub, q, p) for p, q in zip(pieces[:-1], pieces[1:])]
        return join([pieces[0], *middle, pieces[-1]])

    def coefficients(speed, drop, driving, rate, which):
        s_shift = [between(f, which) for f in shifts(speed)]
        d_shift = [between(f, which) for f in shifts(drop)]
        drop, driving, rate = [between(f, which) for f in (drop, driving, rate)]
        sdx, sdy = s_shift[0] - s_shift[1], s_shift[2] - s_shift[3]
        ddx, ddy = d_shift[0] - d_shift[1], d_shift[2] - d_shift[3]
        c2, c3 = ddx * ddx + ddy * ddy, drop * drop
        return [
            (sdx * sdx + sdy * sdy) + 4.0 * FLOOR,
            sdx * ddx + sdy * ddy,
            c2,
            c3,
            c2 + steady * c3,
            (s_shift[0] + s_shift[1]) + (s_shift[2] + s_shift[3]),
            (d_shift[0] + d_shift[1]) + (d_shift[2] + d_shift[3]),
            driving * (2.0 * SHARE / rate),
        ]

    def viscosity(flat, offset):
        for n in range(flat[0].shape[0] // RIM):
            at = slice(offset + RIM * n, offset + RIM * n + RIM)
            c0, c1, c2, c3, c23, n0, n1, dr = [f[RIM * n : RIM * n + RIM] for f in flat]
            higher = None
            for k in reversed(range(LAYERS)):
                wk = float(w[k])
                if k < settled:
                    strain = c0 + (c1 * (2.0 * wk) + c23 * (wk * wk))
                else:
                    strain = c0 + (c1 * (2.0 * wk) + c2 * (wk * wk))
                    if k < LAYERS - 1:
                        strain = strain + c3 * float(4.0 * (w[k + 1] - w[k]) ** 2)
                now = jnp.exp2(jnp.log(strain) * THIRD)
                q_ref[k, at] = now
                r_ref[k, at] = dr + now * (n0 + n1 * wk)
                if k < LAYERS - 1:
                    g_ref[k, at] = 0.5 * (now + higher)
                higher = now

    def step(d, e, t, g, q, r):
        d = e + (g if d is None else g * d)
        return d, q * d + g * e, r * d + g * t

    def from_surface(at):
        d, e, t = None, q_ref[LAYERS - 1, at], r_ref[LAYERS - 1, at]
        for k in range(LAYERS - 1):
            j = LAYERS - 2 - k
            d, e, t = step(d, e, t, g_ref[j, at], q_ref[j, at], r_ref[j, at])
            if k % RESCALE == RESCALE - 1 and k < LAYERS - 2:
                shrink = 1.0 / d
                d, e, t = None, e * shrink, t * shrink
        return d, e, t

    def from_base(at):
        d, e, t, product = None, q_ref[0, at], r_ref[0, at], None
        for k in range(LAYERS - 1):
            g = g_ref[k, at]
            product = g if product is None else product * g
            d, e, t = step(d, e, t, g, q_ref[k + 1, at], r_ref[k + 1, at])
            if k % RESCALE == RESCALE - 1 and k < LAYERS - 2:
                shrink = 1.0 / d
                d, e, t, product = None, e * shrink, t * shrink, product * shrink
        shrink = 1.0 / e
        return t * shrink, product * shrink

    def result_copy(src, planes, where, target):
        return remote(src, out.at[0, planes, where], out_send, out_recv, target)

    inner_chunks = [(0, RIM, rows - 2 * RIM)]
    outer_chunks = [(0, 0, RIM), (RIM, rows - RIM, RIM)]

    def send_results(chunks, k, pressure, surface, sliding, scale):
        count = pressure.shape[0]
        at = pl.ds(0, count)
        send_p[0, at] = pressure[:, :lanes]
        send_p[1, at] = pressure[:, lanes:]
        mine, other = (slice(0, lanes), 1) if k == 0 else (slice(lanes, wide), 0)

        def started(copies):
            for c in copies:
                c.start()

        def pieces(src, planes, target):
            return [result_copy(src(pl.ds(a, n)), planes, pl.ds(b, n), target) for a, b, n in chunks]

        @pl.when(sends_last)
        def _():
            pl.semaphore_wait(credit.at[1], 2)
            for r in (1, 0):
                started(pieces(lambda d, r=r: send_p.at[r, d], strip, {"sec": sectors, "gy": r}))

        @pl.when(is_water)
        def _():
            started(pieces(lambda d: send_p.at[other, d], 0, {"gy": partner}))
            for a, b, n in chunks:
                out[0, 0, b : b + n] = pressure[a : a + n, mine]

        @pl.when(is_ice)
        def _():
            theirs = slice(lanes, wide) if k == 0 else slice(0, lanes)
            for plane, f in enumerate((surface(), sliding, scale * pressure)):
                results[plane, at] = f[:, theirs]
                for a, b, n in chunks:
                    out[0, plane, b : b + n] = f[a : a + n, mine]
            started(pieces(lambda d: results.at[:, d], slice(None), {"gy": partner}))

    tiles = rows // RIM
    await_tiles(main_recv, 10 * tiles)

    def down_of(parts, base):
        d, e, t = parts
        return t / (e + base * d)

    @pl.when(is_inner)
    def _():
        driving, rate, friction, melt, trans, leakage, overburden, scale, ice = fields((own_f, own_i), (part_f, part_i)).values()
        which = range(tiles - 1)
        at = slice(0, rows - RIM)
        speed, drop = first_velocity(driving, rate, friction, ice)
        viscosity(coefficients(speed, drop, driving, rate, which), 0)
        pl.when(starts_first)(send_upwards)
        trans_eff, source = sheet(speed + drop * float(w[0]), trans, melt, friction)
        pressure = water_steps(overburden, trans_eff, leakage, source)[-1]
        friction = scale * pressure
        base = between(friction * (0.5 * SHARE / rate), which)
        basal = down_of(from_surface(at), base)
        quarter = 0.25 * ice
        sliding = restore(split(basal)) * quarter
        trans_eff, source = sheet(sliding, trans, melt, friction)
        pressure = water_steps(pressure, trans_eff, leakage, source)[-1]
        mine = slice(RIM, rows - RIM)

        def surface():
            top, reach = from_base(at)
            return (restore(split(top - base * basal * reach)) * quarter)[mine]

        send_results(inner_chunks, 0, pressure[mine], surface, sliding[mine], scale[mine])

    @pl.when(is_outer)
    def _():
        middle = fields((part_f, part_i), (own_f, own_i))
        driving, rate, friction, melt, trans, leakage, overburden, scale, ice = middle.values()
        m_speed, m_drop = first_velocity(driving, rate, friction, ice)
        which = (0, tiles - 2)
        early = slice(0, 2 * RIM)
        viscosity(coefficients(m_speed, m_drop, driving, rate, which), 0)
        pl.when(starts_first)(send_upwards)
        early_down = from_surface(early)
        top, reach = from_base(early)
        m_first = sheet(m_speed + m_drop * float(w[0]), trans, melt, friction)
        steps_1 = water_steps(overburden, m_first[0], leakage, m_first[1])
        m_friction = scale * steps_1[-1]
        base = between(m_friction * (0.5 * SHARE / rate), which)
        basal = down_of(early_down, base)
        early_basal = split(basal)
        early_surface = split(top - base * basal * reach)
        blank = [jnp.zeros((RIM, wide), jnp.float32)] * (tiles - 3)
        m_second = sheet(
            restore([early_basal[0], *blank, early_basal[1]]) * (0.25 * ice), trans, melt, m_friction
        )
        steps_2 = water_steps(steps_1[-1], m_second[0], leakage, m_second[1])

        halo_sides = ((0, below), (1, above))

        def await_halo(side, exists, part):
            pl.when(exists)(functools.partial(await_tiles, halo_recv.at[side, part], 10))

        def frame(a, f, b):
            return join([a, f, b])

        def ends(f):
            return join([f[: 2 * RIM], f[rows:]])

        def inside(e, f):
            return join([e[: 2 * RIM], f[RIM : rows - RIM], e[2 * RIM :]])

        def end_frame(i):
            return join([low[i], middle[i][:RIM], middle[i][rows - RIM :], high[i]])

        ends_in, end_velocity, late_down = [], [], []
        for side, exists in halo_sides:
            await_halo(side, exists, 0)
            h = halo_fields(side, exists, (0, 1, 2, 8))
            velocity = first_velocity(h[0], h[1], h[2], h[8])
            inner = slice(0, RIM) if side == 0 else slice(rows - RIM, rows)
            pairs = [(velocity[0], m_speed), (velocity[1], m_drop), (h[0], middle[0]), (h[1], middle[1])]
            viscosity(
                coefficients(*[join([a, f[inner]] if side == 0 else [f[inner], a]) for a, f in pairs], (0,)), (2 + side) * RIM
            )
            tile = slice((2 + side) * RIM, (3 + side) * RIM)
            if side == 0:
                late_down.append(from_surface(tile))
            ends_in.append(h)
            end_velocity.append(velocity)
            if side == 0:

                @pl.when(jnp.logical_not(below))
                def _():
                    up_ref[0], up_ref[1] = from_base(tile)

        low, high = ends_in
        low_velocity, high_velocity = end_velocity
        for side, exists in halo_sides:
            await_halo(side, exists, 1)
        late_down.append(from_surface(slice(3 * RIM, 4 * RIM)))
        late_down = [join(p) for p in zip(*late_down)]
        high_up = from_base(slice(3 * RIM, 4 * RIM))
        low |= halo_fields(0, below, (3, 4, 5, 6, 7))
        high |= halo_fields(1, above, (3, 4, 5, 6, 7))
        end_sheets = [
            sheet(s + d * float(w[0]), f[4], f[3], f[2])
            for f, (s, d) in ((low, low_velocity), (high, high_velocity))
        ]
        rate, melt, trans, leakage, overburden, scale, ice = [end_frame(i) for i in (1, 3, 4, 5, 6, 7, 8)]
        quarter = 0.25 * ice
        valid = join([
            jnp.broadcast_to(below, (RIM, wide)), jnp.ones((2 * RIM, wide), jnp.bool_), jnp.broadcast_to(above, (RIM, wide))
        ])
        trans_eff, source = [frame(*f) for f in zip(end_sheets[0], m_first, end_sheets[1])]
        sweep = sweeper(trans_eff, leakage, ends(source), valid, ends)
        pressure = overburden
        for step_1 in steps_1[:-1]:
            pressure = sweep(inside(pressure, step_1))
        friction = scale * pressure
        base = between(friction * (0.5 * SHARE / rate), (0, 2))
        basal = down_of(late_down, base)

        def arrange(early_pieces, late_pieces):
            first, last = late_pieces
            before, after = early_pieces
            return join([first, jnp.where(upper_sub, before, first), jnp.where(upper_sub, last, after), last]) * quarter

        sliding = arrange(early_basal, split(basal))
        trans_eff, source = sheet(sliding, trans, melt, friction)
        sweep = sweeper(inside(trans_eff, m_second[0]), leakage, source, valid, ends)
        for step_2 in steps_2[:-1]:
            pressure = sweep(inside(pressure, step_2))

        mine = slice(RIM, 3 * RIM)

        def surface():
            @pl.when(below)
            def _():
                up_ref[0], up_ref[1] = from_base(slice(2 * RIM, 3 * RIM))

            top, reach = [join([up_ref[n], f]) for n, f in enumerate(high_up)]
            return arrange(early_surface, split(top - base * basal * reach))[mine]

        send_results(outer_chunks, 1, pressure[mine], surface, sliding[mine], scale[mine])

    await_tiles(main_send, 10 * tiles)
    pl.when(both(below, above))(functools.partial(await_tiles, edge_send, 20))
    pl.when(below != above)(functools.partial(await_tiles, edge_send, 10))
    counts = (tiles - 2, 2)
    for role, mine, theirs in ((is_inner, *counts), (is_outer, *counts[::-1])):
        pl.when(both(sends_last, role))(functools.partial(await_tiles, out_send, 5 * mine))
        pl.when(both(first_sector, role))(functools.partial(await_tiles, out_send, 3 * mine))
        pl.when(both(is_water, role))(functools.partial(await_tiles, out_send, mine))
        pl.when(both(is_ice, role))(functools.partial(await_tiles, out_recv, 3 * theirs))
        pl.when(both(is_water, role))(functools.partial(await_tiles, out_recv, theirs + (sectors - 1) * tiles))


def narrow_map(nx, *args):
    sectors, rows, lanes = args[0].shape
    most = max(rows - 2 * RIM, 2 * RIM)
    f32 = jnp.float32
    vmem = pltpu.VMEM
    dma = pltpu.SemaphoreType.DMA
    return pl.pallas_call(
        functools.partial(narrow_kernel, sectors, nx),
        out_shape=pltpu.VMEM((1, sectors, rows, lanes), f32),
        in_specs=[pl.BlockSpec(memory_space=pltpu.HBM)] * len(args),
        out_specs=pl.BlockSpec(memory_space=pltpu.VMEM),
        scratch_shapes=[
            vmem((8, rows, lanes), f32),
            vmem((2, rows, lanes), jnp.int32),
            vmem((8, rows, lanes), f32),
            vmem((2, rows, lanes), jnp.int32),
            vmem((2, 2, 8, RIM, lanes), f32),
            vmem((2, 2, 2, RIM, lanes), jnp.int32),
            vmem((LAYERS, max(rows, 4 * RIM), 2 * lanes), f32),
            vmem((LAYERS, max(rows, 4 * RIM), 2 * lanes), f32),
            vmem((LAYERS, max(rows, 4 * RIM), 2 * lanes), f32),
            vmem((2, RIM, 2 * lanes), f32),
            vmem((2, most, lanes), f32),
            vmem((3, most, lanes), f32),
            dma,
            dma,
            dma,
            dma,
            dma,
            dma((2, 2)),
            dma,
            pltpu.SemaphoreType.REGULAR((3,)),
        ],
        compiler_params=pltpu.CompilerParams(collective_id=0, has_side_effects=True),
    )(*args)


def solution(mesh):
    spec = P(None, "gx", "gy")
    nx, ny = mesh.shape["gx"], mesh.shape["gy"]
    on_device = functools.partial(narrow_map, nx) if ny == 2 else functools.partial(wide_map, nx, ny)
    return jax.shard_map(
        on_device,
        mesh=mesh,
        in_specs=(spec,) * 10,
        out_specs=P("sec", None, "gx", "gy"),
        check_vma=False,
    )
```

```python
import functools

import jax
import jax.numpy as jnp
import numpy as np
from jax import lax
from jax.experimental import pallas as pl
from jax.experimental.pallas import tpu as pltpu
from jax.sharding import PartitionSpec as P

LAYERS = 40
SWEEPS = 4
VERT = 4.0
FLOOR = 0.25
HEATING = 0.5

RIM = 8
HALF = RIM // 2
RESCALE = 10
THIRD = -1.0 / (3.0 * float(np.log(2.0)))
DIRECTIONS = [(dx, dy) for dx in (-1, 0, 1) for dy in (-1, 0, 1) if (dx, dy) != (0, 0)]
MESH = pl.DeviceIdType.MESH


def basal_response():
    matrix = np.zeros((LAYERS, LAYERS))
    for k in range(LAYERS):
        matrix[k, k] = 4.0 + (VERT if k > 0 else 0.0) + (VERT if k < LAYERS - 1 else 0.0)
        if k > 0:
            matrix[k, k - 1] = matrix[k - 1, k] = -VERT
    unit = np.zeros(LAYERS)
    unit[0] = 1.0
    return np.linalg.solve(matrix, unit)


def turn(values, shift, axis):
    return pltpu.roll(values, shift % values.shape[axis], axis)


def neighbours(f):
    return turn(f, -1, 0), turn(f, 1, 0), turn(f, -1, 1), turn(f, 1, 1)


def water_solve(pressure, trans_eff, leakage, source, valid):
    faces = [0.5 * (trans_eff + t) for t in neighbours(trans_eff)]
    total = leakage + ((faces[0] + faces[1]) + (faces[2] + faces[3]))
    inverse = jnp.where(valid, 1.0 / total, 0.0)
    weights = [f * inverse for f in faces]
    base = source * inverse
    for _ in range(SWEEPS):
        parts = [w * p for w, p in zip(weights, neighbours(pressure))]
        pressure = base + ((parts[0] + parts[1]) + (parts[2] + parts[3]))
    return pressure


def wide_kernel(sectors, nx, ny, *refs):
    ins = refs[:10]
    out = refs[10]
    floats, ints, pack_l, pack_r, rim_l, rim_r, q_ref, g_ref, r_ref, send_p = refs[11:21]
    in_sem, send_sem, recv_sem, last_send, last_recv = refs[21:]
    rows, lanes = ins[0].shape[1:]
    sec = lax.axis_index("sec")
    gx = lax.axis_index("gx")
    gy = lax.axis_index("gy")
    strip = lax.rem(sec, sectors)
    is_ice = sec < sectors
    sends_last = jnp.logical_and(sec > 0, is_ice)

    def exists(dx, dy):
        x, y = gx + dx, gy + dy
        return jnp.logical_and(
            jnp.logical_and(x >= 0, x < nx), jnp.logical_and(y >= 0, y < ny)
        )

    float_ids = (0, 1, 2, 5, 6, 7, 8, 9)
    int_ids = (3, 4)
    loads = []
    for slot, arg in enumerate(float_ids):
        loads.append(pltpu.make_async_copy(ins[arg].at[strip], floats.at[slot, pl.ds(RIM, rows)], in_sem.at[0]))
    for slot, arg in enumerate(int_ids):
        loads.append(pltpu.make_async_copy(ins[arg].at[strip], ints.at[slot, pl.ds(RIM, rows)], in_sem.at[1]))
    barrier = pltpu.get_barrier_semaphore()
    count = jnp.int32(0)
    for dx, dy in sorted(DIRECTIONS, key=lambda d: -abs(d[0])):
        here = exists(dx, dy)
        count = count + here.astype(jnp.int32)

        @pl.when(here)
        def _(dx=dx, dy=dy):
            pl.semaphore_signal(barrier, inc=1, device_id={"gx": gx + dx, "gy": gy + dy}, device_id_type=MESH)

    count = count + sends_last.astype(jnp.int32)
    count = count + jnp.where(is_ice, 0, sectors - 1)

    @pl.when(sends_last)
    def _():
        pl.semaphore_signal(barrier, inc=1, device_id={"sec": sectors}, device_id_type=MESH)

    for s in range(1, sectors):

        @pl.when(jnp.logical_not(is_ice))
        def _(s=s):
            pl.semaphore_signal(barrier, inc=1, device_id={"sec": s}, device_id_type=MESH)

    for load in loads:
        load.start()
    for slot, buffer in enumerate((floats, ints)):
        mine = buffer.at[:, pl.ds(RIM, rows)]
        pltpu.make_async_copy(mine, mine, in_sem.at[slot]).wait()

    lane = lax.broadcasted_iota(jnp.int32, (rows, lanes), 1)
    fields = [floats[i, RIM : RIM + rows] for i in range(8)]
    fields += [ints[i, RIM : RIM + rows].astype(jnp.float32) for i in range(2)]
    left = jnp.zeros((rows, lanes), jnp.float32)
    right = jnp.zeros((rows, lanes), jnp.float32)
    for i, f in enumerate(fields):
        moved = turn(f, RIM * i, 1)
        group = lane // RIM
        left = jnp.where(group == i, moved, left)
        right = jnp.where(group == (i - 1) % (lanes // RIM), moved, right)
    pack_l[...] = left
    pack_r[...] = right

    pl.semaphore_wait(barrier, count)

    def copies(dx, dy, n):
        target = {"gx": gx + dx, "gy": gy + dy}

        def remote(src, dst, m):
            return pltpu.make_async_remote_copy(
                src_ref=src, dst_ref=dst, send_sem=send_sem.at[m], recv_sem=recv_sem.at[m],
                device_id=target, device_id_type=MESH,
            )

        if dy == 0:
            first = rows if dx > 0 else RIM
            landing = 0 if dx > 0 else RIM + rows
            return [
                remote(floats.at[:, pl.ds(first, RIM)], floats.at[:, pl.ds(landing, RIM)], n),
                remote(ints.at[:, pl.ds(first, RIM)], ints.at[:, pl.ds(landing, RIM)], 8 + (dx > 0)),
            ]
        src, dst = (pack_r, rim_l) if dy > 0 else (pack_l, rim_r)
        if dx == 0:
            return [remote(src, dst.at[pl.ds(RIM, rows)], n)]
        first = rows - RIM if dx > 0 else 0
        landing = 0 if dx > 0 else RIM + rows
        return [remote(src.at[pl.ds(first, RIM)], dst.at[pl.ds(landing, RIM)], n)]

    order = sorted(range(8), key=lambda n: abs(DIRECTIONS[n][1]))
    for n in order:
        dx, dy = DIRECTIONS[n]

        @pl.when(exists(dx, dy))
        def _(dx=dx, dy=dy, n=n):
            for c in copies(dx, dy, n):
                c.start()

    def arrive(n):
        dx, dy = DIRECTIONS[n]

        @pl.when(exists(-dx, -dy))
        def _():
            for c in copies(dx, dy, n):
                c.wait_recv()

    w = basal_response()
    ext = rows + 2 * RIM
    tall = rows + RIM
    tiles = tall // 8
    wide = 2 * RIM
    slot = lax.broadcasted_iota(jnp.int32, (8, lanes), 1) // wide
    lane_low = jnp.where(gy < ny - 1, lanes + RIM, lanes)
    lane_high = jnp.where(gy > 0, 2 * lanes - RIM, 2 * lanes)

    def in_map_lanes(height):
        lane_i = lax.broadcasted_iota(jnp.int32, (height, 2 * lanes), 1)
        return jnp.logical_or(lane_i < lane_low, lane_i >= lane_high)

    def field_reader(top, height, valid):
        at = slice(top, top + height)
        packed_l, packed_r = rim_l[at], rim_r[at]
        group = lax.broadcasted_iota(jnp.int32, (height, lanes), 1) // RIM

        def field(i, fill):
            main = floats[i, at] if i < 8 else ints[i - 8, at].astype(jnp.float32)
            rim = turn(jnp.where(group == i, packed_r, packed_l), -RIM * i, 1)
            return jnp.where(valid, jnp.concatenate([main, rim], axis=1), fill)

        return field

    def first_velocity(driving, rate, friction, ice):
        viscous = rate * float(FLOOR ** (-1.0 / 3.0))
        speed = driving / (4.0 * viscous)
        drop = -speed * friction / (viscous + friction * float(w[0]))
        return speed * ice, drop * ice

    def squeeze(f, which):
        tile = jnp.zeros((8, lanes), jnp.float32)
        for n, t in enumerate(which):
            moved = turn(f[8 * t : 8 * t + 8, lanes:], wide * n + RIM, 1)
            tile = jnp.where(slot == n, moved, tile)
        return jnp.concatenate([f[8 * t : 8 * t + 8, :lanes] for t in which] + [tile], axis=0)

    def spread(f, count):
        last = f[8 * count :]
        return [
            jnp.concatenate([f[8 * n : 8 * n + 8], turn(last, -(wide * n + RIM), 1)], axis=1)
            for n in range(count)
        ]

    def eliminate(speed, drop, driving, rate, which, offset, lead):
        sxp, sxm, syp, sym = neighbours(speed)
        dxp, dxm, dyp, dym = neighbours(drop)
        sdx, sdy, ddx, ddy = sxp - sxm, syp - sym, dxp - dxm, dyp - dym
        flat = [
            0.03125 * (sdx * sdx + sdy * sdy) + 0.125 * FLOOR,
            0.0625 * (sdx * ddx + sdy * ddy),
            0.03125 * (ddx * ddx + ddy * ddy),
            0.125 * drop * drop,
            0.25 * ((sxp + sxm) + (syp + sym)),
            0.25 * ((dxp + dxm) + (dyp + dym)),
            driving * (0.5 / rate),
        ]
        flat = [squeeze(turn(f, lead, 0), which) for f in flat]
        for n in range(len(which) + 1):
            at = slice(offset + 8 * n, offset + 8 * n + 8)
            c0, c1, c2, c3, n0, n1, dr = [f[8 * n : 8 * n + 8] for f in flat]
            before = None
            for k in range(LAYERS):
                wk = float(w[k])
                strain = c0 + (c1 * wk + c2 * (wk * wk))
                if k < LAYERS - 1:
                    strain = strain + c3 * float((w[k + 1] - w[k]) ** 2)
                twice = jnp.exp2(jnp.log(strain) * THIRD)
                q_ref[k, at] = twice
                r_ref[k, at] = dr + twice * (n0 + n1 * wk)
                if k > 0:
                    g_ref[k - 1, at] = 0.5 * (before + twice)
                before = twice

        at = slice(offset, offset + 8 * (len(which) + 1))
        up_d, up_e, up_t = None, q_ref[0, at], r_ref[0, at]
        down_d, down_e, down_t = None, q_ref[LAYERS - 1, at], r_ref[LAYERS - 1, at]
        product = None

        def step(d, e, t, g, q, r):
            d = e + (g if d is None else g * d)
            return d, q * d + g * e, r * d + g * t

        for k in range(LAYERS - 1):
            j = LAYERS - 2 - k
            g = g_ref[k, at]
            product = g if product is None else product * g
            up_d, up_e, up_t = step(up_d, up_e, up_t, g, q_ref[k + 1, at], r_ref[k + 1, at])
            down_d, down_e, down_t = step(
                down_d, down_e, down_t, g_ref[j, at], q_ref[j, at], r_ref[j, at]
            )
            if k % RESCALE == RESCALE - 1 and k < LAYERS - 2:
                shrink = 1.0 / up_d
                up_d, up_e, up_t, product = None, up_e * shrink, up_t * shrink, product * shrink
                shrink = 1.0 / down_d
                down_d, down_e, down_t = None, down_e * shrink, down_t * shrink
        shrink = 1.0 / up_e
        return down_d, down_e, down_t, up_t * shrink, product * shrink

    def finish(parts, friction, rate, ice, which):
        down_d, down_e, down_t, top, reach = parts
        base = squeeze(turn(friction * (0.5 / rate), -HALF, 0), which)
        mask = squeeze(turn(ice, -HALF, 0), which)
        basal = down_t / (down_e + base * down_d)
        surface = top - base * basal * reach
        return [spread(f * mask, len(which)) for f in (basal, surface)]

    for n in order:
        if DIRECTIONS[n][0] == 0:
            arrive(n)
    early = list(range(1, tiles - 1))
    late = [0, tiles - 1]
    field = field_reader(RIM, rows, in_map_lanes(rows))
    driving, rate = field(0, 0.0), field(1, 1.0)
    speed, drop = first_velocity(driving, rate, field(2, 0.0) * field(9, 0.0), field(8, 0.0))
    early_parts = eliminate(speed, drop, driving, rate, early, 0, HALF)
    for n in order:
        if DIRECTIONS[n][0] != 0:
            arrive(n)

    row_i = lax.broadcasted_iota(jnp.int32, (ext, 2 * lanes), 0)
    row_low = jnp.where(gx > 0, 0, RIM)
    row_high = jnp.where(gx < nx - 1, ext, RIM + rows)
    valid = jnp.logical_and(
        jnp.logical_and(row_i >= row_low, row_i < row_high), in_map_lanes(ext)
    )
    field = field_reader(0, ext, valid)
    driving = field(0, 0.0)
    rate = field(1, 1.0)
    friction = field(2, 0.0)
    melt = field(3, 0.0)
    trans = field(4, 0.0)
    leakage = field(5, 1.0)
    pressure = field(6, 0.0)
    scale = field(7, 0.0)
    ice = field(8, 0.0)
    grounded = field(9, 0.0)
    friction = friction * grounded
    scale = scale * grounded

    speed, drop = first_velocity(driving, rate, friction, ice)
    sliding = speed + drop * float(w[0])
    squared = sliding * sliding
    trans_eff = trans * (1.0 + squared / (1.0 + squared))
    source = melt + HEATING * friction * squared
    pressure = water_solve(pressure, trans_eff, leakage, source, valid)
    friction = scale * pressure

    late_parts = eliminate(speed, drop, driving, rate, late, 8 * (len(early) + 1), -HALF)
    pieces = [None] * tiles
    for parts, which in ((early_parts, early), (late_parts, late)):
        for n, piece in enumerate(zip(*finish(parts, friction, rate, ice, which))):
            pieces[which[n]] = piece
    blank = jnp.zeros((RIM, 2 * lanes), jnp.float32)
    basal = turn(jnp.concatenate([p[0] for p in pieces] + [blank], axis=0), HALF, 0)
    surface = jnp.concatenate([p[1][:, :lanes] for p in pieces], axis=0)
    sliding = jnp.where(valid, basal, 0.0)
    squared = sliding * sliding
    trans_eff = trans * (1.0 + squared / (1.0 + squared))
    source = melt + HEATING * friction * squared
    pressure = water_solve(pressure, trans_eff, leakage, source, valid)
    block = pressure[RIM : RIM + rows, :lanes]
    send_p[...] = block

    def last():
        return pltpu.make_async_remote_copy(
            src_ref=send_p, dst_ref=out.at[0, strip], send_sem=last_send, recv_sem=last_recv.at[strip],
            device_id={"sec": sectors}, device_id_type=MESH,
        )

    @pl.when(sends_last)
    def _():
        last().start()

    @pl.when(is_ice)
    def _():
        out[0, 0] = turn(surface, -HALF, 0)[:rows]
        out[0, 1] = sliding[RIM : RIM + rows, :lanes]
        out[0, 2] = scale[RIM : RIM + rows, :lanes] * block

    @pl.when(jnp.logical_not(is_ice))
    def _():
        out[0, 0] = block

    for n in order:
        dx, dy = DIRECTIONS[n]

        @pl.when(exists(dx, dy))
        def _(dx=dx, dy=dy, n=n):
            for c in copies(dx, dy, n):
                c.wait_send()

    @pl.when(sends_last)
    def _():
        last().wait_send()

    for s in range(1, sectors):

        @pl.when(jnp.logical_not(is_ice))
        def _(s=s):
            pltpu.make_async_remote_copy(
                src_ref=send_p, dst_ref=out.at[0, s], send_sem=last_send, recv_sem=last_recv.at[s],
                device_id={"sec": 0}, device_id_type=MESH,
            ).wait_recv()


def wide_map(nx, ny, *args):
    sectors, rows, lanes = args[0].shape
    ext = rows + 2 * RIM
    f32 = jnp.float32
    vmem = pltpu.VMEM
    dma = pltpu.SemaphoreType.DMA
    return pl.pallas_call(
        functools.partial(wide_kernel, sectors, nx, ny),
        out_shape=pltpu.VMEM((1, sectors, rows, lanes), f32),
        in_specs=[pl.BlockSpec(memory_space=pltpu.HBM)] * len(args),
        out_specs=pl.BlockSpec(memory_space=pltpu.VMEM),
        scratch_shapes=[
            vmem((8, ext, lanes), f32),
            vmem((2, ext, lanes), jnp.int32),
            vmem((rows, lanes), f32),
            vmem((rows, lanes), f32),
            vmem((ext, lanes), f32),
            vmem((ext, lanes), f32),
            vmem((LAYERS, ext + RIM, lanes), f32),
            vmem((LAYERS, ext + RIM, lanes), f32),
            vmem((LAYERS, ext + RIM, lanes), f32),
            vmem((rows, lanes), f32),
            dma((2,)),
            dma((10,)),
            dma((10,)),
            dma,
            dma((sectors,)),
        ],
        compiler_params=pltpu.CompilerParams(collective_id=0, has_side_effects=True),
    )(*args)


SHARE = 32.0 ** (-1.0 / 3.0)


def steady_drop(w):
    ratios = np.float32(4.0 * ((w[1:] - w[:-1]) / w[:-1]) ** 2)
    same = np.cumprod(ratios == ratios[0])
    return float(ratios[0]), int(same.sum())


ORDER = (0, 1, 2, 5, 6, 7, 8, 9, 3, 4)


def narrow_kernel(sectors, nx, *refs):
    ins = refs[:10]
    out = refs[10]
    own_f, own_i, part_f, part_i, halo_f, halo_i, q_ref, g_ref, r_ref, up_ref, send_p, results = refs[11:23]
    in_sem, main_send, out_send, main_recv, halo_recv, out_recv, credit = refs[23:]
    rows, lanes = ins[0].shape[1:]
    sec = lax.axis_index("sec")
    gx = lax.axis_index("gx")
    gy = lax.axis_index("gy")
    partner = 1 - gy
    is_outer = gy == 1
    is_inner = gy == 0
    strip = lax.rem(sec, sectors)
    is_ice = sec < sectors
    is_water = jnp.logical_not(is_ice)
    sends_last = jnp.logical_and(sec > 0, is_ice)
    below, above = gx > 0, gx < nx - 1
    first_sector = sec == 0

    def both(p, q):
        return jnp.logical_and(p, q)

    def number(condition):
        return condition.astype(jnp.int32)

    def await_tiles(sem, count):
        wide_tiles = count % 2 == 0
        room = q_ref.at[pl.ds(0, count // 2 if wide_tiles else count), pl.ds(0, RIM), pl.ds(0, (1 + wide_tiles) * lanes)]
        pltpu.make_async_copy(room, room, sem).wait()

    def copy_in(n):
        dst = own_f.at[n] if n < 8 else own_i.at[n - 8]
        return pltpu.make_async_copy(ins[ORDER[n]].at[strip], dst, in_sem)

    def load():
        for n in range(10):
            copy_in(n).start()

    pl.when(is_outer)(load)
    barrier = pltpu.get_barrier_semaphore()

    def signal(condition, sem, target, role=True):
        @pl.when(jnp.logical_and(condition, role))
        def _():
            pl.semaphore_signal(sem, inc=1, device_id=target, device_id_type=MESH)

    signal(above, barrier, {"gx": gx + 1, "gy": 0}, is_outer)
    signal(above, barrier, {"gx": gx + 1, "gy": 1}, is_outer)
    signal(is_outer, barrier, {"gy": 0})
    signal(sends_last, barrier, {"sec": sectors, "gy": partner})
    signal(sends_last, barrier, {"sec": sectors})
    count = number(is_inner) + number(below) + jnp.where(is_ice, 0, 2 * (sectors - 1))

    @pl.when(count > 0)
    def _():
        pl.semaphore_wait(barrier, count)

    signal(below, credit.at[0], {"gx": gx - 1, "gy": 1}, is_outer)

    def remote(src, dst, sent, landed, target):
        return pltpu.make_async_remote_copy(
            src_ref=src, dst_ref=dst, send_sem=sent, recv_sem=landed, device_id=target, device_id_type=MESH,
        )

    def main_copies():
        target = {"gy": partner}
        return [remote(own_f, part_f, main_send, main_recv, target), remote(own_i, part_i, main_send, main_recv, target)]

    def edge_copies():
        src = pl.ds(rows - RIM, RIM)
        target = {"gx": gx + 1, "gy": 1}
        first, rest = pl.ds(0, 3), pl.ds(3, 5)
        return [
            remote(own_f.at[first, src], halo_f.at[0, gy, first], main_send, halo_recv.at[0], target),
            remote(own_i.at[:, src], halo_i.at[0, gy], main_send, halo_recv.at[0], target),
            remote(own_f.at[rest, src], halo_f.at[0, gy, rest], main_send, halo_recv.at[2], target),
        ]

    def start(condition, copies):
        @pl.when(condition)
        def _():
            for c in copies:
                c.start()

    def await_credit(condition, which, amount):
        @pl.when(condition)
        def _():
            pl.semaphore_wait(credit.at[which], amount)

    @pl.when(below)
    def _():
        for n in (0, 1, 2, 8, 9, 3, 4, 5, 6, 7):
            src = ins[ORDER[n]].at[strip, pl.ds(0, RIM)]
            dst = halo_f.at[1, gy, n] if n < 8 else halo_i.at[1, gy, n - 8]
            part = int(3 <= n < 8)
            remote(src, dst, main_send, halo_recv.at[1 + part], {"gx": gx - 1, "gy": 1}).start()

    signal(is_inner, credit.at[2], {"gy": 1})
    pl.when(is_inner)(load)

    @pl.when(is_inner)
    def _():
        for n in (0, 1, 2, 8, 9, 3, 4, 5, 6, 7):
            dst = part_f.at[n] if n < 8 else part_i.at[n - 8]
            remote(ins[ORDER[n]].at[strip], dst, main_send, main_recv, {"gy": 1}).start()

    for s in range(1, sectors):
        signal(is_water, credit.at[1], {"sec": s, "gy": partner})
        signal(is_water, credit.at[1], {"sec": s})
    await_tiles(in_sem, 10 * rows // RIM)
    await_credit(is_outer, 2, 1)
    start(is_outer, main_copies())

    def send_upwards():
        await_credit(both(above, is_outer), 0, 1)
        signal(is_outer, credit.at[0], {"gy": 0})
        await_credit(is_inner, 0, 1)
        start(above, edge_copies())

    starts_first = both(first_sector, gx == 0)
    pl.when(jnp.logical_not(starts_first))(send_upwards)


    w = basal_response()
    steady, settled = steady_drop(w)
    wide = 2 * lanes
    lane = lax.broadcasted_iota(jnp.int32, (RIM, wide), 1)
    upper_sub = lax.broadcasted_iota(jnp.int32, (RIM, wide), 0) >= HALF
    last_lane = lane == wide - 1
    first_lane = lane == 0

    def join(parts):
        return jnp.concatenate(parts, axis=0)

    def tall_mask(mask, count):
        return join([mask] * count)

    def beside(f, i):
        return f[i] if i < 8 else f[i - 8].astype(jnp.float32)

    def fields(left, right, which=range(9)):
        def field(i):
            return jnp.concatenate([beside(left[i >= 8], i), beside(right[i >= 8], i)], axis=1)

        return {i: field(i) * field(9) if i in (2, 7) else field(i) for i in which}

    def halo_fields(side, exists, which):
        left, right = [(halo_f.at[side, r], halo_i.at[side, r]) for r in range(2)]
        return {
            i: jnp.where(exists, f, 1.0 if i in (1, 5) else 0.0) for i, f in fields(left, right, which).items()
        }

    def first_velocity(driving, rate, friction, ice):
        viscous = rate * float(FLOOR ** (-1.0 / 3.0))
        speed = driving / (4.0 * viscous)
        drop = -speed * friction / (viscous + friction * float(w[0]))
        return speed * ice, drop * ice

    def shifts(f):
        count = f.shape[0] // RIM
        yp = jnp.where(tall_mask(last_lane, count), 0.0, turn(f, -1, 1))
        ym = jnp.where(tall_mask(first_lane, count), 0.0, turn(f, 1, 1))
        return turn(f, -1, 0), turn(f, 1, 0), yp, ym

    def sheet(sliding, trans, melt, friction):
        squared = sliding * sliding
        return trans * (1.0 + squared / (1.0 + squared)), melt + HEATING * friction * squared

    def sweeper(trans_eff, leakage, source, valid, keep):
        here = keep(trans_eff)
        faces = [0.5 * (here + keep(t)) for t in shifts(trans_eff)]
        total = leakage + ((faces[0] + faces[1]) + (faces[2] + faces[3]))
        inverse = 1.0 / total if valid is None else jnp.where(valid, 1.0 / total, 0.0)
        weights = [f * inverse for f in faces]
        count = here.shape[0] // RIM
        weights[2] = jnp.where(tall_mask(last_lane, count), 0.0, weights[2])
        weights[3] = jnp.where(tall_mask(first_lane, count), 0.0, weights[3])
        base = source * inverse

        def sweep(pressure):
            parts = [w * keep(p) for w, p in zip(weights, neighbours(pressure))]
            return base + ((parts[0] + parts[1]) + (parts[2] + parts[3]))

        return sweep

    def water_steps(pressure, trans_eff, leakage, source):
        sweep = sweeper(trans_eff, leakage, source, None, lambda f: f)
        steps = [pressure]
        for _ in range(SWEEPS):
            steps.append(sweep(steps[-1]))
        return steps

    def split(f):
        return [f[RIM * k : RIM * k + RIM] for k in range(f.shape[0] // RIM)]

    def between(f, which):
        pieces = split(f)
        return join([jnp.where(upper_sub, pieces[k], pieces[k + 1]) for k in which])

    def restore(pieces):
        middle = [jnp.where(upper_sub, q, p) for p, q in zip(pieces[:-1], pieces[1:])]
        return join([pieces[0], *middle, pieces[-1]])

    def coefficients(speed, drop, driving, rate, which):
        s_shift = [between(f, which) for f in shifts(speed)]
        d_shift = [between(f, which) for f in shifts(drop)]
        drop, driving, rate = [between(f, which) for f in (drop, driving, rate)]
        sdx, sdy = s_shift[0] - s_shift[1], s_shift[2] - s_shift[3]
        ddx, ddy = d_shift[0] - d_shift[1], d_shift[2] - d_shift[3]
        c2, c3 = ddx * ddx + ddy * ddy, drop * drop
        return [
            (sdx * sdx + sdy * sdy) + 4.0 * FLOOR,
            sdx * ddx + sdy * ddy,
            c2,
            c3,
            c2 + steady * c3,
            (s_shift[0] + s_shift[1]) + (s_shift[2] + s_shift[3]),
            (d_shift[0] + d_shift[1]) + (d_shift[2] + d_shift[3]),
            driving * (2.0 * SHARE / rate),
        ]

    def viscosity(flat, offset):
        for n in range(flat[0].shape[0] // RIM):
            at = slice(offset + RIM * n, offset + RIM * n + RIM)
            c0, c1, c2, c3, c23, n0, n1, dr = [f[RIM * n : RIM * n + RIM] for f in flat]
            higher = None
            for k in reversed(range(LAYERS)):
                wk = float(w[k])
                if k < settled:
                    strain = c0 + (c1 * (2.0 * wk) + c23 * (wk * wk))
                else:
                    strain = c0 + (c1 * (2.0 * wk) + c2 * (wk * wk))
                    if k < LAYERS - 1:
                        strain = strain + c3 * float(4.0 * (w[k + 1] - w[k]) ** 2)
                now = jnp.exp2(jnp.log(strain) * THIRD)
                q_ref[k, at] = now
                r_ref[k, at] = dr + now * (n0 + n1 * wk)
                if k < LAYERS - 1:
                    g_ref[k, at] = 0.5 * (now + higher)
                higher = now

    def step(d, e, t, g, q, r):
        d = e + (g if d is None else g * d)
        return d, q * d + g * e, r * d + g * t

    def from_surface(at):
        d, e, t = None, q_ref[LAYERS - 1, at], r_ref[LAYERS - 1, at]
        for k in range(LAYERS - 1):
            j = LAYERS - 2 - k
            d, e, t = step(d, e, t, g_ref[j, at], q_ref[j, at], r_ref[j, at])
            if k % RESCALE == RESCALE - 1 and k < LAYERS - 2:
                shrink = 1.0 / d
                d, e, t = None, e * shrink, t * shrink
        return d, e, t

    def from_base(at):
        d, e, t, product = None, q_ref[0, at], r_ref[0, at], None
        for k in range(LAYERS - 1):
            g = g_ref[k, at]
            product = g if product is None else product * g
            d, e, t = step(d, e, t, g, q_ref[k + 1, at], r_ref[k + 1, at])
            if k % RESCALE == RESCALE - 1 and k < LAYERS - 2:
                shrink = 1.0 / d
                d, e, t, product = None, e * shrink, t * shrink, product * shrink
        shrink = 1.0 / e
        return t * shrink, product * shrink

    def result_copy(src, planes, where, target):
        return remote(src, out.at[0, planes, where], out_send, out_recv, target)

    inner_chunks = [(0, RIM, rows - 2 * RIM)]
    outer_chunks = [(0, 0, RIM), (RIM, rows - RIM, RIM)]

    def send_results(chunks, k, pressure, surface, sliding, scale):
        count = pressure.shape[0]
        at = pl.ds(0, count)
        send_p[0, at] = pressure[:, :lanes]
        send_p[1, at] = pressure[:, lanes:]
        mine, other = (slice(0, lanes), 1) if k == 0 else (slice(lanes, wide), 0)

        def started(copies):
            for c in copies:
                c.start()

        def pieces(src, planes, target):
            return [result_copy(src(pl.ds(a, n)), planes, pl.ds(b, n), target) for a, b, n in chunks]

        @pl.when(sends_last)
        def _():
            pl.semaphore_wait(credit.at[1], 2)
            for r in (1, 0):
                started(pieces(lambda d, r=r: send_p.at[r, d], strip, {"sec": sectors, "gy": r}))

        @pl.when(is_water)
        def _():
            started(pieces(lambda d: send_p.at[other, d], 0, {"gy": partner}))
            for a, b, n in chunks:
                out[0, 0, b : b + n] = pressure[a : a + n, mine]

        @pl.when(is_ice)
        def _():
            theirs = slice(lanes, wide) if k == 0 else slice(0, lanes)
            for plane, f in enumerate((surface(), sliding, scale * pressure)):
                results[plane, at] = f[:, theirs]
                for a, b, n in chunks:
                    out[0, plane, b : b + n] = f[a : a + n, mine]
            started(pieces(lambda d: results.at[:, d], slice(None), {"gy": partner}))

    tiles = rows // RIM
    await_tiles(main_recv, 10 * tiles)

    def down_of(parts, base):
        d, e, t = parts
        return t / (e + base * d)

    @pl.when(is_inner)
    def _():
        driving, rate, friction, melt, trans, leakage, overburden, scale, ice = fields((own_f, own_i), (part_f, part_i)).values()
        which = range(tiles - 1)
        at = slice(0, rows - RIM)
        speed, drop = first_velocity(driving, rate, friction, ice)
        viscosity(coefficients(speed, drop, driving, rate, which), 0)
        pl.when(starts_first)(send_upwards)
        trans_eff, source = sheet(speed + drop * float(w[0]), trans, melt, friction)
        pressure = water_steps(overburden, trans_eff, leakage, source)[-1]
        friction = scale * pressure
        base = between(friction * (0.5 * SHARE / rate), which)
        basal = down_of(from_surface(at), base)
        quarter = 0.25 * ice
        sliding = restore(split(basal)) * quarter
        trans_eff, source = sheet(sliding, trans, melt, friction)
        pressure = water_steps(pressure, trans_eff, leakage, source)[-1]
        mine = slice(RIM, rows - RIM)

        def surface():
            top, reach = from_base(at)
            return (restore(split(top - base * basal * reach)) * quarter)[mine]

        send_results(inner_chunks, 0, pressure[mine], surface, sliding[mine], scale[mine])

    @pl.when(is_outer)
    def _():
        middle = fields((part_f, part_i), (own_f, own_i))
        driving, rate, friction, melt, trans, leakage, overburden, scale, ice = middle.values()
        m_speed, m_drop = first_velocity(driving, rate, friction, ice)
        which = (0, tiles - 2)
        early = slice(0, 2 * RIM)
        viscosity(coefficients(m_speed, m_drop, driving, rate, which), 0)
        pl.when(starts_first)(send_upwards)
        early_down = from_surface(early)
        top, reach = from_base(early)
        m_first = sheet(m_speed + m_drop * float(w[0]), trans, melt, friction)
        steps_1 = water_steps(overburden, m_first[0], leakage, m_first[1])
        m_friction = scale * steps_1[-1]
        base = between(m_friction * (0.5 * SHARE / rate), which)
        basal = down_of(early_down, base)
        early_basal = split(basal)
        early_surface = split(top - base * basal * reach)
        blank = [jnp.zeros((RIM, wide), jnp.float32)] * (tiles - 3)
        m_second = sheet(
            restore([early_basal[0], *blank, early_basal[1]]) * (0.25 * ice), trans, melt, m_friction
        )
        steps_2 = water_steps(steps_1[-1], m_second[0], leakage, m_second[1])

        halo_sides = ((0, below), (1, above))

        def await_halo(side, exists):
            pl.when(exists)(functools.partial(await_tiles, halo_recv.at[side], 10))

        def frame(a, f, b):
            return join([a, f, b])

        def ends(f):
            return join([f[: 2 * RIM], f[rows:]])

        def inside(e, f):
            return join([e[: 2 * RIM], f[RIM : rows - RIM], e[2 * RIM :]])

        def end_frame(i):
            return join([low[i], middle[i][:RIM], middle[i][rows - RIM :], high[i]])

        ends_in, end_velocity, late_down = [], [], []
        for side, exists in halo_sides:
            await_halo(side, exists)
            h = halo_fields(side, exists, (0, 1, 2, 8))
            velocity = first_velocity(h[0], h[1], h[2], h[8])
            inner = slice(0, RIM) if side == 0 else slice(rows - RIM, rows)
            pairs = [(velocity[0], m_speed), (velocity[1], m_drop), (h[0], middle[0]), (h[1], middle[1])]
            viscosity(
                coefficients(*[join([a, f[inner]] if side == 0 else [f[inner], a]) for a, f in pairs], (0,)), (2 + side) * RIM
            )
            tile = slice((2 + side) * RIM, (3 + side) * RIM)
            if side == 0:
                late_down.append(from_surface(tile))
            ends_in.append(h)
            end_velocity.append(velocity)
            if side == 0:

                @pl.when(jnp.logical_not(below))
                def _():
                    up_ref[0], up_ref[1] = from_base(tile)

        low, high = ends_in
        low_velocity, high_velocity = end_velocity
        pl.when(both(below, above))(functools.partial(await_tiles, halo_recv.at[2], 20))
        pl.when(below != above)(functools.partial(await_tiles, halo_recv.at[2], 10))
        late_down.append(from_surface(slice(3 * RIM, 4 * RIM)))
        late_down = [join(p) for p in zip(*late_down)]
        high_up = from_base(slice(3 * RIM, 4 * RIM))
        low |= halo_fields(0, below, (3, 4, 5, 6, 7))
        high |= halo_fields(1, above, (3, 4, 5, 6, 7))
        end_sheets = [
            sheet(s + d * float(w[0]), f[4], f[3], f[2])
            for f, (s, d) in ((low, low_velocity), (high, high_velocity))
        ]
        rate, melt, trans, leakage, overburden, scale, ice = [end_frame(i) for i in (1, 3, 4, 5, 6, 7, 8)]
        quarter = 0.25 * ice
        valid = join([
            jnp.broadcast_to(below, (RIM, wide)), jnp.ones((2 * RIM, wide), jnp.bool_), jnp.broadcast_to(above, (RIM, wide))
        ])
        trans_eff, source = [frame(*f) for f in zip(end_sheets[0], m_first, end_sheets[1])]
        sweep = sweeper(trans_eff, leakage, ends(source), valid, ends)
        pressure = overburden
        for step_1 in steps_1[:-1]:
            pressure = sweep(inside(pressure, step_1))
        friction = scale * pressure
        base = between(friction * (0.5 * SHARE / rate), (0, 2))
        basal = down_of(late_down, base)

        def arrange(early_pieces, late_pieces):
            first, last = late_pieces
            before, after = early_pieces
            return join([first, jnp.where(upper_sub, before, first), jnp.where(upper_sub, last, after), last]) * quarter

        sliding = arrange(early_basal, split(basal))
        trans_eff, source = sheet(sliding, trans, melt, friction)
        sweep = sweeper(inside(trans_eff, m_second[0]), leakage, source, valid, ends)
        for step_2 in steps_2[:-1]:
            pressure = sweep(inside(pressure, step_2))

        mine = slice(RIM, 3 * RIM)

        def surface():
            @pl.when(below)
            def _():
                up_ref[0], up_ref[1] = from_base(slice(2 * RIM, 3 * RIM))

            top, reach = [join([up_ref[n], f]) for n, f in enumerate(high_up)]
            return arrange(early_surface, split(top - base * basal * reach))[mine]

        send_results(outer_chunks, 1, pressure[mine], surface, sliding[mine], scale[mine])

    for condition, edges in ((both(below, above), 20), (below != above, 10), (jnp.logical_not(jnp.logical_or(below, above)), 0)):
        pl.when(condition)(functools.partial(await_tiles, main_send, 10 * tiles + edges))
    counts = (tiles - 2, 2)
    for role, mine, theirs in ((is_inner, *counts), (is_outer, *counts[::-1])):
        pl.when(both(sends_last, role))(functools.partial(await_tiles, out_send, 5 * mine))
        pl.when(both(first_sector, role))(functools.partial(await_tiles, out_send, 3 * mine))
        pl.when(both(is_water, role))(functools.partial(await_tiles, out_send, mine))
        pl.when(both(is_ice, role))(functools.partial(await_tiles, out_recv, 3 * theirs))
        pl.when(both(is_water, role))(functools.partial(await_tiles, out_recv, theirs + (sectors - 1) * tiles))


def narrow_map(nx, *args):
    sectors, rows, lanes = args[0].shape
    most = max(rows - 2 * RIM, 2 * RIM)
    f32 = jnp.float32
    vmem = pltpu.VMEM
    dma = pltpu.SemaphoreType.DMA
    return pl.pallas_call(
        functools.partial(narrow_kernel, sectors, nx),
        out_shape=pltpu.VMEM((1, sectors, rows, lanes), f32),
        in_specs=[pl.BlockSpec(memory_space=pltpu.HBM)] * len(args),
        out_specs=pl.BlockSpec(memory_space=pltpu.VMEM),
        scratch_shapes=[
            vmem((8, rows, lanes), f32),
            vmem((2, rows, lanes), jnp.int32),
            vmem((8, rows, lanes), f32),
            vmem((2, rows, lanes), jnp.int32),
            vmem((2, 2, 8, RIM, lanes), f32),
            vmem((2, 2, 2, RIM, lanes), jnp.int32),
            vmem((LAYERS, max(rows, 4 * RIM), 2 * lanes), f32),
            vmem((LAYERS, max(rows, 4 * RIM), 2 * lanes), f32),
            vmem((LAYERS, max(rows, 4 * RIM), 2 * lanes), f32),
            vmem((2, RIM, 2 * lanes), f32),
            vmem((2, most, lanes), f32),
            vmem((3, most, lanes), f32),
            dma,
            dma,
            dma,
            dma,
            dma((3,)),
            dma,
            pltpu.SemaphoreType.REGULAR((3,)),
        ],
        compiler_params=pltpu.CompilerParams(
            collective_id=0,
            has_side_effects=True,
        ),
    )(*args)


def solution(mesh):
    spec = P(None, "gx", "gy")
    nx, ny = mesh.shape["gx"], mesh.shape["gy"]
    on_device = functools.partial(narrow_map, nx) if ny == 2 else functools.partial(wide_map, nx, ny)
    return jax.shard_map(
        on_device,
        mesh=mesh,
        in_specs=(spec,) * 10,
        out_specs=P("sec", None, "gx", "gy"),
        check_vma=False,
    )
```

```python
import functools

import jax
import jax.numpy as jnp
import numpy as np
from jax import lax
from jax.experimental import pallas as pl
from jax.experimental.pallas import tpu as pltpu
from jax.sharding import PartitionSpec as P

LAYERS = 40
SWEEPS = 4
VERT = 4.0
FLOOR = 0.25
HEATING = 0.5

RIM = 8
HALF = RIM // 2
RESCALE = 10
THIRD = -1.0 / (3.0 * float(np.log(2.0)))
DIRECTIONS = [(dx, dy) for dx in (-1, 0, 1) for dy in (-1, 0, 1) if (dx, dy) != (0, 0)]
MESH = pl.DeviceIdType.MESH


def basal_response():
    matrix = np.zeros((LAYERS, LAYERS))
    for k in range(LAYERS):
        matrix[k, k] = 4.0 + (VERT if k > 0 else 0.0) + (VERT if k < LAYERS - 1 else 0.0)
        if k > 0:
            matrix[k, k - 1] = matrix[k - 1, k] = -VERT
    unit = np.zeros(LAYERS)
    unit[0] = 1.0
    return np.linalg.solve(matrix, unit)


def turn(values, shift, axis):
    return pltpu.roll(values, shift % values.shape[axis], axis)


def neighbours(f):
    return turn(f, -1, 0), turn(f, 1, 0), turn(f, -1, 1), turn(f, 1, 1)


def water_solve(pressure, trans_eff, leakage, source, valid):
    faces = [0.5 * (trans_eff + t) for t in neighbours(trans_eff)]
    total = leakage + ((faces[0] + faces[1]) + (faces[2] + faces[3]))
    inverse = jnp.where(valid, 1.0 / total, 0.0)
    weights = [f * inverse for f in faces]
    base = source * inverse
    for _ in range(SWEEPS):
        parts = [w * p for w, p in zip(weights, neighbours(pressure))]
        pressure = base + ((parts[0] + parts[1]) + (parts[2] + parts[3]))
    return pressure


def wide_kernel(sectors, nx, ny, *refs):
    ins = refs[:10]
    out = refs[10]
    floats, ints, pack_l, pack_r, rim_l, rim_r, q_ref, g_ref, r_ref, send_p = refs[11:21]
    in_sem, send_sem, recv_sem, last_send, last_recv = refs[21:]
    rows, lanes = ins[0].shape[1:]
    sec = lax.axis_index("sec")
    gx = lax.axis_index("gx")
    gy = lax.axis_index("gy")
    strip = lax.rem(sec, sectors)
    is_ice = sec < sectors
    sends_last = jnp.logical_and(sec > 0, is_ice)

    def exists(dx, dy):
        x, y = gx + dx, gy + dy
        return jnp.logical_and(
            jnp.logical_and(x >= 0, x < nx), jnp.logical_and(y >= 0, y < ny)
        )

    float_ids = (0, 1, 2, 5, 6, 7, 8, 9)
    int_ids = (3, 4)
    loads = []
    for slot, arg in enumerate(float_ids):
        loads.append(pltpu.make_async_copy(ins[arg].at[strip], floats.at[slot, pl.ds(RIM, rows)], in_sem.at[0]))
    for slot, arg in enumerate(int_ids):
        loads.append(pltpu.make_async_copy(ins[arg].at[strip], ints.at[slot, pl.ds(RIM, rows)], in_sem.at[1]))
    barrier = pltpu.get_barrier_semaphore()
    count = jnp.int32(0)
    for dx, dy in sorted(DIRECTIONS, key=lambda d: -abs(d[0])):
        here = exists(dx, dy)
        count = count + here.astype(jnp.int32)

        @pl.when(here)
        def _(dx=dx, dy=dy):
            pl.semaphore_signal(barrier, inc=1, device_id={"gx": gx + dx, "gy": gy + dy}, device_id_type=MESH)

    count = count + sends_last.astype(jnp.int32)
    count = count + jnp.where(is_ice, 0, sectors - 1)

    @pl.when(sends_last)
    def _():
        pl.semaphore_signal(barrier, inc=1, device_id={"sec": sectors}, device_id_type=MESH)

    for s in range(1, sectors):

        @pl.when(jnp.logical_not(is_ice))
        def _(s=s):
            pl.semaphore_signal(barrier, inc=1, device_id={"sec": s}, device_id_type=MESH)

    for load in loads:
        load.start()
    for slot, buffer in enumerate((floats, ints)):
        mine = buffer.at[:, pl.ds(RIM, rows)]
        pltpu.make_async_copy(mine, mine, in_sem.at[slot]).wait()

    lane = lax.broadcasted_iota(jnp.int32, (rows, lanes), 1)
    fields = [floats[i, RIM : RIM + rows] for i in range(8)]
    fields += [ints[i, RIM : RIM + rows].astype(jnp.float32) for i in range(2)]
    left = jnp.zeros((rows, lanes), jnp.float32)
    right = jnp.zeros((rows, lanes), jnp.float32)
    for i, f in enumerate(fields):
        moved = turn(f, RIM * i, 1)
        group = lane // RIM
        left = jnp.where(group == i, moved, left)
        right = jnp.where(group == (i - 1) % (lanes // RIM), moved, right)
    pack_l[...] = left
    pack_r[...] = right

    pl.semaphore_wait(barrier, count)

    def copies(dx, dy, n):
        target = {"gx": gx + dx, "gy": gy + dy}

        def remote(src, dst, m):
            return pltpu.make_async_remote_copy(
                src_ref=src, dst_ref=dst, send_sem=send_sem.at[m], recv_sem=recv_sem.at[m],
                device_id=target, device_id_type=MESH,
            )

        if dy == 0:
            first = rows if dx > 0 else RIM
            landing = 0 if dx > 0 else RIM + rows
            return [
                remote(floats.at[:, pl.ds(first, RIM)], floats.at[:, pl.ds(landing, RIM)], n),
                remote(ints.at[:, pl.ds(first, RIM)], ints.at[:, pl.ds(landing, RIM)], 8 + (dx > 0)),
            ]
        src, dst = (pack_r, rim_l) if dy > 0 else (pack_l, rim_r)
        if dx == 0:
            return [remote(src, dst.at[pl.ds(RIM, rows)], n)]
        first = rows - RIM if dx > 0 else 0
        landing = 0 if dx > 0 else RIM + rows
        return [remote(src.at[pl.ds(first, RIM)], dst.at[pl.ds(landing, RIM)], n)]

    order = sorted(range(8), key=lambda n: abs(DIRECTIONS[n][1]))
    for n in order:
        dx, dy = DIRECTIONS[n]

        @pl.when(exists(dx, dy))
        def _(dx=dx, dy=dy, n=n):
            for c in copies(dx, dy, n):
                c.start()

    def arrive(n):
        dx, dy = DIRECTIONS[n]

        @pl.when(exists(-dx, -dy))
        def _():
            for c in copies(dx, dy, n):
                c.wait_recv()

    w = basal_response()
    ext = rows + 2 * RIM
    tall = rows + RIM
    tiles = tall // 8
    wide = 2 * RIM
    slot = lax.broadcasted_iota(jnp.int32, (8, lanes), 1) // wide
    lane_low = jnp.where(gy < ny - 1, lanes + RIM, lanes)
    lane_high = jnp.where(gy > 0, 2 * lanes - RIM, 2 * lanes)

    def in_map_lanes(height):
        lane_i = lax.broadcasted_iota(jnp.int32, (height, 2 * lanes), 1)
        return jnp.logical_or(lane_i < lane_low, lane_i >= lane_high)

    def field_reader(top, height, valid):
        at = slice(top, top + height)
        packed_l, packed_r = rim_l[at], rim_r[at]
        group = lax.broadcasted_iota(jnp.int32, (height, lanes), 1) // RIM

        def field(i, fill):
            main = floats[i, at] if i < 8 else ints[i - 8, at].astype(jnp.float32)
            rim = turn(jnp.where(group == i, packed_r, packed_l), -RIM * i, 1)
            return jnp.where(valid, jnp.concatenate([main, rim], axis=1), fill)

        return field

    def first_velocity(driving, rate, friction, ice):
        viscous = rate * float(FLOOR ** (-1.0 / 3.0))
        speed = driving / (4.0 * viscous)
        drop = -speed * friction / (viscous + friction * float(w[0]))
        return speed * ice, drop * ice

    def squeeze(f, which):
        tile = jnp.zeros((8, lanes), jnp.float32)
        for n, t in enumerate(which):
            moved = turn(f[8 * t : 8 * t + 8, lanes:], wide * n + RIM, 1)
            tile = jnp.where(slot == n, moved, tile)
        return jnp.concatenate([f[8 * t : 8 * t + 8, :lanes] for t in which] + [tile], axis=0)

    def spread(f, count):
        last = f[8 * count :]
        return [
            jnp.concatenate([f[8 * n : 8 * n + 8], turn(last, -(wide * n + RIM), 1)], axis=1)
            for n in range(count)
        ]

    def eliminate(speed, drop, driving, rate, which, offset, lead):
        sxp, sxm, syp, sym = neighbours(speed)
        dxp, dxm, dyp, dym = neighbours(drop)
        sdx, sdy, ddx, ddy = sxp - sxm, syp - sym, dxp - dxm, dyp - dym
        flat = [
            0.03125 * (sdx * sdx + sdy * sdy) + 0.125 * FLOOR,
            0.0625 * (sdx * ddx + sdy * ddy),
            0.03125 * (ddx * ddx + ddy * ddy),
            0.125 * drop * drop,
            0.25 * ((sxp + sxm) + (syp + sym)),
            0.25 * ((dxp + dxm) + (dyp + dym)),
            driving * (0.5 / rate),
        ]
        flat = [squeeze(turn(f, lead, 0), which) for f in flat]
        for n in range(len(which) + 1):
            at = slice(offset + 8 * n, offset + 8 * n + 8)
            c0, c1, c2, c3, n0, n1, dr = [f[8 * n : 8 * n + 8] for f in flat]
            before = None
            for k in range(LAYERS):
                wk = float(w[k])
                strain = c0 + (c1 * wk + c2 * (wk * wk))
                if k < LAYERS - 1:
                    strain = strain + c3 * float((w[k + 1] - w[k]) ** 2)
                twice = jnp.exp2(jnp.log(strain) * THIRD)
                q_ref[k, at] = twice
                r_ref[k, at] = dr + twice * (n0 + n1 * wk)
                if k > 0:
                    g_ref[k - 1, at] = 0.5 * (before + twice)
                before = twice

        at = slice(offset, offset + 8 * (len(which) + 1))
        up_d, up_e, up_t = None, q_ref[0, at], r_ref[0, at]
        down_d, down_e, down_t = None, q_ref[LAYERS - 1, at], r_ref[LAYERS - 1, at]
        product = None

        def step(d, e, t, g, q, r):
            d = e + (g if d is None else g * d)
            return d, q * d + g * e, r * d + g * t

        for k in range(LAYERS - 1):
            j = LAYERS - 2 - k
            g = g_ref[k, at]
            product = g if product is None else product * g
            up_d, up_e, up_t = step(up_d, up_e, up_t, g, q_ref[k + 1, at], r_ref[k + 1, at])
            down_d, down_e, down_t = step(
                down_d, down_e, down_t, g_ref[j, at], q_ref[j, at], r_ref[j, at]
            )
            if k % RESCALE == RESCALE - 1 and k < LAYERS - 2:
                shrink = 1.0 / up_d
                up_d, up_e, up_t, product = None, up_e * shrink, up_t * shrink, product * shrink
                shrink = 1.0 / down_d
                down_d, down_e, down_t = None, down_e * shrink, down_t * shrink
        shrink = 1.0 / up_e
        return down_d, down_e, down_t, up_t * shrink, product * shrink

    def finish(parts, friction, rate, ice, which):
        down_d, down_e, down_t, top, reach = parts
        base = squeeze(turn(friction * (0.5 / rate), -HALF, 0), which)
        mask = squeeze(turn(ice, -HALF, 0), which)
        basal = down_t / (down_e + base * down_d)
        surface = top - base * basal * reach
        return [spread(f * mask, len(which)) for f in (basal, surface)]

    for n in order:
        if DIRECTIONS[n][0] == 0:
            arrive(n)
    early = list(range(1, tiles - 1))
    late = [0, tiles - 1]
    field = field_reader(RIM, rows, in_map_lanes(rows))
    driving, rate = field(0, 0.0), field(1, 1.0)
    speed, drop = first_velocity(driving, rate, field(2, 0.0) * field(9, 0.0), field(8, 0.0))
    early_parts = eliminate(speed, drop, driving, rate, early, 0, HALF)
    for n in order:
        if DIRECTIONS[n][0] != 0:
            arrive(n)

    row_i = lax.broadcasted_iota(jnp.int32, (ext, 2 * lanes), 0)
    row_low = jnp.where(gx > 0, 0, RIM)
    row_high = jnp.where(gx < nx - 1, ext, RIM + rows)
    valid = jnp.logical_and(
        jnp.logical_and(row_i >= row_low, row_i < row_high), in_map_lanes(ext)
    )
    field = field_reader(0, ext, valid)
    driving = field(0, 0.0)
    rate = field(1, 1.0)
    friction = field(2, 0.0)
    melt = field(3, 0.0)
    trans = field(4, 0.0)
    leakage = field(5, 1.0)
    pressure = field(6, 0.0)
    scale = field(7, 0.0)
    ice = field(8, 0.0)
    grounded = field(9, 0.0)
    friction = friction * grounded
    scale = scale * grounded

    speed, drop = first_velocity(driving, rate, friction, ice)
    sliding = speed + drop * float(w[0])
    squared = sliding * sliding
    trans_eff = trans * (1.0 + squared / (1.0 + squared))
    source = melt + HEATING * friction * squared
    pressure = water_solve(pressure, trans_eff, leakage, source, valid)
    friction = scale * pressure

    late_parts = eliminate(speed, drop, driving, rate, late, 8 * (len(early) + 1), -HALF)
    pieces = [None] * tiles
    for parts, which in ((early_parts, early), (late_parts, late)):
        for n, piece in enumerate(zip(*finish(parts, friction, rate, ice, which))):
            pieces[which[n]] = piece
    blank = jnp.zeros((RIM, 2 * lanes), jnp.float32)
    basal = turn(jnp.concatenate([p[0] for p in pieces] + [blank], axis=0), HALF, 0)
    surface = jnp.concatenate([p[1][:, :lanes] for p in pieces], axis=0)
    sliding = jnp.where(valid, basal, 0.0)
    squared = sliding * sliding
    trans_eff = trans * (1.0 + squared / (1.0 + squared))
    source = melt + HEATING * friction * squared
    pressure = water_solve(pressure, trans_eff, leakage, source, valid)
    block = pressure[RIM : RIM + rows, :lanes]
    send_p[...] = block

    def last():
        return pltpu.make_async_remote_copy(
            src_ref=send_p, dst_ref=out.at[0, strip], send_sem=last_send, recv_sem=last_recv.at[strip],
            device_id={"sec": sectors}, device_id_type=MESH,
        )

    @pl.when(sends_last)
    def _():
        last().start()

    @pl.when(is_ice)
    def _():
        out[0, 0] = turn(surface, -HALF, 0)[:rows]
        out[0, 1] = sliding[RIM : RIM + rows, :lanes]
        out[0, 2] = scale[RIM : RIM + rows, :lanes] * block

    @pl.when(jnp.logical_not(is_ice))
    def _():
        out[0, 0] = block

    for n in order:
        dx, dy = DIRECTIONS[n]

        @pl.when(exists(dx, dy))
        def _(dx=dx, dy=dy, n=n):
            for c in copies(dx, dy, n):
                c.wait_send()

    @pl.when(sends_last)
    def _():
        last().wait_send()

    for s in range(1, sectors):

        @pl.when(jnp.logical_not(is_ice))
        def _(s=s):
            pltpu.make_async_remote_copy(
                src_ref=send_p, dst_ref=out.at[0, s], send_sem=last_send, recv_sem=last_recv.at[s],
                device_id={"sec": 0}, device_id_type=MESH,
            ).wait_recv()


def wide_map(nx, ny, *args):
    sectors, rows, lanes = args[0].shape
    ext = rows + 2 * RIM
    f32 = jnp.float32
    vmem = pltpu.VMEM
    dma = pltpu.SemaphoreType.DMA
    return pl.pallas_call(
        functools.partial(wide_kernel, sectors, nx, ny),
        out_shape=pltpu.VMEM((1, sectors, rows, lanes), f32),
        in_specs=[pl.BlockSpec(memory_space=pltpu.HBM)] * len(args),
        out_specs=pl.BlockSpec(memory_space=pltpu.VMEM),
        scratch_shapes=[
            vmem((8, ext, lanes), f32),
            vmem((2, ext, lanes), jnp.int32),
            vmem((rows, lanes), f32),
            vmem((rows, lanes), f32),
            vmem((ext, lanes), f32),
            vmem((ext, lanes), f32),
            vmem((LAYERS, ext + RIM, lanes), f32),
            vmem((LAYERS, ext + RIM, lanes), f32),
            vmem((LAYERS, ext + RIM, lanes), f32),
            vmem((rows, lanes), f32),
            dma((2,)),
            dma((10,)),
            dma((10,)),
            dma,
            dma((sectors,)),
        ],
        compiler_params=pltpu.CompilerParams(collective_id=0, has_side_effects=True),
    )(*args)


SHARE = 32.0 ** (-1.0 / 3.0)


def steady_drop(w):
    ratios = np.float32(4.0 * ((w[1:] - w[:-1]) / w[:-1]) ** 2)
    same = np.cumprod(ratios == ratios[0])
    return float(ratios[0]), int(same.sum())


ORDER = (0, 1, 2, 5, 6, 7, 8, 9, 3, 4)


def narrow_kernel(sectors, nx, *refs):
    ins = refs[:10]
    out = refs[10]
    own_f, own_i, part_f, part_i, halo_f, halo_i, q_ref, g_ref, r_ref, up_ref, send_p, results = refs[11:23]
    own_sem, main_send, main_recv, halo_recv, out_recv, credit = refs[23:]
    rows, lanes = ins[0].shape[1:]
    sec = lax.axis_index("sec")
    gx = lax.axis_index("gx")
    gy = lax.axis_index("gy")
    partner = 1 - gy
    is_outer = gy == 1
    is_inner = gy == 0
    strip = lax.rem(sec, sectors)
    is_ice = sec < sectors
    is_water = jnp.logical_not(is_ice)
    sends_last = jnp.logical_and(sec > 0, is_ice)
    below, above = gx > 0, gx < nx - 1
    first_sector = sec == 0

    def both(p, q):
        return jnp.logical_and(p, q)

    def number(condition):
        return condition.astype(jnp.int32)

    def await_tiles(sem, count):
        wide_tiles = count % 2 == 0
        room = q_ref.at[pl.ds(0, count // 2 if wide_tiles else count), pl.ds(0, RIM), pl.ds(0, (1 + wide_tiles) * lanes)]
        pltpu.make_async_copy(room, room, sem).wait()

    def copy_in(n):
        dst = own_f.at[n] if n < 8 else own_i.at[n - 8]
        return pltpu.make_async_copy(ins[ORDER[n]].at[strip], dst, own_sem)

    def load():
        for n in range(10):
            copy_in(n).start()

    pl.when(is_outer)(load)
    barrier = pltpu.get_barrier_semaphore()

    def signal(condition, sem, target, role=True):
        @pl.when(jnp.logical_and(condition, role))
        def _():
            pl.semaphore_signal(sem, inc=1, device_id=target, device_id_type=MESH)

    signal(above, barrier, {"gx": gx + 1, "gy": 0}, is_outer)
    signal(above, barrier, {"gx": gx + 1, "gy": 1}, is_outer)
    signal(is_outer, barrier, {"gy": 0})
    signal(sends_last, barrier, {"sec": sectors, "gy": partner})
    signal(sends_last, barrier, {"sec": sectors})
    count = number(is_inner) + number(below) + jnp.where(is_ice, 0, 2 * (sectors - 1))

    @pl.when(count > 0)
    def _():
        pl.semaphore_wait(barrier, count)

    signal(below, credit.at[0], {"gx": gx - 1, "gy": 1}, is_outer)

    def remote(src, dst, sent, landed, target):
        return pltpu.make_async_remote_copy(
            src_ref=src, dst_ref=dst, send_sem=sent, recv_sem=landed, device_id=target, device_id_type=MESH,
        )

    def main_copies():
        target = {"gy": partner}
        return [remote(own_f, part_f, main_send, main_recv, target), remote(own_i, part_i, main_send, main_recv, target)]

    def edge_copies():
        src = pl.ds(rows - RIM, RIM)
        target = {"gx": gx + 1, "gy": 1}
        first, rest = pl.ds(0, 3), pl.ds(3, 5)
        return [
            remote(own_f.at[first, src], halo_f.at[0, gy, first], main_send, halo_recv.at[0], target),
            remote(own_i.at[:, src], halo_i.at[0, gy], main_send, halo_recv.at[0], target),
            remote(own_f.at[rest, src], halo_f.at[0, gy, rest], main_send, halo_recv.at[2], target),
        ]

    def start(condition, copies):
        @pl.when(condition)
        def _():
            for c in copies:
                c.start()

    def await_credit(condition, which, amount):
        @pl.when(condition)
        def _():
            pl.semaphore_wait(credit.at[which], amount)

    @pl.when(below)
    def _():
        for n in (0, 1, 2, 8, 9, 3, 4, 5, 6, 7):
            src = ins[ORDER[n]].at[strip, pl.ds(0, RIM)]
            dst = halo_f.at[1, gy, n] if n < 8 else halo_i.at[1, gy, n - 8]
            part = int(3 <= n < 8)
            remote(src, dst, main_send, halo_recv.at[1 + part], {"gx": gx - 1, "gy": 1}).start()

    signal(is_inner, credit.at[2], {"gy": 1})
    pl.when(is_inner)(load)

    @pl.when(is_inner)
    def _():
        for n in (0, 1, 2, 8, 9, 3, 4, 5, 6, 7):
            dst = part_f.at[n] if n < 8 else part_i.at[n - 8]
            remote(ins[ORDER[n]].at[strip], dst, main_send, main_recv, {"gy": 1}).start()

    for s in range(1, sectors):
        signal(is_water, credit.at[1], {"sec": s, "gy": partner})
        signal(is_water, credit.at[1], {"sec": s})
    await_tiles(own_sem, 10 * rows // RIM)
    await_credit(is_outer, 2, 1)
    start(is_outer, main_copies())

    def send_upwards():
        await_credit(both(above, is_outer), 0, 1)
        signal(is_outer, credit.at[0], {"gy": 0})
        await_credit(is_inner, 0, 1)
        start(above, edge_copies())

    starts_first = both(first_sector, gx == 0)
    pl.when(jnp.logical_not(starts_first))(send_upwards)


    w = basal_response()
    steady, settled = steady_drop(w)
    wide = 2 * lanes
    lane = lax.broadcasted_iota(jnp.int32, (RIM, wide), 1)
    upper_sub = lax.broadcasted_iota(jnp.int32, (RIM, wide), 0) >= HALF
    last_lane = lane == wide - 1
    first_lane = lane == 0

    def join(parts):
        return jnp.concatenate(parts, axis=0)

    def tall_mask(mask, count):
        return join([mask] * count)

    def beside(f, i):
        return f[i] if i < 8 else f[i - 8].astype(jnp.float32)

    def fields(left, right, which=range(9)):
        def field(i):
            return jnp.concatenate([beside(left[i >= 8], i), beside(right[i >= 8], i)], axis=1)

        return {i: field(i) * field(9) if i in (2, 7) else field(i) for i in which}

    def halo_fields(side, exists, which):
        left, right = [(halo_f.at[side, r], halo_i.at[side, r]) for r in range(2)]
        return {
            i: jnp.where(exists, f, 1.0 if i in (1, 5) else 0.0) for i, f in fields(left, right, which).items()
        }

    def first_velocity(driving, rate, friction, ice):
        viscous = rate * float(FLOOR ** (-1.0 / 3.0))
        speed = driving / (4.0 * viscous)
        drop = -speed * friction / (viscous + friction * float(w[0]))
        return speed * ice, drop * ice

    def shifts(f):
        count = f.shape[0] // RIM
        yp = jnp.where(tall_mask(last_lane, count), 0.0, turn(f, -1, 1))
        ym = jnp.where(tall_mask(first_lane, count), 0.0, turn(f, 1, 1))
        return turn(f, -1, 0), turn(f, 1, 0), yp, ym

    def sheet(sliding, trans, melt, friction):
        squared = sliding * sliding
        return trans * (1.0 + squared / (1.0 + squared)), melt + HEATING * friction * squared

    def sweeper(trans_eff, leakage, source, valid, keep):
        here = keep(trans_eff)
        faces = [0.5 * (here + keep(t)) for t in shifts(trans_eff)]
        total = leakage + ((faces[0] + faces[1]) + (faces[2] + faces[3]))
        inverse = 1.0 / total if valid is None else jnp.where(valid, 1.0 / total, 0.0)
        weights = [f * inverse for f in faces]
        count = here.shape[0] // RIM
        weights[2] = jnp.where(tall_mask(last_lane, count), 0.0, weights[2])
        weights[3] = jnp.where(tall_mask(first_lane, count), 0.0, weights[3])
        base = source * inverse

        def sweep(pressure):
            parts = [w * keep(p) for w, p in zip(weights, neighbours(pressure))]
            return base + ((parts[0] + parts[1]) + (parts[2] + parts[3]))

        return sweep

    def water_steps(pressure, trans_eff, leakage, source):
        sweep = sweeper(trans_eff, leakage, source, None, lambda f: f)
        steps = [pressure]
        for _ in range(SWEEPS):
            steps.append(sweep(steps[-1]))
        return steps

    def split(f):
        return [f[RIM * k : RIM * k + RIM] for k in range(f.shape[0] // RIM)]

    def between(f, which):
        pieces = split(f)
        return join([jnp.where(upper_sub, pieces[k], pieces[k + 1]) for k in which])

    def restore(pieces):
        middle = [jnp.where(upper_sub, q, p) for p, q in zip(pieces[:-1], pieces[1:])]
        return join([pieces[0], *middle, pieces[-1]])

    def coefficients(speed, drop, driving, rate, which):
        s_shift = [between(f, which) for f in shifts(speed)]
        d_shift = [between(f, which) for f in shifts(drop)]
        drop, driving, rate = [between(f, which) for f in (drop, driving, rate)]
        sdx, sdy = s_shift[0] - s_shift[1], s_shift[2] - s_shift[3]
        ddx, ddy = d_shift[0] - d_shift[1], d_shift[2] - d_shift[3]
        c2, c3 = ddx * ddx + ddy * ddy, drop * drop
        return [
            (sdx * sdx + sdy * sdy) + 4.0 * FLOOR,
            sdx * ddx + sdy * ddy,
            c2,
            c3,
            c2 + steady * c3,
            (s_shift[0] + s_shift[1]) + (s_shift[2] + s_shift[3]),
            (d_shift[0] + d_shift[1]) + (d_shift[2] + d_shift[3]),
            driving * (2.0 * SHARE / rate),
        ]

    def viscosity(flat, offset):
        for n in range(flat[0].shape[0] // RIM):
            at = slice(offset + RIM * n, offset + RIM * n + RIM)
            c0, c1, c2, c3, c23, n0, n1, dr = [f[RIM * n : RIM * n + RIM] for f in flat]
            higher = None
            for k in reversed(range(LAYERS)):
                wk = float(w[k])
                if k < settled:
                    strain = c0 + (c1 * (2.0 * wk) + c23 * (wk * wk))
                else:
                    strain = c0 + (c1 * (2.0 * wk) + c2 * (wk * wk))
                    if k < LAYERS - 1:
                        strain = strain + c3 * float(4.0 * (w[k + 1] - w[k]) ** 2)
                now = jnp.exp2(jnp.log(strain) * THIRD)
                q_ref[k, at] = now
                r_ref[k, at] = dr + now * (n0 + n1 * wk)
                if k < LAYERS - 1:
                    g_ref[k, at] = 0.5 * (now + higher)
                higher = now

    def step(d, e, t, g, q, r):
        d = e + (g if d is None else g * d)
        return d, q * d + g * e, r * d + g * t

    def from_surface(at):
        d, e, t = None, q_ref[LAYERS - 1, at], r_ref[LAYERS - 1, at]
        for k in range(LAYERS - 1):
            j = LAYERS - 2 - k
            d, e, t = step(d, e, t, g_ref[j, at], q_ref[j, at], r_ref[j, at])
            if k % RESCALE == RESCALE - 1 and k < LAYERS - 2:
                shrink = 1.0 / d
                d, e, t = None, e * shrink, t * shrink
        return d, e, t

    def from_base(at):
        d, e, t, product = None, q_ref[0, at], r_ref[0, at], None
        for k in range(LAYERS - 1):
            g = g_ref[k, at]
            product = g if product is None else product * g
            d, e, t = step(d, e, t, g, q_ref[k + 1, at], r_ref[k + 1, at])
            if k % RESCALE == RESCALE - 1 and k < LAYERS - 2:
                shrink = 1.0 / d
                d, e, t, product = None, e * shrink, t * shrink, product * shrink
        shrink = 1.0 / e
        return t * shrink, product * shrink

    def result_copy(src, planes, where, target):
        return remote(src, out.at[0, planes, where], own_sem, out_recv, target)

    inner_chunks = [(0, RIM, rows - 2 * RIM)]
    outer_chunks = [(0, 0, RIM), (RIM, rows - RIM, RIM)]

    def send_results(chunks, k, pressure, surface, sliding, scale):
        count = pressure.shape[0]
        at = pl.ds(0, count)
        send_p[0, at] = pressure[:, :lanes]
        send_p[1, at] = pressure[:, lanes:]
        mine, other = (slice(0, lanes), 1) if k == 0 else (slice(lanes, wide), 0)

        def started(copies):
            for c in copies:
                c.start()

        def pieces(src, planes, target):
            return [result_copy(src(pl.ds(a, n)), planes, pl.ds(b, n), target) for a, b, n in chunks]

        @pl.when(sends_last)
        def _():
            pl.semaphore_wait(credit.at[1], 2)
            for r in (1, 0):
                started(pieces(lambda d, r=r: send_p.at[r, d], strip, {"sec": sectors, "gy": r}))

        @pl.when(is_water)
        def _():
            started(pieces(lambda d: send_p.at[other, d], 0, {"gy": partner}))
            for a, b, n in chunks:
                out[0, 0, b : b + n] = pressure[a : a + n, mine]

        @pl.when(is_ice)
        def _():
            theirs = slice(lanes, wide) if k == 0 else slice(0, lanes)
            for plane, f in enumerate((surface(), sliding, scale * pressure)):
                results[plane, at] = f[:, theirs]
                for a, b, n in chunks:
                    out[0, plane, b : b + n] = f[a : a + n, mine]
            started(pieces(lambda d: results.at[:, d], slice(None), {"gy": partner}))

    tiles = rows // RIM
    await_tiles(main_recv, 10 * tiles)

    def down_of(parts, base):
        d, e, t = parts
        return t / (e + base * d)

    @pl.when(is_inner)
    def _():
        driving, rate, friction, melt, trans, leakage, overburden, scale, ice = fields((own_f, own_i), (part_f, part_i)).values()
        which = range(tiles - 1)
        at = slice(0, rows - RIM)
        speed, drop = first_velocity(driving, rate, friction, ice)
        viscosity(coefficients(speed, drop, driving, rate, which), 0)
        pl.when(starts_first)(send_upwards)
        trans_eff, source = sheet(speed + drop * float(w[0]), trans, melt, friction)
        pressure = water_steps(overburden, trans_eff, leakage, source)[-1]
        friction = scale * pressure
        base = between(friction * (0.5 * SHARE / rate), which)
        basal = down_of(from_surface(at), base)
        quarter = 0.25 * ice
        sliding = restore(split(basal)) * quarter
        trans_eff, source = sheet(sliding, trans, melt, friction)
        pressure = water_steps(pressure, trans_eff, leakage, source)[-1]
        mine = slice(RIM, rows - RIM)

        def surface():
            top, reach = from_base(at)
            return (restore(split(top - base * basal * reach)) * quarter)[mine]

        send_results(inner_chunks, 0, pressure[mine], surface, sliding[mine], scale[mine])

    @pl.when(is_outer)
    def _():
        middle = fields((part_f, part_i), (own_f, own_i))
        driving, rate, friction, melt, trans, leakage, overburden, scale, ice = middle.values()
        m_speed, m_drop = first_velocity(driving, rate, friction, ice)
        which = (0, tiles - 2)
        early = slice(0, 2 * RIM)
        viscosity(coefficients(m_speed, m_drop, driving, rate, which), 0)
        pl.when(starts_first)(send_upwards)
        early_down = from_surface(early)
        top, reach = from_base(early)
        m_first = sheet(m_speed + m_drop * float(w[0]), trans, melt, friction)
        steps_1 = water_steps(overburden, m_first[0], leakage, m_first[1])
        m_friction = scale * steps_1[-1]
        base = between(m_friction * (0.5 * SHARE / rate), which)
        basal = down_of(early_down, base)
        early_basal = split(basal)
        early_surface = split(top - base * basal * reach)
        blank = [jnp.zeros((RIM, wide), jnp.float32)] * (tiles - 3)
        m_second = sheet(
            restore([early_basal[0], *blank, early_basal[1]]) * (0.25 * ice), trans, melt, m_friction
        )
        steps_2 = water_steps(steps_1[-1], m_second[0], leakage, m_second[1])

        halo_sides = ((0, below), (1, above))

        def await_halo(side, exists):
            pl.when(exists)(functools.partial(await_tiles, halo_recv.at[side], 10))

        def frame(a, f, b):
            return join([a, f, b])

        def ends(f):
            return join([f[: 2 * RIM], f[rows:]])

        def inside(e, f):
            return join([e[: 2 * RIM], f[RIM : rows - RIM], e[2 * RIM :]])

        def end_frame(i):
            return join([low[i], middle[i][:RIM], middle[i][rows - RIM :], high[i]])

        ends_in, end_velocity, late_down = [], [], []
        for side, exists in halo_sides:
            await_halo(side, exists)
            h = halo_fields(side, exists, (0, 1, 2, 8))
            velocity = first_velocity(h[0], h[1], h[2], h[8])
            inner = slice(0, RIM) if side == 0 else slice(rows - RIM, rows)
            pairs = [(velocity[0], m_speed), (velocity[1], m_drop), (h[0], middle[0]), (h[1], middle[1])]
            viscosity(
                coefficients(*[join([a, f[inner]] if side == 0 else [f[inner], a]) for a, f in pairs], (0,)), (2 + side) * RIM
            )
            tile = slice((2 + side) * RIM, (3 + side) * RIM)
            if side == 0:
                late_down.append(from_surface(tile))
            ends_in.append(h)
            end_velocity.append(velocity)
            if side == 0:

                @pl.when(jnp.logical_not(below))
                def _():
                    up_ref[0], up_ref[1] = from_base(tile)

        low, high = ends_in
        low_velocity, high_velocity = end_velocity
        pl.when(both(below, above))(functools.partial(await_tiles, halo_recv.at[2], 20))
        pl.when(below != above)(functools.partial(await_tiles, halo_recv.at[2], 10))
        late_down.append(from_surface(slice(3 * RIM, 4 * RIM)))
        late_down = [join(p) for p in zip(*late_down)]
        high_up = from_base(slice(3 * RIM, 4 * RIM))
        low |= halo_fields(0, below, (3, 4, 5, 6, 7))
        high |= halo_fields(1, above, (3, 4, 5, 6, 7))
        end_sheets = [
            sheet(s + d * float(w[0]), f[4], f[3], f[2])
            for f, (s, d) in ((low, low_velocity), (high, high_velocity))
        ]
        rate, melt, trans, leakage, overburden, scale, ice = [end_frame(i) for i in (1, 3, 4, 5, 6, 7, 8)]
        quarter = 0.25 * ice
        valid = join([
            jnp.broadcast_to(below, (RIM, wide)), jnp.ones((2 * RIM, wide), jnp.bool_), jnp.broadcast_to(above, (RIM, wide))
        ])
        trans_eff, source = [frame(*f) for f in zip(end_sheets[0], m_first, end_sheets[1])]
        sweep = sweeper(trans_eff, leakage, ends(source), valid, ends)
        pressure = overburden
        for step_1 in steps_1[:-1]:
            pressure = sweep(inside(pressure, step_1))
        friction = scale * pressure
        base = between(friction * (0.5 * SHARE / rate), (0, 2))
        basal = down_of(late_down, base)

        def arrange(early_pieces, late_pieces):
            first, last = late_pieces
            before, after = early_pieces
            return join([first, jnp.where(upper_sub, before, first), jnp.where(upper_sub, last, after), last]) * quarter

        sliding = arrange(early_basal, split(basal))
        trans_eff, source = sheet(sliding, trans, melt, friction)
        sweep = sweeper(inside(trans_eff, m_second[0]), leakage, source, valid, ends)
        for step_2 in steps_2[:-1]:
            pressure = sweep(inside(pressure, step_2))

        mine = slice(RIM, 3 * RIM)

        def surface():
            @pl.when(below)
            def _():
                up_ref[0], up_ref[1] = from_base(slice(2 * RIM, 3 * RIM))

            top, reach = [join([up_ref[n], f]) for n, f in enumerate(high_up)]
            return arrange(early_surface, split(top - base * basal * reach))[mine]

        send_results(outer_chunks, 1, pressure[mine], surface, sliding[mine], scale[mine])

    for condition, edges in ((both(below, above), 20), (below != above, 10), (jnp.logical_not(jnp.logical_or(below, above)), 0)):
        pl.when(condition)(functools.partial(await_tiles, main_send, 10 * tiles + edges))
    counts = (tiles - 2, 2)
    for role, mine, theirs in ((is_inner, *counts), (is_outer, *counts[::-1])):
        pl.when(both(sends_last, role))(functools.partial(await_tiles, own_sem, 5 * mine))
        pl.when(both(first_sector, role))(functools.partial(await_tiles, own_sem, 3 * mine))
        pl.when(both(is_water, role))(functools.partial(await_tiles, own_sem, mine))
        pl.when(both(is_ice, role))(functools.partial(await_tiles, out_recv, 3 * theirs))
        pl.when(both(is_water, role))(functools.partial(await_tiles, out_recv, theirs + (sectors - 1) * tiles))


def narrow_map(nx, *args):
    sectors, rows, lanes = args[0].shape
    most = max(rows - 2 * RIM, 2 * RIM)
    f32 = jnp.float32
    vmem = pltpu.VMEM
    dma = pltpu.SemaphoreType.DMA
    return pl.pallas_call(
        functools.partial(narrow_kernel, sectors, nx),
        out_shape=pltpu.VMEM((1, sectors, rows, lanes), f32),
        in_specs=[pl.BlockSpec(memory_space=pltpu.HBM)] * len(args),
        out_specs=pl.BlockSpec(memory_space=pltpu.VMEM),
        scratch_shapes=[
            vmem((8, rows, lanes), f32),
            vmem((2, rows, lanes), jnp.int32),
            vmem((8, rows, lanes), f32),
            vmem((2, rows, lanes), jnp.int32),
            vmem((2, 2, 8, RIM, lanes), f32),
            vmem((2, 2, 2, RIM, lanes), jnp.int32),
            vmem((LAYERS, max(rows, 4 * RIM), 2 * lanes), f32),
            vmem((LAYERS, max(rows, 4 * RIM), 2 * lanes), f32),
            vmem((LAYERS, max(rows, 4 * RIM), 2 * lanes), f32),
            vmem((2, RIM, 2 * lanes), f32),
            vmem((2, most, lanes), f32),
            vmem((3, most, lanes), f32),
            dma,
            dma,
            dma,
            dma((3,)),
            dma,
            pltpu.SemaphoreType.REGULAR((3,)),
        ],
        compiler_params=pltpu.CompilerParams(
            collective_id=0,
            has_side_effects=True,
        ),
    )(*args)


def solution(mesh):
    spec = P(None, "gx", "gy")
    nx, ny = mesh.shape["gx"], mesh.shape["gy"]
    on_device = functools.partial(narrow_map, nx) if ny == 2 else functools.partial(wide_map, nx, ny)
    return jax.shard_map(
        on_device,
        mesh=mesh,
        in_specs=(spec,) * 10,
        out_specs=P("sec", None, "gx", "gy"),
        check_vma=False,
    )
```
